128 devices in a mesh: img: 4 (over z), depth: 32 (over y, x, core).
Axes of the slice: x: 4, y: 4, z: 4, core: 2. Of those that a mesh axis runs over, the one named last changes fastest.
Arguments:
- volume: bfloat16 [128, 2048, 512], P('depth', 'img'), may hold values from 0 to 1
- transfer_table: bfloat16 [4, 128], replicated, may hold values from 0 to 3
Outputs:
- image: float32 [4, 1048576], P(None, ('img', 'depth'))
The draws below stay inside these ranges and needn't reach their ends.
All inputs are finite; a program needn't handle non-finite values.
Results may differ from the reference program's by a relative error of at most 0.00044.
Values may be sent and summed in bfloat16 or wider, within the bound.
No kernel may reach another device: no remote copies, remote signals or barrier semaphores. Data moves between devices by JAX's collectives and lax.ppermute only.
A program may use at most 64 MiB of HBM per device.

```python
import jax
import jax.numpy as jnp
from jax import lax

TY = 512
ENTRIES = 128
NXV = 2048
NZ = 128


def block_levels(own_key, shape, split, least, largest):
    def one(dim, shards_of):
        steps = jax.random.uniform(jax.random.fold_in(jax.random.fold_in(own_key, 6), dim), (shards_of,), jnp.float32, least / len(split), largest / len(split))
        return jnp.repeat(jnp.exp(steps), shape[dim] // shards_of).reshape((-1,) + (1,) * (len(shape) - dim - 1))

    loudness = one(*split[0])
    for cut in split[1:]:
        loudness = loudness * one(*cut)
    return loudness


def setup_inputs(seed: int = 0) -> dict:
    key_list = jax.random.split(jax.random.key(seed), 3)
    return {
        "volume": jnp.clip(1.0 * jax.random.uniform(key_list[0], (NZ, NXV, TY), jnp.float32) ** block_levels(key_list[0], (NZ, NXV, TY), ((0, 32), (1, 4)), -0.2, 0.2), 0.0, 1.0).astype(jnp.bfloat16),
        "transfer_table": jnp.clip(jax.random.uniform(key_list[1], (4, ENTRIES), jnp.float32, 0.0, 3.0), 0.0, 3.0).astype(jnp.bfloat16),
    }


def colorize(center, grad_z, grad_x, grad_y, transfer_table, depth_total):
    lambert = jnp.abs(2.0 / 3.0 * grad_z + 1.0 / 3.0 * grad_x + 2.0 / 3.0 * grad_y)
    shading = 0.3 + 0.7 * lambert / jnp.sqrt(grad_z * grad_z + grad_x * grad_x + grad_y * grad_y + 0.01)
    entries = transfer_table.shape[1]
    position = center.reshape(-1) * jnp.float32(entries - 1)
    knot_list = jnp.arange(entries, dtype=jnp.float32)
    weights = jnp.maximum(0.0, 1.0 - jnp.abs(position[None, :] - knot_list[:, None])).astype(jnp.bfloat16)
    values = jnp.dot(transfer_table, weights, preferred_element_type=jnp.float32)
    colour = values[0:3] * shading.reshape(-1)[None, :]
    opacity = 1.0 - jnp.exp(-values[3] / jnp.float32(depth_total))
    return (colour, opacity)

def reference(volume, transfer_table):
    padded = jnp.pad(volume, 1)
    pixels = volume.shape[1] * volume.shape[2]

    def advance(state_pair, slab_index):
        accum, transmit = state_pair
        before = lax.dynamic_index_in_dim(padded, slab_index, 0, False)[1:-1, 1:-1].astype(jnp.float32)
        middle = lax.dynamic_index_in_dim(padded, slab_index + 1, 0, False).astype(jnp.float32)
        after = lax.dynamic_index_in_dim(padded, slab_index + 2, 0, False)[1:-1, 1:-1].astype(jnp.float32)
        center = middle[1:-1, 1:-1]
        grad_z = (after - before) * 0.5
        grad_x = (middle[2:, 1:-1] - middle[:-2, 1:-1]) * 0.5
        grad_y = (middle[1:-1, 2:] - middle[1:-1, :-2]) * 0.5
        colour, opacity = colorize(center, grad_z, grad_x, grad_y, transfer_table, NZ)
        accum = accum + transmit[None, :] * opacity[None, :] * colour
        transmit = transmit * (1.0 - opacity)
        return ((accum, transmit), None)
    start = (jnp.zeros((3, pixels), jnp.float32), jnp.ones((pixels,), jnp.float32))
    (accum, transmit), _ = lax.scan(advance, start, jnp.arange(NZ, dtype=jnp.int32))
    return jnp.concatenate([accum, (1.0 - transmit)[None, :]], axis=0)
```

```python
import functools

import jax
import jax.numpy as jnp
import numpy as np
from jax import lax
from jax.experimental import pallas as pl
from jax.experimental.pallas import tpu as pltpu
from jax.sharding import PartitionSpec as P

F32 = jnp.float32
BF16 = jnp.bfloat16
BLOCK = 16
LANES = 128
CHUNKS = 2
TINY = 1e-30


def row_differences(rows):
    local = np.arange(rows // 2)
    out = np.zeros((2, rows // 2, rows), np.float32)
    for parity in range(2):
        own = local // BLOCK * (2 * BLOCK) + parity * BLOCK + local % BLOCK
        for step in (1, -1):
            there = own + step
            keep = (there >= 0) & (there < rows)
            out[parity, local[keep], there[keep]] += step
    return out


def column_differences(cols):
    k = np.arange(cols)
    return (k[:, None] == k[None, :] + 1).astype(np.float32) - (
        k[:, None] == k[None, :] - 1
    ).astype(np.float32)


def look_up(table, index):
    return jnp.take_along_axis(table, index, axis=1, mode="promise_in_bounds")


def slab_kernel(
    core, own, other, outer_own, outer_other, edge_own, edge_other, rows_op, cols_op, tables,
    out, dx_ref, dy_ref, *, chunk, width,
):
    slices = own.shape[0]
    blocks = own.shape[1]
    cols = own.shape[4]
    entries = tables.shape[2]
    left = chunk * width
    window = slice(left, left + width)

    def slab(near, far, before, after, near_edge, far_edge, parity):
        stack = [(near, s) for s in range(slices)] + [(far, s) for s in range(slices)]
        edges = [(near_edge, s) for s in range(slices)] + [(far_edge, s) for s in range(slices)]
        for s, (ref, z) in enumerate(stack):
            strip = ref[z, :, :, :, window].reshape(blocks * 2 * BLOCK, width)
            dx = jnp.dot(rows_op[parity], strip, preferred_element_type=F32)
            dx_ref[s] = dx
            mine = ref[z, :, parity].reshape(blocks * BLOCK, cols)
            dy_ref[s] = jnp.dot(mine, cols_op[:, window], preferred_element_type=F32)
            edge_ref, edge_z = edges[s]
            row = edge_ref[edge_z : edge_z + 1, window].astype(F32)
            if parity == 0:
                dx_ref[s, 0:1, :] = dx[0:1] - row
            else:
                last = blocks * BLOCK
                dx_ref[s, last - 1 : last, :] = dx[last - 1 : last] + row

        tabs = [jnp.broadcast_to(tables[i, 0:1], (BLOCK, entries)) for i in range(8)]

        def block(b, carry):
            rows = pl.ds(pl.multiple_of(b * BLOCK, BLOCK), BLOCK)
            for start in range(0, width, LANES):
                here = slice(left + start, left + start + LANES)
                local = slice(start, start + LANES)
                accum = [jnp.zeros((BLOCK, LANES), F32) for _ in range(3)]
                transmit = jnp.ones((BLOCK, LANES), F32)
                prev = before[b, :, here].astype(F32)
                centre = stack[0][0][stack[0][1], b, parity, :, here].astype(F32)
                for s in range(2 * slices):
                    if s + 1 < 2 * slices:
                        ref, z = stack[s + 1]
                        following = ref[z, b, parity, :, here].astype(F32)
                    else:
                        following = after[b, :, here].astype(F32)
                    dz = following - prev
                    dx = dx_ref[s, rows, local]
                    dy = dy_ref[s, rows, local]
                    position = centre * float(entries - 1)
                    knot = position.astype(jnp.int32)
                    part = position - knot.astype(F32)
                    upper = part.astype(BF16).astype(F32)
                    lower = (1.0 - part).astype(BF16).astype(F32)
                    values = [
                        lower * look_up(tabs[c], knot) + upper * look_up(tabs[c + 4], knot)
                        for c in range(4)
                    ]
                    lambert = jnp.abs(2.0 * (dz + dy) + dx) * (0.7 / 6.0)
                    square = 0.25 * (dz * dz + dx * dx + dy * dy) + 0.01
                    shading = 0.3 + lambert * lax.rsqrt(square)
                    clear = jnp.exp2(values[3])
                    gain = transmit * (1.0 - clear) * shading
                    transmit = transmit * clear
                    accum = [a + gain * v for a, v in zip(accum, values[:3])]
                    prev, centre = centre, following
                for c in range(3):
                    out[b, c * BLOCK : (c + 1) * BLOCK, local] = accum[c]
                out[b, 3 * BLOCK : 4 * BLOCK, local] = (1.0 - transmit) * tables[8, 0:1, 0:1]
            return carry

        lax.fori_loop(0, blocks, block, 0)

    @pl.when(core[0] == 0)
    def _():
        slab(own, other, outer_own, outer_other, edge_own, edge_other, 0)

    @pl.when(core[0] != 0)
    def _():
        slab(other, own, outer_other, outer_own, edge_other, edge_own, 1)


def merge_kernel(scales, *refs):
    ins, out = refs[:-1], refs[-1]
    width = ins[0].shape[2]
    cols = width * len(ins)
    for q, ref in enumerate(ins):
        for start in range(0, width, LANES):
            local = slice(start, start + LANES)
            accum = [jnp.zeros((BLOCK, LANES), F32) for _ in range(3)]
            transmit = jnp.ones((BLOCK, LANES), F32)
            for s in range(ref.shape[0]):
                for c in range(3):
                    accum[c] = accum[c] + transmit * ref[s, c * BLOCK : (c + 1) * BLOCK, local]
                opacity = ref[s, 3 * BLOCK : 4 * BLOCK, local] * scales[1]
                transmit = transmit - transmit * opacity
            image = [a * scales[0] for a in accum] + [1.0 - transmit]
            for c in range(4):
                for r in range(BLOCK):
                    at = r * cols + q * width + start
                    out[c : c + 1, at : at + LANES] = image[c][r : r + 1]


def shards(volume, transfer_table):
    slices, rows, cols = volume.shape
    depth_count = lax.axis_size("depth")
    img_count = lax.axis_size("img")
    chips = depth_count // 2
    depth_total = slices * depth_count
    entries = transfer_table.shape[1]
    blocks = rows // (2 * BLOCK)
    width = cols // CHUNKS
    core = lax.axis_index("depth") % 2

    def shift(x, img_step, depth_step):
        pairs = []
        for i in range(img_count):
            for d in range(depth_count):
                to_i, to_d = i + img_step(d % 2), d + depth_step(d % 2)
                if 0 <= to_i < img_count and 0 <= to_d < depth_count:
                    pairs.append((i * depth_count + d, to_i * depth_count + to_d))
        return lax.ppermute(x, ("img", "depth"), pairs)

    other = lax.ppermute(volume, "depth", [(d, d ^ 1) for d in range(depth_count)])
    plane = lax.dynamic_index_in_dim(volume, (slices - 1) * core, 0, False)
    plane = plane.reshape(blocks, 2, BLOCK, cols)
    to_other_core = lax.dynamic_index_in_dim(plane, 1 - core, 1, False)
    to_same_core = lax.dynamic_index_in_dim(plane, core, 1, False)
    outer_own = shift(to_other_core, lambda c: 0, lambda c: 1 if c else -1)
    outer_other = shift(to_same_core, lambda c: 0, lambda c: 2 if c else -2)
    edge_same = lax.dynamic_index_in_dim(volume, (rows - 1) * (1 - core), 1, False)
    edge_cross = lax.dynamic_index_in_dim(volume, (rows - 1) * core, 1, False)
    edge_own = shift(edge_same, lambda c: -1 if c else 1, lambda c: 0)
    edge_other = shift(edge_cross, lambda c: 1 if c else -1, lambda c: -1 if c else 1)

    table = transfer_table.astype(F32)
    colour_top = jnp.maximum(jnp.max(table[0:3]), TINY)
    opacity_top = jnp.maximum(jnp.max(table[3]) * (2.0 * slices / depth_total), TINY)
    factor = jnp.concatenate(
        [
            jnp.full((3, 1), 1.0 / (colour_top * opacity_top), F32),
            jnp.full((1, 1), -np.log2(np.e) / depth_total, F32),
        ]
    )
    lower = table * factor
    upper = jnp.concatenate([lower[:, 1:], lower[:, -1:]], axis=1)
    scale_row = jnp.full((1, entries), 1.0 / opacity_top, F32)
    tables = jnp.concatenate([lower, upper, scale_row])[:, None, :]
    scales = jnp.stack([colour_top * opacity_top, opacity_top])

    split = (slices, blocks, 2, BLOCK, cols)
    own_view, other_view = volume.reshape(split), other.reshape(split)
    rows_op = jnp.asarray(row_differences(rows), BF16)
    cols_op = jnp.asarray(column_differences(cols), BF16)
    core_arg = core.astype(jnp.int32).reshape(1)
    same_core = [[2 * j + c for j in range(chips)] for c in range(2)]
    vmem = pl.BlockSpec(memory_space=pltpu.MemorySpace.VMEM)
    smem = pl.BlockSpec(memory_space=pltpu.MemorySpace.SMEM)
    received = []
    for q in range(CHUNKS):
        partial_image = pl.pallas_call(
            functools.partial(slab_kernel, chunk=q, width=width),
            out_shape=jax.ShapeDtypeStruct((blocks, 4 * BLOCK, width), F32),
            in_specs=[smem] + [vmem] * 9,
            out_specs=vmem,
            scratch_shapes=[pltpu.VMEM((2 * slices, blocks * BLOCK, width), F32)] * 2,
            compiler_params=pltpu.CompilerParams(vmem_limit_bytes=40 << 20),
            name="slab",
        )(
            core_arg, own_view, other_view, outer_own, outer_other, edge_own, edge_other,
            rows_op, cols_op, tables,
        )
        pieces = partial_image.astype(jnp.float16)
        pieces = lax.all_to_all(
            pieces, "depth", split_axis=0, concat_axis=0, tiled=True, axis_index_groups=same_core
        )
        received.append(pieces.astype(F32))
    return pl.pallas_call(
        merge_kernel,
        out_shape=jax.ShapeDtypeStruct((4, BLOCK * cols), F32),
        in_specs=[smem] + [vmem] * CHUNKS,
        out_specs=vmem,
        name="merge",
    )(scales, *received)


def solution(mesh):
    placed = (P("depth", "img", None), P())
    return jax.shard_map(
        shards, mesh=mesh, in_specs=placed, out_specs=P(None, ("img", "depth")), check_vma=False
    )
```

```python
import functools

import jax
import jax.numpy as jnp
import numpy as np
from jax import lax
from jax.experimental import pallas as pl
from jax.experimental.pallas import tpu as pltpu
from jax.sharding import PartitionSpec as P

F32 = jnp.float32
BF16 = jnp.bfloat16
LANES = 128
EARLY = 3


def column_differences(cols):
    k = np.arange(cols)
    return (k[:, None] == k[None, :] + 1).astype(np.float32) - (
        k[:, None] == k[None, :] - 1
    ).astype(np.float32)


def look_up(table, index):
    return jnp.take_along_axis(table, index, axis=1, mode="promise_in_bounds")


def classify(centre, tabs, entries):
    position = centre * float(entries - 1)
    knot = position.astype(jnp.int32)
    part = position - knot.astype(F32)
    upper = part.astype(BF16).astype(F32)
    lower = (1.0 - part).astype(BF16).astype(F32)
    values = [
        lower * look_up(tabs[c], knot) + upper * look_up(tabs[c + 4], knot) for c in range(4)
    ]
    return values[:3] + [jnp.exp2(values[3])]


def spread_tables(tables, rows):
    return [jnp.broadcast_to(tables[i, 0:1], (rows, tables.shape[2])) for i in range(8)]


def classify_kernel(cells, cols_op, tables, values, dy, *, rows):
    entries = tables.shape[2]
    total, cols = cells.shape
    tabs = spread_tables(tables, rows)
    dy[...] = jnp.dot(cells[...], cols_op[...], preferred_element_type=F32)

    def block(b, carry):
        here = pl.ds(pl.multiple_of(b * rows, rows), rows)
        for start in range(0, cols, LANES):
            lanes = slice(start, start + LANES)
            found = classify(cells[here, lanes].astype(F32), tabs, entries)
            for c in range(4):
                values[c, here, lanes] = found[c]
        return carry

    lax.fori_loop(0, total // rows, block, 0)


def composite_kernel(early, late, values, dy_early, cols_op, tables, out, dy_late, *, rows):
    slabs, early_rows, cols = early.shape
    entries = tables.shape[2]
    count = early_rows // rows
    slices = count + 1
    tabs = spread_tables(tables, rows)
    for s in range(slabs):
        dy_late[s * rows : (s + 1) * rows] = jnp.dot(
            late[s, 0:rows], cols_op[...], preferred_element_type=F32
        )
    row = lax.broadcasted_iota(jnp.int32, (rows, LANES), 0)
    first, last = row == 0, row == rows - 1

    for start in range(0, cols, LANES):
        lanes = slice(start, start + LANES)

        def slab(s, carry):
            accum, transmit, prev, centre = carry
            accum = list(accum)
            halo = late[s, rows : rows + 2 * slices, lanes].astype(F32)
            after = jnp.minimum(s + 1, slabs - 1)
            inside = jnp.where(s + 1 < slabs, 1.0, 0.0)
            stack = [early[s, q * rows : (q + 1) * rows, lanes].astype(F32) for q in range(1, count)]
            stack.append(late[s, 0:rows, lanes].astype(F32))
            stack.append(early[after, 0:rows, lanes].astype(F32) * inside)
            for q in range(slices):
                following = stack[q]
                if q < count:
                    here = pl.ds(pl.multiple_of(s * early_rows + q * rows, rows), rows)
                    found = [values[c, here, lanes] for c in range(4)]
                    dy = dy_early[here, lanes]
                else:
                    here = pl.ds(pl.multiple_of(s * rows, rows), rows)
                    found = classify(centre, tabs, entries)
                    dy = dy_late[here, lanes]
                above = jnp.where(first, halo[q : q + 1], pltpu.roll(centre, 1, 0))
                below = jnp.where(
                    last, halo[slices + q : slices + q + 1], pltpu.roll(centre, rows - 1, 0)
                )
                dx = below - above
                dz = following - prev
                lambert = jnp.abs(2.0 * (dz + dy) + dx) * (0.7 / 6.0)
                square = 0.25 * (dz * dz + dx * dx + dy * dy) + 0.01
                shading = 0.3 + lambert * lax.rsqrt(square)
                clear = found[3]
                gain = transmit * (1.0 - clear) * shading
                transmit = transmit * clear
                accum = [a + gain * v for a, v in zip(accum, found[:3])]
                prev, centre = centre, following
            return tuple(accum), transmit, prev, centre

        zero = jnp.zeros((rows, LANES), F32)
        state = ((zero, zero, zero), zero + 1.0, zero, early[0, 0:rows, lanes].astype(F32))
        accum, transmit, _, _ = lax.fori_loop(0, slabs, slab, state)
        image = list(accum) + [1.0 - transmit]
        for c in range(4):
            for r in range(rows):
                at = r * cols + start
                out[c : c + 1, at : at + LANES] = image[c][r : r + 1]


def shards(volume, transfer_table):
    slices, strip, cols = volume.shape
    slabs = lax.axis_size("depth")
    img_count = lax.axis_size("img")
    depth_total = slices * slabs
    entries = transfer_table.shape[1]
    rows = strip // slabs

    table = transfer_table.astype(F32)
    factor = np.array([[1.0], [1.0], [1.0], [-np.log2(np.e) / depth_total]], np.float32)
    lower = table * factor
    upper = jnp.concatenate([lower[:, 1:], lower[:, -1:]], axis=1)
    tables = jnp.concatenate([lower, upper])[:, None, :]
    cols_op = jnp.asarray(column_differences(cols), BF16)

    def exchange(pieces):
        return lax.all_to_all(pieces, "depth", split_axis=0, concat_axis=0, tiled=True)

    blocks = volume.reshape(slices, slabs, rows, cols)
    early = exchange(
        jnp.swapaxes(blocks[:EARLY], 0, 1).reshape(slabs, EARLY * rows, cols)
    )
    forward = [(i, i + 1) for i in range(img_count - 1)]
    backward = [(i + 1, i) for i in range(img_count - 1)]
    top_edge = lax.ppermute(volume[:, strip - 1], "img", forward)
    bottom_edge = lax.ppermute(volume[:, 0], "img", backward)
    top = jnp.concatenate([top_edge[:, None], blocks[:, :-1, rows - 1]], axis=1)
    bottom = jnp.concatenate([blocks[:, 1:, 0], bottom_edge[:, None]], axis=1)
    late = exchange(
        jnp.concatenate(
            [blocks[EARLY], jnp.swapaxes(top, 0, 1), jnp.swapaxes(bottom, 0, 1)], axis=1
        )
    )

    vmem = pl.BlockSpec(memory_space=pltpu.MemorySpace.VMEM)
    total = slabs * EARLY * rows
    values, dy_early = pl.pallas_call(
        functools.partial(classify_kernel, rows=rows),
        out_shape=(
            jax.ShapeDtypeStruct((4, total, cols), F32),
            jax.ShapeDtypeStruct((total, cols), F32),
        ),
        in_specs=[vmem] * 3,
        out_specs=(vmem, vmem),
        compiler_params=pltpu.CompilerParams(vmem_limit_bytes=40 << 20),
        name="classify",
    )(early.reshape(total, cols), cols_op, tables)
    return pl.pallas_call(
        functools.partial(composite_kernel, rows=rows),
        out_shape=jax.ShapeDtypeStruct((4, rows * cols), F32),
        in_specs=[vmem] * 6,
        out_specs=vmem,
        scratch_shapes=[pltpu.VMEM((slabs * rows, cols), F32)],
        compiler_params=pltpu.CompilerParams(vmem_limit_bytes=40 << 20),
        name="composite",
    )(early, late, values, dy_early, cols_op, tables)


def solution(mesh):
    placed = (P("depth", "img", None), P())
    return jax.shard_map(
        shards, mesh=mesh, in_specs=placed, out_specs=P(None, ("img", "depth")), check_vma=False
    )
```

```python
import jax
import jax.numpy as jnp
import numpy as np
from jax import lax
from jax.experimental import pallas as pl
from jax.experimental.pallas import tpu as pltpu
from jax.sharding import PartitionSpec as P

F32 = jnp.float32
BF16 = jnp.bfloat16
BLOCK = 16
HALF = 8
LANES = 128
TINY = 1e-30


def row_differences(rows):
    local = np.arange(rows // 2)
    out = np.zeros((2, rows // 2, rows), np.float32)
    for parity in range(2):
        own = local // BLOCK * (2 * BLOCK) + parity * BLOCK + local % BLOCK
        for step in (1, -1):
            there = own + step
            keep = (there >= 0) & (there < rows)
            out[parity, local[keep], there[keep]] += step
    return out


def column_differences(cols):
    k = np.arange(cols)
    return (k[:, None] == k[None, :] + 1).astype(np.float32) - (
        k[:, None] == k[None, :] - 1
    ).astype(np.float32)


def look_up(table, index):
    return jnp.take_along_axis(table, index, axis=1, mode="promise_in_bounds")


def classify(centre, tabs):
    position = centre * float(tabs[0].shape[1] - 1)
    knot = position.astype(jnp.int32)
    part = position - knot.astype(F32)
    upper = part.astype(BF16).astype(F32)
    lower = (1.0 - part).astype(BF16).astype(F32)
    values = [
        lower * look_up(tabs[c], knot) + upper * look_up(tabs[c + 4], knot) for c in range(4)
    ]
    return values[:3] + [jnp.exp2(values[3])]


def spread(tables):
    return [jnp.broadcast_to(tables[i, 0:1], (HALF, tables.shape[2])) for i in range(8)]


def plane_terms(cells, z, parity, edge, core, rows_op, cols_op, slope, norm):
    blocks, cols = cells.shape[1], cells.shape[4]
    rows = blocks * BLOCK
    dx = jnp.dot(
        rows_op[parity], cells[z].reshape(2 * rows, cols), preferred_element_type=F32
    )
    dy = jnp.dot(
        cells[z, :, parity].reshape(rows, cols), cols_op[...], preferred_element_type=F32
    )
    slope[z] = 2.0 * dy + dx
    norm[z] = dx * dx + dy * dy
    halo = edge[z : z + 1, :].astype(F32)
    for at, sign in ((0, jnp.where(core == 0, -1.0, 0.0)), (rows - 1, jnp.where(core == 0, 0.0, 1.0))):
        dx_row = dx[at : at + 1] + halo * sign
        dy_row = dy[at : at + 1]
        slope[z, at : at + 1, :] = 2.0 * dy_row + dx_row
        norm[z, at : at + 1, :] = dx_row * dx_row + dy_row * dy_row


def own_kernel(core_ref, own, edge, rows_op, cols_op, tables, values, slope, norm):
    slices, blocks, _, _, cols = own.shape
    core = core_ref[0]
    for z in range(slices):
        plane_terms(own, z, core, edge, core, rows_op, cols_op, slope, norm)
    tabs = spread(tables)

    def block(b, carry):
        for z in range(slices):
            for half in range(0, BLOCK, HALF):
                here = pl.ds(pl.multiple_of(b * BLOCK + half, HALF), HALF)
                for start in range(0, cols, LANES):
                    lanes = slice(start, start + LANES)
                    centre = own[z, b, core, half : half + HALF, lanes].astype(F32)
                    found = classify(centre, tabs)
                    for c in range(4):
                        values[c, z, here, lanes] = found[c]
        return carry

    lax.fori_loop(0, blocks, block, 0)


def slab_kernel(
    core_ref, own, other, outer_own, outer_other, edge, rows_op, cols_op, tables,
    values, own_slope, own_norm, out, slope, norm,
):
    slices, blocks, _, _, cols = own.shape
    core = core_ref[0]
    front = core == 0
    for z in range(slices):
        plane_terms(other, z, core, edge, core, rows_op, cols_op, slope, norm)
    tabs = spread(tables)
    opacity_scale = tables[8, 0:1, 0:1]

    def shade(accum, transmit, dz, slope_xy, norm_xy, found):
        lambert = jnp.abs(2.0 * dz + slope_xy) * (0.7 / 6.0)
        shading = 0.3 + lambert * lax.rsqrt(0.25 * (dz * dz + norm_xy) + 0.01)
        gain = transmit * (1.0 - found[3]) * shading
        return [a + gain * v for a, v in zip(accum, found[:3])], transmit * found[3]

    def block(b, carry):
        for half in range(0, BLOCK, HALF):
            here = pl.ds(pl.multiple_of(b * BLOCK + half, HALF), HALF)
            rows = slice(half, half + HALF)
            for start in range(0, cols, LANES):
                lanes = slice(start, start + LANES)
                mine = [own[z, b, core, rows, lanes].astype(F32) for z in range(slices)]
                theirs = [other[z, b, core, rows, lanes].astype(F32) for z in range(slices)]
                end_own = outer_own[b, rows, lanes].astype(F32)
                end_other = outer_other[b, rows, lanes].astype(F32)
                stack = (
                    [jnp.where(front, end_own, theirs[-1])]
                    + mine
                    + [jnp.where(front, theirs[0], end_own)]
                )
                accum = [jnp.zeros((HALF, LANES), F32) for _ in range(3)]
                transmit = jnp.ones((HALF, LANES), F32)
                for z in range(slices):
                    found = [values[c, z, here, lanes] for c in range(4)]
                    accum, transmit = shade(
                        accum, transmit, stack[z + 2] - stack[z],
                        own_slope[z, here, lanes], own_norm[z, here, lanes], found,
                    )
                own_part = accum + [transmit]
                stack = (
                    [jnp.where(front, mine[-1], end_other)]
                    + theirs
                    + [jnp.where(front, end_other, mine[0])]
                )
                accum = [jnp.zeros((HALF, LANES), F32) for _ in range(3)]
                transmit = jnp.ones((HALF, LANES), F32)
                for z in range(slices):
                    accum, transmit = shade(
                        accum, transmit, stack[z + 2] - stack[z],
                        slope[z, here, lanes], norm[z, here, lanes], classify(theirs[z], tabs),
                    )
                other_part = accum + [transmit]
                near = [jnp.where(front, a, o) for a, o in zip(own_part, other_part)]
                far = [jnp.where(front, o, a) for a, o in zip(own_part, other_part)]
                for c in range(3):
                    at = c * BLOCK + half
                    out[b, at : at + HALF, lanes] = near[c] + near[3] * far[c]
                at = 3 * BLOCK + half
                out[b, at : at + HALF, lanes] = (1.0 - near[3] * far[3]) * opacity_scale
        return carry

    lax.fori_loop(0, blocks, block, 0)


def merge_kernel(scales, parts, out):
    cols = parts.shape[2]
    for start in range(0, cols, LANES):
        lanes = slice(start, start + LANES)
        accum = [jnp.zeros((BLOCK, LANES), F32) for _ in range(3)]
        transmit = jnp.ones((BLOCK, LANES), F32)
        for s in range(parts.shape[0]):
            for c in range(3):
                accum[c] = accum[c] + transmit * parts[s, c * BLOCK : (c + 1) * BLOCK, lanes]
            opacity = parts[s, 3 * BLOCK : 4 * BLOCK, lanes] * scales[1]
            transmit = transmit - transmit * opacity
        image = [a * scales[0] for a in accum] + [1.0 - transmit]
        for c in range(4):
            for r in range(BLOCK):
                at = r * cols + start
                out[c : c + 1, at : at + LANES] = image[c][r : r + 1]


def shards(volume, transfer_table):
    slices, rows, cols = volume.shape
    depth_count = lax.axis_size("depth")
    img_count = lax.axis_size("img")
    chips = depth_count // 2
    depth_total = slices * depth_count
    entries = transfer_table.shape[1]
    blocks = rows // (2 * BLOCK)
    core = lax.axis_index("depth") % 2

    def shift(x, img_step, depth_step):
        pairs = []
        for i in range(img_count):
            for d in range(depth_count):
                to_i, to_d = i + img_step(d % 2), d + depth_step(d % 2)
                if 0 <= to_i < img_count and 0 <= to_d < depth_count:
                    pairs.append((i * depth_count + d, to_i * depth_count + to_d))
        return lax.ppermute(x, ("img", "depth"), pairs)

    edge_same = lax.dynamic_index_in_dim(volume, (rows - 1) * (1 - core), 1, False)
    edge_cross = lax.dynamic_index_in_dim(volume, (rows - 1) * core, 1, False)
    edge_own = shift(edge_same, lambda c: -1 if c else 1, lambda c: 0)
    edge_other = shift(edge_cross, lambda c: 1 if c else -1, lambda c: -1 if c else 1)
    plane = lax.dynamic_index_in_dim(volume, (slices - 1) * core, 0, False)
    plane = plane.reshape(blocks, 2, BLOCK, cols)
    to_other_core = lax.dynamic_index_in_dim(plane, 1 - core, 1, False)
    to_same_core = lax.dynamic_index_in_dim(plane, core, 1, False)
    outer_own = shift(to_other_core, lambda c: 0, lambda c: 1 if c else -1)
    outer_other = shift(to_same_core, lambda c: 0, lambda c: 2 if c else -2)
    other = lax.ppermute(volume, "depth", [(d, d ^ 1) for d in range(depth_count)])

    table = transfer_table.astype(F32)
    colour_top = jnp.maximum(jnp.max(table[0:3]), TINY)
    opacity_top = jnp.maximum(jnp.max(table[3]) * (2.0 * slices / depth_total), TINY)
    factor = jnp.concatenate(
        [
            jnp.full((3, 1), 1.0 / (colour_top * opacity_top), F32),
            jnp.full((1, 1), -np.log2(np.e) / depth_total, F32),
        ]
    )
    lower = table * factor
    upper = jnp.concatenate([lower[:, 1:], lower[:, -1:]], axis=1)
    scale_row = jnp.full((1, entries), 1.0 / opacity_top, F32)
    tables = jnp.concatenate([lower, upper, scale_row])[:, None, :]
    scales = jnp.stack([colour_top * opacity_top, opacity_top])

    split = (slices, blocks, 2, BLOCK, cols)
    own_view, other_view = volume.reshape(split), other.reshape(split)
    rows_op = jnp.asarray(row_differences(rows), BF16)
    cols_op = jnp.asarray(column_differences(cols), BF16)
    core_arg = core.astype(jnp.int32).reshape(1)
    same_core = [[2 * j + c for j in range(chips)] for c in range(2)]
    vmem = pl.BlockSpec(memory_space=pltpu.MemorySpace.VMEM)
    smem = pl.BlockSpec(memory_space=pltpu.MemorySpace.SMEM)
    half = rows // 2
    values, own_slope, own_norm = pl.pallas_call(
        own_kernel,
        out_shape=(
            jax.ShapeDtypeStruct((4, slices, half, cols), F32),
            jax.ShapeDtypeStruct((slices, half, cols), F32),
            jax.ShapeDtypeStruct((slices, half, cols), F32),
        ),
        in_specs=[smem] + [vmem] * 5,
        out_specs=(vmem,) * 3,
        compiler_params=pltpu.CompilerParams(vmem_limit_bytes=20 << 20),
        name="own",
    )(core_arg, own_view, edge_own, rows_op, cols_op, tables)
    partial_image = pl.pallas_call(
        slab_kernel,
        out_shape=jax.ShapeDtypeStruct((blocks, 4 * BLOCK, cols), F32),
        in_specs=[smem] + [vmem] * 11,
        out_specs=vmem,
        scratch_shapes=[pltpu.VMEM((slices, half, cols), F32)] * 2,
        compiler_params=pltpu.CompilerParams(vmem_limit_bytes=20 << 20),
        name="slab",
    )(
        core_arg, own_view, other_view, outer_own, outer_other, edge_other,
        rows_op, cols_op, tables, values, own_slope, own_norm,
    )
    pieces = lax.all_to_all(
        partial_image.astype(jnp.float16), "depth", split_axis=0, concat_axis=0, tiled=True,
        axis_index_groups=same_core,
    )
    return pl.pallas_call(
        merge_kernel,
        out_shape=jax.ShapeDtypeStruct((4, BLOCK * cols), F32),
        in_specs=[smem, vmem],
        out_specs=vmem,
        name="merge",
    )(scales, pieces.astype(F32))


def solution(mesh):
    placed = (P("depth", "img", None), P())
    return jax.shard_map(
        shards, mesh=mesh, in_specs=placed, out_specs=P(None, ("img", "depth")), check_vma=False
    )
```

```python
import functools

import jax
import jax.numpy as jnp
import numpy as np
from jax import lax
from jax.experimental import pallas as pl
from jax.experimental.pallas import tpu as pltpu
from jax.sharding import PartitionSpec as P

F32 = jnp.float32
BF16 = jnp.bfloat16
BLOCK = 16
HALF = 8
LANES = 128
TINY = 1e-30


def row_differences(rows, core):
    shape = (rows // 2, rows)
    local = lax.broadcasted_iota(jnp.int32, shape, 0)
    there = lax.broadcasted_iota(jnp.int32, shape, 1)
    step = there - (local + (local & -BLOCK) + core * BLOCK)
    return jnp.where(step == 1, 1.0, jnp.where(step == -1, -1.0, 0.0)).astype(BF16)


def column_differences(cols):
    step = lax.broadcasted_iota(jnp.int32, (cols, cols), 0) - lax.broadcasted_iota(
        jnp.int32, (cols, cols), 1
    )
    return jnp.where(step == 1, 1.0, jnp.where(step == -1, -1.0, 0.0)).astype(BF16)


def tops(table, slab_share):
    colour = jnp.max(jnp.max(table[0:3], axis=0, keepdims=True), axis=1, keepdims=True)
    extinction = jnp.max(table[3:4], axis=1, keepdims=True)
    return jnp.maximum(colour, TINY), jnp.maximum(extinction * slab_share, TINY)


def spread(table, slab_share, depth_total):
    entries = table.shape[1]
    colour_top, opacity_top = tops(table, slab_share)
    scale = 1.0 / (colour_top * opacity_top)
    lower = [table[c : c + 1] * scale for c in range(3)]
    lower.append(table[3:4] * float(-np.log2(np.e) / depth_total))
    lower = [jnp.broadcast_to(t, (HALF, entries)) for t in lower]
    last = lax.broadcasted_iota(jnp.int32, (HALF, entries), 1) == entries - 1
    upper = [jnp.where(last, t, pltpu.roll(t, entries - 1, 1)) for t in lower]
    return lower + upper


def look_up(table, index):
    return jnp.take_along_axis(table, index, axis=1, mode="promise_in_bounds")


def classify(centre, tabs):
    position = centre * float(tabs[0].shape[1] - 1)
    knot = position.astype(jnp.int32)
    part = position - knot.astype(F32)
    upper = part.astype(BF16).astype(F32)
    lower = (1.0 - part).astype(BF16).astype(F32)
    values = [
        lower * look_up(tabs[c], knot) + upper * look_up(tabs[c + 4], knot) for c in range(4)
    ]
    return values[:3] + [jnp.exp2(values[3])]


def plane_terms(cells, z, edge, core, rows_op, cols_op, slope, norm):
    blocks, cols = cells.shape[1], cells.shape[4]
    rows = blocks * BLOCK
    dx = jnp.dot(rows_op[...], cells[z].reshape(2 * rows, cols), preferred_element_type=F32)
    dy = jnp.dot(
        cells[z, :, core].reshape(rows, cols), cols_op[...], preferred_element_type=F32
    )
    slope[z] = 2.0 * dy + dx
    norm[z] = dx * dx + dy * dy
    halo = edge[z : z + 1, :].astype(F32)
    top, bottom = jnp.where(core == 0, -1.0, 0.0), jnp.where(core == 0, 0.0, 1.0)
    for at, sign in ((0, top), (rows - 1, bottom)):
        dx_row = dx[at : at + 1] + halo * sign
        dy_row = dy[at : at + 1]
        slope[z, at : at + 1, :] = 2.0 * dy_row + dx_row
        norm[z, at : at + 1, :] = dx_row * dx_row + dy_row * dy_row


def shade(accum, transmit, dz, slope_xy, norm_xy, found):
    lambert = jnp.abs(2.0 * dz + slope_xy) * (0.7 / 6.0)
    shading = 0.3 + lambert * lax.rsqrt(0.25 * (dz * dz + norm_xy) + 0.01)
    gain = transmit * (1.0 - found[3]) * shading
    return [a + gain * v for a, v in zip(accum, found[:3])], transmit * found[3]


def over(near, far):
    return [n + near[3] * f for n, f in zip(near[:3], far[:3])] + [near[3] * far[3]]


def nothing():
    return [jnp.zeros((HALF, LANES), F32)] * 3, jnp.ones((HALF, LANES), F32)


def own_kernel(
    core_ref, own, edge, table, first, last, middle, slope, norm, rows_op, cols_op,
    *, slab_share, depth_total,
):
    slices, blocks, _, _, cols = own.shape
    core = core_ref[0]
    rows_op[...] = row_differences(2 * blocks * BLOCK, core)
    cols_op[...] = column_differences(cols)
    for z in range(slices):
        plane_terms(own, z, edge, core, rows_op, cols_op, slope, norm)
    tabs = spread(table[...].astype(F32), slab_share, depth_total)

    def block(b, carry):
        for half in range(0, BLOCK, HALF):
            here = pl.ds(pl.multiple_of(b * BLOCK + half, HALF), HALF)
            rows = slice(half, half + HALF)
            for start in range(0, cols, LANES):
                lanes = slice(start, start + LANES)
                mine = [own[z, b, core, rows, lanes].astype(F32) for z in range(slices)]
                accum, transmit = nothing()
                for z in range(slices):
                    found = classify(mine[z], tabs)
                    if z in (0, slices - 1):
                        ref = last if z else first
                        for c in range(4):
                            ref[c, here, lanes] = found[c]
                    else:
                        accum, transmit = shade(
                            accum, transmit, mine[z + 1] - mine[z - 1],
                            slope[z, here, lanes], norm[z, here, lanes], found,
                        )
                for c in range(3):
                    middle[c, here, lanes] = accum[c]
                middle[3, here, lanes] = transmit
        return carry

    lax.fori_loop(0, blocks, block, 0)


def slab_kernel(
    core_ref, own, other, outer_own, outer_other, edge, table,
    first, last, middle, own_slope, own_norm, rows_op, cols_op, out, slope, norm,
    *, slab_share, depth_total,
):
    slices, blocks, _, _, cols = own.shape
    core = core_ref[0]
    front = core == 0
    for z in range(slices):
        plane_terms(other, z, edge, core, rows_op, cols_op, slope, norm)
    table_values = table[...].astype(F32)
    tabs = spread(table_values, slab_share, depth_total)
    opacity_scale = 1.0 / tops(table_values, slab_share)[1]

    def block(b, carry):
        for half in range(0, BLOCK, HALF):
            here = pl.ds(pl.multiple_of(b * BLOCK + half, HALF), HALF)
            rows = slice(half, half + HALF)
            for start in range(0, cols, LANES):
                lanes = slice(start, start + LANES)
                mine = [own[z, b, core, rows, lanes].astype(F32) for z in range(slices)]
                theirs = [other[z, b, core, rows, lanes].astype(F32) for z in range(slices)]
                end_own = outer_own[b, rows, lanes].astype(F32)
                end_other = outer_other[b, rows, lanes].astype(F32)

                def one(found, dz, z):
                    accum, transmit = shade(
                        *nothing(), dz, own_slope[z, here, lanes], own_norm[z, here, lanes],
                        [found[c, here, lanes] for c in range(4)],
                    )
                    return accum + [transmit]

                end = slices - 1
                own_part = over(
                    one(first, mine[1] - jnp.where(front, end_own, theirs[end]), 0),
                    over(
                        [middle[c, here, lanes] for c in range(4)],
                        one(last, jnp.where(front, theirs[0], end_own) - mine[end - 1], end),
                    ),
                )
                stack = (
                    [jnp.where(front, mine[end], end_other)]
                    + theirs
                    + [jnp.where(front, end_other, mine[0])]
                )
                accum, transmit = nothing()
                for z in range(slices):
                    accum, transmit = shade(
                        accum, transmit, stack[z + 2] - stack[z],
                        slope[z, here, lanes], norm[z, here, lanes], classify(theirs[z], tabs),
                    )
                other_part = accum + [transmit]
                near = [jnp.where(front, a, o) for a, o in zip(own_part, other_part)]
                far = [jnp.where(front, o, a) for a, o in zip(own_part, other_part)]
                both = over(near, far)
                both[3] = (1.0 - both[3]) * opacity_scale
                for c in range(4):
                    at = c * BLOCK + half
                    out[b, at : at + HALF, lanes] = both[c]
        return carry

    lax.fori_loop(0, blocks, block, 0)


def merge_kernel(parts, table, out, image, *, slab_share):
    cols = parts.shape[2]
    colour_top, opacity_top = tops(table[...].astype(F32), slab_share)
    for half in range(0, BLOCK, HALF):
        for start in range(0, cols, LANES):
            lanes = slice(start, start + LANES)
            accum, transmit = nothing()
            for s in range(parts.shape[0]):
                part = [
                    parts[s, c * BLOCK + half : c * BLOCK + half + HALF, lanes] for c in range(4)
                ]
                accum = [a + transmit * p for a, p in zip(accum, part[:3])]
                transmit = transmit - transmit * (part[3] * opacity_top)
            whole = [a * (colour_top * opacity_top) for a in accum] + [1.0 - transmit]
            for c in range(4):
                at = start // LANES, slice(c * BLOCK + half, c * BLOCK + half + HALF)
                image[at] = whole[c]
    for r in range(BLOCK):
        for start in range(0, cols, LANES):
            out[:, r * cols + start : r * cols + start + LANES] = image[
                start // LANES, pl.ds(r, 4, stride=BLOCK)
            ]


def shards(volume, transfer_table):
    slices, rows, cols = volume.shape
    depth_count = lax.axis_size("depth")
    img_count = lax.axis_size("img")
    chips = depth_count // 2
    depth_total = slices * depth_count
    blocks = rows // (2 * BLOCK)
    core = lax.axis_index("depth") % 2

    def shift(x, img_step, depth_step):
        pairs = []
        for i in range(img_count):
            for d in range(depth_count):
                to_i, to_d = i + img_step(d % 2), d + depth_step(d % 2)
                if 0 <= to_i < img_count and 0 <= to_d < depth_count:
                    pairs.append((i * depth_count + d, to_i * depth_count + to_d))
        return lax.ppermute(x, ("img", "depth"), pairs)

    plane = lax.dynamic_index_in_dim(volume, (slices - 1) * core, 0, False)
    plane = plane.reshape(blocks, 2, BLOCK, cols)
    to_other_core = lax.dynamic_index_in_dim(plane, 1 - core, 1, False)
    to_same_core = lax.dynamic_index_in_dim(plane, core, 1, False)
    edge_same = lax.dynamic_index_in_dim(volume, (rows - 1) * (1 - core), 1, False)
    edge_cross = lax.dynamic_index_in_dim(volume, (rows - 1) * core, 1, False)
    to_other_core, to_same_core, edge_same, edge_cross = lax.optimization_barrier(
        (to_other_core, to_same_core, edge_same, edge_cross)
    )
    outer_other = shift(to_same_core, lambda c: 0, lambda c: 2 if c else -2)
    outer_own = shift(to_other_core, lambda c: 0, lambda c: 1 if c else -1)
    edge_own = shift(edge_same, lambda c: -1 if c else 1, lambda c: 0)
    edge_other = shift(edge_cross, lambda c: 1 if c else -1, lambda c: -1 if c else 1)
    held = lax.optimization_barrier((volume, edge_own, edge_other))[0]
    other = lax.ppermute(held, "depth", [(d, d ^ 1) for d in range(depth_count)])

    split = (slices, blocks, 2, BLOCK, cols)
    own_view, other_view = volume.reshape(split), other.reshape(split)
    core_arg = core.astype(jnp.int32).reshape(1)
    same_core = [[2 * j + c for j in range(chips)] for c in range(2)]
    vmem = pl.BlockSpec(memory_space=pltpu.MemorySpace.VMEM)
    smem = pl.BlockSpec(memory_space=pltpu.MemorySpace.SMEM)
    half = rows // 2
    shares = dict(slab_share=2.0 * slices / depth_total, depth_total=depth_total)
    params = pltpu.CompilerParams(vmem_limit_bytes=16 << 20)
    quad = jax.ShapeDtypeStruct((4, half, cols), F32)
    slab_terms = jax.ShapeDtypeStruct((slices, half, cols), F32)
    own_terms = pl.pallas_call(
        functools.partial(own_kernel, **shares),
        out_shape=(
            quad, quad, quad, slab_terms, slab_terms,
            jax.ShapeDtypeStruct((half, rows), BF16),
            jax.ShapeDtypeStruct((cols, cols), BF16),
        ),
        in_specs=[smem] + [vmem] * 3,
        out_specs=(vmem,) * 7,
        compiler_params=params,
        name="own",
    )(core_arg, own_view, edge_own, transfer_table)
    partial_image = pl.pallas_call(
        functools.partial(slab_kernel, **shares),
        out_shape=jax.ShapeDtypeStruct((blocks, 4 * BLOCK, cols), F32),
        in_specs=[smem] + [vmem] * 13,
        out_specs=vmem,
        scratch_shapes=[pltpu.VMEM((slices, half, cols), F32)] * 2,
        compiler_params=params,
        name="slab",
    )(
        core_arg, own_view, other_view, outer_own, outer_other, edge_other, transfer_table,
        *own_terms,
    )
    pieces = lax.all_to_all(
        partial_image.astype(jnp.float16), "depth", split_axis=0, concat_axis=0, tiled=True,
        axis_index_groups=same_core,
    )
    return pl.pallas_call(
        functools.partial(merge_kernel, slab_share=shares["slab_share"]),
        out_shape=jax.ShapeDtypeStruct((4, BLOCK * cols), F32),
        in_specs=[vmem, vmem],
        out_specs=vmem,
        scratch_shapes=[pltpu.VMEM((cols // LANES, 4 * BLOCK, LANES), F32)],
        compiler_params=params,
        name="merge",
    )(pieces.astype(F32), transfer_table)


def solution(mesh):
    placed = (P("depth", "img", None), P())
    return jax.shard_map(
        shards, mesh=mesh, in_specs=placed, out_specs=P(None, ("img", "depth")), check_vma=False
    )
```

```python
import functools

import jax
import jax.numpy as jnp
import numpy as np
from jax import lax
from jax.experimental import pallas as pl
from jax.experimental.pallas import tpu as pltpu
from jax.sharding import PartitionSpec as P

F32 = jnp.float32
BF16 = jnp.bfloat16
BLOCK = 16
HALF = 8
LANES = 128
TINY = 1e-30


def row_differences(rows, core):
    shape = (rows // 2, rows)
    local = lax.broadcasted_iota(jnp.int32, shape, 0)
    there = lax.broadcasted_iota(jnp.int32, shape, 1)
    step = there - (local + (local & -BLOCK) + core * BLOCK)
    return jnp.where(step == 1, 1.0, jnp.where(step == -1, -1.0, 0.0)).astype(BF16)


def column_differences(cols):
    step = lax.broadcasted_iota(jnp.int32, (cols, cols), 0) - lax.broadcasted_iota(
        jnp.int32, (cols, cols), 1
    )
    return jnp.where(step == 1, 1.0, jnp.where(step == -1, -1.0, 0.0)).astype(BF16)


def tops(table, slab_share):
    colour = jnp.max(jnp.max(table[0:3], axis=0, keepdims=True), axis=1, keepdims=True)
    extinction = jnp.max(table[3:4], axis=1, keepdims=True)
    return jnp.maximum(colour, TINY), jnp.maximum(extinction * slab_share, TINY)


def spread(table, slab_share, depth_total):
    entries = table.shape[1]
    colour_top, opacity_top = tops(table, slab_share)
    scale = 1.0 / (colour_top * opacity_top)
    lower = [table[c : c + 1] * scale for c in range(3)]
    lower.append(table[3:4] * float(-np.log2(np.e) / depth_total))
    lower = [jnp.broadcast_to(t, (HALF, entries)) for t in lower]
    last = lax.broadcasted_iota(jnp.int32, (HALF, entries), 1) == entries - 1
    upper = [jnp.where(last, t, pltpu.roll(t, entries - 1, 1)) for t in lower]
    return lower + upper


def look_up(table, index):
    return jnp.take_along_axis(table, index, axis=1, mode="promise_in_bounds")


def classify(centre, tabs):
    position = centre * float(tabs[0].shape[1] - 1)
    knot = position.astype(jnp.int32)
    part = position - knot.astype(F32)
    upper = part.astype(BF16).astype(F32)
    lower = (1.0 - part).astype(BF16).astype(F32)
    values = [
        lower * look_up(tabs[c], knot) + upper * look_up(tabs[c + 4], knot) for c in range(4)
    ]
    return values[:3] + [jnp.exp2(values[3])]


def plane_terms(cells, z, edge, core, rows_op, cols_op, slope, norm):
    blocks, cols = cells.shape[1], cells.shape[4]
    rows = blocks * BLOCK
    dx = jnp.dot(rows_op[...], cells[z].reshape(2 * rows, cols), preferred_element_type=F32)
    dy = jnp.dot(
        cells[z, :, core].reshape(rows, cols), cols_op[...], preferred_element_type=F32
    )
    slope[z] = 2.0 * dy + dx
    norm[z] = dx * dx + dy * dy
    halo = edge[z].astype(F32)
    halo = jnp.where(core == 0, halo[HALF - 1 : HALF], halo[0:1])
    top, bottom = jnp.where(core == 0, -1.0, 0.0), jnp.where(core == 0, 0.0, 1.0)
    for at, sign in ((0, top), (rows - 1, bottom)):
        dx_row = dx[at : at + 1] + halo * sign
        dy_row = dy[at : at + 1]
        slope[z, at : at + 1, :] = 2.0 * dy_row + dx_row
        norm[z, at : at + 1, :] = dx_row * dx_row + dy_row * dy_row


def shade(accum, transmit, dz, slope_xy, norm_xy, found):
    lambert = jnp.abs(2.0 * dz + slope_xy) * (0.7 / 6.0)
    shading = 0.3 + lambert * lax.rsqrt(0.25 * (dz * dz + norm_xy) + 0.01)
    gain = transmit * (1.0 - found[3]) * shading
    return [a + gain * v for a, v in zip(accum, found[:3])], transmit * found[3]


def over(near, far):
    return [n + near[3] * f for n, f in zip(near[:3], far[:3])] + [near[3] * far[3]]


def nothing():
    return [jnp.zeros((HALF, LANES), F32)] * 3, jnp.ones((HALF, LANES), F32)


def own_kernel(
    core_ref, own, edge, table, first, last, middle, slope, norm, rows_op, cols_op,
    *, slab_share, depth_total,
):
    slices, blocks, _, _, cols = own.shape
    core = core_ref[0]
    rows_op[...] = row_differences(2 * blocks * BLOCK, core)
    cols_op[...] = column_differences(cols)
    for z in range(slices):
        plane_terms(own, z, edge, core, rows_op, cols_op, slope, norm)
    tabs = spread(table[...].astype(F32), slab_share, depth_total)

    def block(b, carry):
        for half in range(0, BLOCK, HALF):
            here = pl.ds(pl.multiple_of(b * BLOCK + half, HALF), HALF)
            rows = slice(half, half + HALF)
            for start in range(0, cols, LANES):
                lanes = slice(start, start + LANES)
                mine = [own[z, b, core, rows, lanes].astype(F32) for z in range(slices)]
                accum, transmit = nothing()
                for z in range(slices):
                    found = classify(mine[z], tabs)
                    if z in (0, slices - 1):
                        ref = last if z else first
                        for c in range(4):
                            ref[c, here, lanes] = found[c]
                    else:
                        accum, transmit = shade(
                            accum, transmit, mine[z + 1] - mine[z - 1],
                            slope[z, here, lanes], norm[z, here, lanes], found,
                        )
                for c in range(3):
                    middle[c, here, lanes] = accum[c]
                middle[3, here, lanes] = transmit
        return carry

    lax.fori_loop(0, blocks, block, 0)


def slab_kernel(
    core_ref, own, other, outer_own, outer_other, edge, table,
    first, last, middle, own_slope, own_norm, rows_op, cols_op, out, slope, norm,
    *, slab_share, depth_total,
):
    slices, blocks, _, _, cols = own.shape
    core = core_ref[0]
    front = core == 0
    for z in range(slices):
        plane_terms(other, z, edge, core, rows_op, cols_op, slope, norm)
    table_values = table[...].astype(F32)
    tabs = spread(table_values, slab_share, depth_total)
    opacity_scale = 1.0 / tops(table_values, slab_share)[1]

    def block(b, carry):
        for half in range(0, BLOCK, HALF):
            here = pl.ds(pl.multiple_of(b * BLOCK + half, HALF), HALF)
            rows = slice(half, half + HALF)
            for start in range(0, cols, LANES):
                lanes = slice(start, start + LANES)
                mine = [own[z, b, core, rows, lanes].astype(F32) for z in range(slices)]
                theirs = [other[z, b, core, rows, lanes].astype(F32) for z in range(slices)]
                end_own = outer_own[b, rows, lanes].astype(F32)
                end_other = outer_other[b, rows, lanes].astype(F32)

                def one(found, dz, z):
                    accum, transmit = shade(
                        *nothing(), dz, own_slope[z, here, lanes], own_norm[z, here, lanes],
                        [found[c, here, lanes] for c in range(4)],
                    )
                    return accum + [transmit]

                end = slices - 1
                own_part = over(
                    one(first, mine[1] - jnp.where(front, end_own, theirs[end]), 0),
                    over(
                        [middle[c, here, lanes] for c in range(4)],
                        one(last, jnp.where(front, theirs[0], end_own) - mine[end - 1], end),
                    ),
                )
                stack = (
                    [jnp.where(front, mine[end], end_other)]
                    + theirs
                    + [jnp.where(front, end_other, mine[0])]
                )
                accum, transmit = nothing()
                for z in range(slices):
                    accum, transmit = shade(
                        accum, transmit, stack[z + 2] - stack[z],
                        slope[z, here, lanes], norm[z, here, lanes], classify(theirs[z], tabs),
                    )
                other_part = accum + [transmit]
                near = [jnp.where(front, a, o) for a, o in zip(own_part, other_part)]
                far = [jnp.where(front, o, a) for a, o in zip(own_part, other_part)]
                both = over(near, far)
                both[3] = (1.0 - both[3]) * opacity_scale
                for c in range(4):
                    at = c * BLOCK + half
                    out[b, at : at + HALF, lanes] = both[c]
        return carry

    lax.fori_loop(0, blocks, block, 0)


def merge_kernel(parts, table, out, image, *, slab_share):
    cols = parts.shape[2]
    colour_top, opacity_top = tops(table[...].astype(F32), slab_share)
    for half in range(0, BLOCK, HALF):
        for start in range(0, cols, LANES):
            lanes = slice(start, start + LANES)
            accum, transmit = nothing()
            for s in range(parts.shape[0]):
                part = [
                    parts[s, c * BLOCK + half : c * BLOCK + half + HALF, lanes] for c in range(4)
                ]
                accum = [a + transmit * p for a, p in zip(accum, part[:3])]
                transmit = transmit - transmit * (part[3] * opacity_top)
            whole = [a * (colour_top * opacity_top) for a in accum] + [1.0 - transmit]
            for c in range(4):
                at = start // LANES, slice(c * BLOCK + half, c * BLOCK + half + HALF)
                image[at] = whole[c]
    for r in range(BLOCK):
        for start in range(0, cols, LANES):
            out[:, r * cols + start : r * cols + start + LANES] = image[
                start // LANES, pl.ds(r, 4, stride=BLOCK)
            ]


def shards(volume, transfer_table):
    slices, rows, cols = volume.shape
    depth_count = lax.axis_size("depth")
    img_count = lax.axis_size("img")
    chips = depth_count // 2
    depth_total = slices * depth_count
    blocks = rows // (2 * BLOCK)
    core = lax.axis_index("depth") % 2

    def shift(x, img_step, depth_step):
        pairs = []
        for i in range(img_count):
            for d in range(depth_count):
                to_i, to_d = i + img_step(d % 2), d + depth_step(d % 2)
                if 0 <= to_i < img_count and 0 <= to_d < depth_count:
                    pairs.append((i * depth_count + d, to_i * depth_count + to_d))
        return lax.ppermute(x, ("img", "depth"), pairs)

    split = (slices, blocks, 2, BLOCK, cols)
    own_view = volume.reshape(split)

    def outer_plane(parity):
        at = ((slices - 1) * core, 0, parity, 0, 0)
        return lax.dynamic_slice(own_view, at, (1, blocks, 1, BLOCK, cols)).reshape(
            blocks, BLOCK, cols
        )

    def edge_rows(at_end):
        return lax.dynamic_slice(volume, (0, (rows - HALF) * at_end, 0), (slices, HALF, cols))

    edge_own = shift(edge_rows(1 - core), lambda c: -1 if c else 1, lambda c: 0)
    edge_other = shift(edge_rows(core), lambda c: 1 if c else -1, lambda c: -1 if c else 1)
    outer_other = shift(outer_plane(core), lambda c: 0, lambda c: 2 if c else -2)
    outer_own = shift(outer_plane(1 - core), lambda c: 0, lambda c: 1 if c else -1)
    held = lax.optimization_barrier((volume, edge_own, edge_other, outer_other, outer_own))[0]
    other = lax.ppermute(held, "depth", [(d, d ^ 1) for d in range(depth_count)])

    other_view = other.reshape(split)
    core_arg = core.astype(jnp.int32).reshape(1)
    same_core = [[2 * j + c for j in range(chips)] for c in range(2)]
    vmem = pl.BlockSpec(memory_space=pltpu.MemorySpace.VMEM)
    smem = pl.BlockSpec(memory_space=pltpu.MemorySpace.SMEM)
    half = rows // 2
    shares = dict(slab_share=2.0 * slices / depth_total, depth_total=depth_total)
    params = pltpu.CompilerParams(vmem_limit_bytes=16 << 20)
    quad = jax.ShapeDtypeStruct((4, half, cols), F32)
    slab_terms = jax.ShapeDtypeStruct((slices, half, cols), F32)
    own_terms = pl.pallas_call(
        functools.partial(own_kernel, **shares),
        out_shape=(
            quad, quad, quad, slab_terms, slab_terms,
            jax.ShapeDtypeStruct((half, rows), BF16),
            jax.ShapeDtypeStruct((cols, cols), BF16),
        ),
        in_specs=[smem] + [vmem] * 3,
        out_specs=(vmem,) * 7,
        compiler_params=params,
        name="own",
    )(core_arg, own_view, edge_own, transfer_table)
    partial_image = pl.pallas_call(
        functools.partial(slab_kernel, **shares),
        out_shape=jax.ShapeDtypeStruct((blocks, 4 * BLOCK, cols), F32),
        in_specs=[smem] + [vmem] * 13,
        out_specs=vmem,
        scratch_shapes=[pltpu.VMEM((slices, half, cols), F32)] * 2,
        compiler_params=params,
        name="slab",
    )(
        core_arg, own_view, other_view, outer_own, outer_other, edge_other, transfer_table,
        *own_terms,
    )
    pieces = lax.all_to_all(
        partial_image.astype(jnp.float16), "depth", split_axis=0, concat_axis=0, tiled=True,
        axis_index_groups=same_core,
    )
    return pl.pallas_call(
        functools.partial(merge_kernel, slab_share=shares["slab_share"]),
        out_shape=jax.ShapeDtypeStruct((4, BLOCK * cols), F32),
        in_specs=[vmem, vmem],
        out_specs=vmem,
        scratch_shapes=[pltpu.VMEM((cols // LANES, 4 * BLOCK, LANES), F32)],
        compiler_params=params,
        name="merge",
    )(pieces.astype(F32), transfer_table)


def solution(mesh):
    placed = (P("depth", "img", None), P())
    return jax.shard_map(
        shards, mesh=mesh, in_specs=placed, out_specs=P(None, ("img", "depth")), check_vma=False
    )
```

```python
import functools

import jax
import jax.numpy as jnp
import numpy as np
from jax import lax
from jax.experimental import pallas as pl
from jax.experimental.pallas import tpu as pltpu
from jax.sharding import PartitionSpec as P

F32 = jnp.float32
BF16 = jnp.bfloat16
BLOCK = 16
HALF = 8
LANES = 128
TINY = 1e-30
SLOPE = 1.4 / 3.0


def row_differences(rows, core):
    shape = (rows // 2, rows)
    local = lax.broadcasted_iota(jnp.int32, shape, 0)
    there = lax.broadcasted_iota(jnp.int32, shape, 1)
    step = there - (local + (local & -BLOCK) + core * BLOCK)
    return jnp.where(step == 1, 1.0, jnp.where(step == -1, -1.0, 0.0)).astype(BF16)


def column_differences(cols):
    step = lax.broadcasted_iota(jnp.int32, (cols, cols), 0) - lax.broadcasted_iota(
        jnp.int32, (cols, cols), 1
    )
    return jnp.where(step == 1, 1.0, jnp.where(step == -1, -1.0, 0.0)).astype(BF16)


def tops(table, slab_share):
    colour = jnp.max(jnp.max(table[0:3], axis=0, keepdims=True), axis=1, keepdims=True)
    extinction = jnp.max(table[3:4], axis=1, keepdims=True)
    return jnp.maximum(colour, TINY), jnp.maximum(extinction * slab_share, TINY)


def spread(table, slab_share, depth_total):
    entries = table.shape[1]
    colour_top, opacity_top = tops(table, slab_share)
    scale = SLOPE / (colour_top * opacity_top)
    lower = [table[c : c + 1] * scale for c in range(3)]
    lower.append(table[3:4] * float(-np.log2(np.e) / depth_total))
    lower = [jnp.broadcast_to(t, (HALF, entries)) for t in lower]
    last = lax.broadcasted_iota(jnp.int32, (HALF, entries), 1) == entries - 1
    upper = [jnp.where(last, t, pltpu.roll(t, entries - 1, 1)) for t in lower]
    return lower + upper


def look_up(table, index):
    return jnp.take_along_axis(table, index, axis=1, mode="promise_in_bounds")


def classify(centre, tabs):
    position = centre * float(tabs[0].shape[1] - 1)
    knot = position.astype(jnp.int32)
    part = position - knot.astype(F32)
    upper = part.astype(BF16).astype(F32)
    lower = (1.0 - part).astype(BF16).astype(F32)
    values = [
        lower * look_up(tabs[c], knot) + upper * look_up(tabs[c + 4], knot) for c in range(4)
    ]
    return values[:3] + [jnp.exp2(values[3])]


def shade(accum, transmit, dz, slope_xy, norm_xy, found):
    shading = 0.3 / SLOPE + jnp.abs(dz + slope_xy) * lax.rsqrt(dz * dz + norm_xy)
    left = transmit * found[3]
    gain = (transmit - left) * shading
    return [a + gain * v for a, v in zip(accum, found[:3])], left


def slope_of(dx, dy):
    return 0.5 * dx + dy


def norm_of(dx, dy):
    return dx * dx + dy * dy + 0.04


def over(near, far):
    return [n + near[3] * f for n, f in zip(near[:3], far[:3])] + [near[3] * far[3]]


def nothing():
    return [jnp.zeros((HALF, LANES), F32)] * 3, jnp.ones((HALF, LANES), F32)


def pick(condition, a, b):
    return [jnp.where(condition, x, y) for x, y in zip(a, b)]


def slices_kernel(cells, core, rows_op, cols_op, table, outs, inner_slope, inner_norm, shares):
    first, last, middle, slope, norm, edge_dx, edge_dy = outs
    slices, blocks, _, _, cols = cells.shape
    rows = blocks * BLOCK
    ends = (0, slices - 1)
    for z in range(slices):
        dx = jnp.dot(rows_op[...], cells[z].reshape(2 * rows, cols), preferred_element_type=F32)
        dy = jnp.dot(
            cells[z, :, core].reshape(rows, cols), cols_op[...], preferred_element_type=F32
        )
        to_slope, to_norm, at = (
            (slope, norm, ends.index(z)) if z in ends else (inner_slope, inner_norm, z - 1)
        )
        to_slope[at] = slope_of(dx, dy)
        to_norm[at] = norm_of(dx, dy)
        edge_dx[z] = jnp.where(core == 0, dx[:HALF], dx[rows - HALF :])
        edge_dy[z] = jnp.where(core == 0, dy[:HALF], dy[rows - HALF :])
    tabs = spread(table[...].astype(F32), **shares)

    def block(b, carry):
        for half in range(0, BLOCK, HALF):
            here = pl.ds(pl.multiple_of(b * BLOCK + half, HALF), HALF)
            rows = slice(half, half + HALF)
            for start in range(0, cols, LANES):
                lanes = slice(start, start + LANES)
                mine = [cells[z, b, core, rows, lanes].astype(F32) for z in range(slices)]
                accum, transmit = nothing()
                for z in range(slices):
                    found = classify(mine[z], tabs)
                    if z in ends:
                        ref = last if z else first
                        for c in range(4):
                            ref[c, here, lanes] = found[c]
                    else:
                        accum, transmit = shade(
                            accum, transmit, mine[z + 1] - mine[z - 1],
                            inner_slope[z - 1, here, lanes], inner_norm[z - 1, here, lanes], found,
                        )
                for c in range(3):
                    middle[c, here, lanes] = accum[c]
                middle[3, here, lanes] = transmit
        return carry

    lax.fori_loop(0, blocks, block, 0)


def own_kernel(core_ref, cells, table, *refs, shares):
    outs, rest = refs[:7], refs[7:]
    rows_op, cols_op, to_other, to_same, edge_same, edge_cross, inner_slope, inner_norm = rest
    slices, blocks, _, _, cols = cells.shape
    core = core_ref[0]
    outer = (slices - 1) * core
    to_other[...] = cells[outer, :, 1 - core]
    to_same[...] = cells[outer, :, core]

    @pl.when(core == 0)
    def _():
        edge_same[...] = cells[:, blocks - 1, 1, HALF:, :]
        edge_cross[...] = cells[:, 0, 0, :HALF, :]

    @pl.when(core != 0)
    def _():
        edge_same[...] = cells[:, 0, 0, :HALF, :]
        edge_cross[...] = cells[:, blocks - 1, 1, HALF:, :]

    rows_op[...] = row_differences(2 * blocks * BLOCK, core)
    cols_op[...] = column_differences(cols)
    slices_kernel(
        cells, core, rows_op, cols_op, table, outs, inner_slope, inner_norm, shares
    )


def other_kernel(core_ref, cells, table, rows_op, cols_op, *refs, shares):
    slices_kernel(
        cells, core_ref[0], rows_op, cols_op, table, refs[:7], refs[7], refs[8], shares
    )


def slab_kernel(
    core_ref, own, other, outer_own, outer_other, edge_own, edge_other, table, *refs, shares
):
    own_terms, other_terms, out = refs[:7], refs[7:14], refs[14]
    slices, blocks, _, _, cols = own.shape
    core = core_ref[0]
    front = core == 0
    end = slices - 1
    table_values = table[...].astype(F32)
    opacity_scale = 1.0 / tops(table_values, shares["slab_share"])[1]

    def stacks(mine, theirs, end_own, end_other):
        own_stack = (
            [jnp.where(front, end_own, theirs[end])] + mine + [jnp.where(front, theirs[0], end_own)]
        )
        other_stack = (
            [jnp.where(front, mine[end], end_other)]
            + theirs
            + [jnp.where(front, end_other, mine[0])]
        )
        return own_stack, other_stack

    def finish(own_part, other_part):
        both = over(pick(front, own_part, other_part), pick(front, other_part, own_part))
        both[3] = (1.0 - both[3]) * opacity_scale
        return both

    def block(b, carry):
        for half in range(0, BLOCK, HALF):
            here = pl.ds(pl.multiple_of(b * BLOCK + half, HALF), HALF)
            rows = slice(half, half + HALF)
            for start in range(0, cols, LANES):
                lanes = slice(start, start + LANES)

                def half_slab(stack, terms):
                    first, last, middle, slope, norm = terms[:5]
                    parts = []
                    for ref, at, z in ((first, 0, 0), (last, 1, end)):
                        accum, transmit = shade(
                            *nothing(), stack[z + 2] - stack[z],
                            slope[at, here, lanes], norm[at, here, lanes],
                            [ref[c, here, lanes] for c in range(4)],
                        )
                        parts.append(accum + [transmit])
                    inner = [middle[c, here, lanes] for c in range(4)]
                    return over(parts[0], over(inner, parts[1]))

                own_stack, other_stack = stacks(
                    [own[z, b, core, rows, lanes].astype(F32) for z in range(slices)],
                    [other[z, b, core, rows, lanes].astype(F32) for z in range(slices)],
                    outer_own[b, rows, lanes].astype(F32),
                    outer_other[b, rows, lanes].astype(F32),
                )
                both = finish(half_slab(own_stack, own_terms), half_slab(other_stack, other_terms))
                for c in range(4):
                    at = c * BLOCK + half
                    out[b, at : at + HALF, lanes] = both[c]
        return carry

    lax.fori_loop(0, blocks, block, 0)

    tabs = spread(table_values, **shares)
    b = jnp.where(front, 0, blocks - 1)
    row = lax.broadcasted_iota(jnp.int32, (HALF, LANES), 0)
    at_edge = row == jnp.where(front, 0, HALF - 1)
    for start in range(0, cols, LANES):
        lanes = slice(start, start + LANES)

        def load(ref, *index):
            top = ref[(*index, slice(0, HALF), lanes)].astype(F32)
            return jnp.where(front, top, ref[(*index, slice(HALF, BLOCK), lanes)].astype(F32))

        def half_slab(stack, terms, edge):
            accum, transmit = nothing()
            for z in range(slices):
                halo = edge[z, :, lanes].astype(F32)
                halo = jnp.where(front, -halo[HALF - 1 : HALF], halo[0:1])
                dx = terms[5][z, :, lanes] + jnp.where(at_edge, halo, 0.0)
                dy = terms[6][z, :, lanes]
                accum, transmit = shade(
                    accum, transmit, stack[z + 2] - stack[z],
                    slope_of(dx, dy), norm_of(dx, dy), classify(stack[z + 1], tabs),
                )
            return accum + [transmit]

        own_stack, other_stack = stacks(
            [load(own, z, b, core) for z in range(slices)],
            [load(other, z, b, core) for z in range(slices)],
            load(outer_own, b),
            load(outer_other, b),
        )
        both = finish(
            half_slab(own_stack, own_terms, edge_own), half_slab(other_stack, other_terms, edge_other)
        )
        for c in range(4):
            at = pl.multiple_of(c * BLOCK + core * HALF, HALF)
            out[b, pl.ds(at, HALF), lanes] = both[c]


def merge_kernel(parts, table, out, image, *, slab_share):
    cols = parts.shape[2]
    colour_top, opacity_top = tops(table[...].astype(F32), slab_share)
    for half in range(0, BLOCK, HALF):
        for start in range(0, cols, LANES):
            lanes = slice(start, start + LANES)
            accum, transmit = nothing()
            for s in range(parts.shape[0]):
                part = [
                    parts[s, c * BLOCK + half : c * BLOCK + half + HALF, lanes] for c in range(4)
                ]
                accum = [a + transmit * p for a, p in zip(accum, part[:3])]
                transmit = transmit - transmit * (part[3] * opacity_top)
            whole = [a * (colour_top * opacity_top) for a in accum] + [1.0 - transmit]
            for c in range(4):
                at = start // LANES, slice(c * BLOCK + half, c * BLOCK + half + HALF)
                image[at] = whole[c]
    for r in range(BLOCK):
        for start in range(0, cols, LANES):
            out[:, r * cols + start : r * cols + start + LANES] = image[
                start // LANES, pl.ds(r, 4, stride=BLOCK)
            ]


def shards(volume, transfer_table):
    slices, rows, cols = volume.shape
    depth_count = lax.axis_size("depth")
    img_count = lax.axis_size("img")
    chips = depth_count // 2
    depth_total = slices * depth_count
    blocks = rows // (2 * BLOCK)
    core = lax.axis_index("depth") % 2

    def shift(x, img_step, depth_step):
        pairs = []
        for i in range(img_count):
            for d in range(depth_count):
                to_i, to_d = i + img_step(d % 2), d + depth_step(d % 2)
                if 0 <= to_i < img_count and 0 <= to_d < depth_count:
                    pairs.append((i * depth_count + d, to_i * depth_count + to_d))
        return lax.ppermute(x, ("img", "depth"), pairs)

    half = rows // 2
    split = (slices, blocks, 2, BLOCK, cols)
    core_arg = core.astype(jnp.int32).reshape(1)
    same_core = [[2 * j + c for j in range(chips)] for c in range(2)]
    vmem = pl.BlockSpec(memory_space=pltpu.MemorySpace.VMEM)
    smem = pl.BlockSpec(memory_space=pltpu.MemorySpace.SMEM)
    shares = dict(slab_share=2.0 * slices / depth_total, depth_total=depth_total)
    params = pltpu.CompilerParams(vmem_limit_bytes=16 << 20)
    quad = jax.ShapeDtypeStruct((4, half, cols), F32)
    two = jax.ShapeDtypeStruct((2, half, cols), F32)
    unit = jax.ShapeDtypeStruct((slices, HALF, cols), F32)
    plane = jax.ShapeDtypeStruct((blocks, BLOCK, cols), BF16)
    edge = jax.ShapeDtypeStruct((slices, HALF, cols), BF16)
    terms = (quad, quad, quad, two, two, unit, unit)
    operators = (
        jax.ShapeDtypeStruct((half, rows), BF16), jax.ShapeDtypeStruct((cols, cols), BF16)
    )
    inner = [pltpu.VMEM((slices - 2, half, cols), F32)] * 2

    other = lax.ppermute(volume, "depth", [(d, d ^ 1) for d in range(depth_count)]).reshape(split)
    own = volume.reshape(split)
    results = pl.pallas_call(
        functools.partial(own_kernel, shares=shares),
        out_shape=(*terms, *operators, plane, plane, edge, edge),
        in_specs=[smem, vmem, vmem],
        out_specs=(vmem,) * 13,
        scratch_shapes=inner,
        compiler_params=params,
        name="own",
    )(core_arg, own, transfer_table)
    own_terms, ops, (to_other, to_same, edge_same, edge_cross) = (
        results[:7], results[7:9], results[9:]
    )
    outer_other = shift(to_same, lambda c: 0, lambda c: 2 if c else -2)
    outer_own = shift(to_other, lambda c: 0, lambda c: 1 if c else -1)
    edge_own = shift(edge_same, lambda c: -1 if c else 1, lambda c: 0)
    edge_other = shift(edge_cross, lambda c: 1 if c else -1, lambda c: -1 if c else 1)
    other_terms = pl.pallas_call(
        functools.partial(other_kernel, shares=shares),
        out_shape=terms,
        in_specs=[smem] + [vmem] * 4,
        out_specs=(vmem,) * 7,
        scratch_shapes=inner,
        compiler_params=params,
        name="other",
    )(core_arg, other, transfer_table, *ops)
    partial_image = pl.pallas_call(
        functools.partial(slab_kernel, shares=shares),
        out_shape=jax.ShapeDtypeStruct((blocks, 4 * BLOCK, cols), F32),
        in_specs=[smem] + [vmem] * 21,
        out_specs=vmem,
        compiler_params=params,
        name="slab",
    )(
        core_arg, own, other, outer_own, outer_other, edge_own, edge_other, transfer_table,
        *own_terms, *other_terms,
    )
    pieces = lax.all_to_all(
        partial_image.astype(jnp.float16), "depth", split_axis=0, concat_axis=0, tiled=True,
        axis_index_groups=same_core,
    )
    return pl.pallas_call(
        functools.partial(merge_kernel, slab_share=shares["slab_share"]),
        out_shape=jax.ShapeDtypeStruct((4, BLOCK * cols), F32),
        in_specs=[vmem, vmem],
        out_specs=vmem,
        scratch_shapes=[pltpu.VMEM((cols // LANES, 4 * BLOCK, LANES), F32)],
        compiler_params=params,
        name="merge",
    )(pieces.astype(F32), transfer_table)


def solution(mesh):
    placed = (P("depth", "img", None), P())
    return jax.shard_map(
        shards, mesh=mesh, in_specs=placed, out_specs=P(None, ("img", "depth")), check_vma=False
    )
```

```python
import functools

import jax
import jax.numpy as jnp
import numpy as np
from jax import lax
from jax.experimental import pallas as pl
from jax.experimental.pallas import tpu as pltpu
from jax.sharding import PartitionSpec as P

F32 = jnp.float32
BF16 = jnp.bfloat16
BLOCK = 16
HALF = 8
LANES = 128
TINY = 1e-30
SLOPE = 1.4 / 3.0


def row_differences(rows, core):
    shape = (rows // 2, rows)
    local = lax.broadcasted_iota(jnp.int32, shape, 0)
    there = lax.broadcasted_iota(jnp.int32, shape, 1)
    step = there - (local + (local & -BLOCK) + core * BLOCK)
    return jnp.where(step == 1, 1.0, jnp.where(step == -1, -1.0, 0.0)).astype(BF16)


def column_differences(cols):
    step = lax.broadcasted_iota(jnp.int32, (cols, cols), 0) - lax.broadcasted_iota(
        jnp.int32, (cols, cols), 1
    )
    return jnp.where(step == 1, 1.0, jnp.where(step == -1, -1.0, 0.0)).astype(BF16)


def tops(table, slab_share):
    colour = jnp.max(jnp.max(table[0:3], axis=0, keepdims=True), axis=1, keepdims=True)
    extinction = jnp.max(table[3:4], axis=1, keepdims=True)
    return jnp.maximum(colour, TINY), jnp.maximum(extinction * slab_share, TINY)


def prepare_kernel(core_ref, table_ref, rows_op, cols_op, tables, scales, *, slab_share, depth_total):
    table = table_ref[...].astype(F32)
    entries = table.shape[1]
    rows_op[...] = row_differences(rows_op.shape[1], core_ref[0])
    cols_op[...] = column_differences(cols_op.shape[1])
    colour_top, opacity_top = tops(table, slab_share)
    scale = SLOPE / (colour_top * opacity_top)
    last = lax.broadcasted_iota(jnp.int32, (HALF, entries), 1) == entries - 1
    for c in range(4):
        factor = scale if c < 3 else float(-np.log2(np.e) / depth_total)
        lower = jnp.broadcast_to(table[c : c + 1] * factor, (HALF, entries))
        tables[c] = lower
        tables[c + 4] = jnp.where(last, lower, pltpu.roll(lower, entries - 1, 1))
    for at, value in enumerate((colour_top * opacity_top, opacity_top, 1.0 / opacity_top)):
        scales[at] = jnp.broadcast_to(value, (HALF, LANES))


def look_up(table, index):
    return jnp.take_along_axis(table, index, axis=1, mode="promise_in_bounds")


def classify(centre, tabs):
    position = centre * float(tabs[0].shape[1] - 1)
    knot = position.astype(jnp.int32)
    part = position - knot.astype(F32)
    upper = part.astype(BF16).astype(F32)
    lower = (1.0 - part).astype(BF16).astype(F32)
    values = [
        lower * look_up(tabs[c], knot) + upper * look_up(tabs[c + 4], knot) for c in range(4)
    ]
    return values[:3] + [jnp.exp2(values[3])]


def shade(accum, transmit, dz, slope_xy, norm_xy, found):
    shading = 0.3 / SLOPE + jnp.abs(dz + slope_xy) * lax.rsqrt(dz * dz + norm_xy)
    left = transmit * found[3]
    gain = (transmit - left) * shading
    return [a + gain * v for a, v in zip(accum, found[:3])], left


def slope_of(dx, dy):
    return 0.5 * dx + dy


def norm_of(dx, dy):
    return dx * dx + dy * dy + 0.04


def over(near, far):
    return [n + near[3] * f for n, f in zip(near[:3], far[:3])] + [near[3] * far[3]]


def nothing():
    return [jnp.zeros((HALF, LANES), F32)] * 3, jnp.ones((HALF, LANES), F32)


def pick(condition, a, b):
    return [jnp.where(condition, x, y) for x, y in zip(a, b)]


def pair_terms(cells, end, core, rows_op, cols_op, tables, outs, inner_slope, inner_norm):
    kept, inner, slope, norm, edge_dx, edge_dy = outs
    slices, blocks, _, _, cols = cells.shape
    rows = blocks * BLOCK
    near = 1 if end == 0 else end - 1
    for at, z, to_slope, to_norm in (
        (0, end, slope, norm), (1, near, inner_slope, inner_norm)
    ):
        dx = jnp.dot(rows_op[...], cells[z].reshape(2 * rows, cols), preferred_element_type=F32)
        dy = jnp.dot(
            cells[z, :, core].reshape(rows, cols), cols_op[...], preferred_element_type=F32
        )
        to_slope[...] = slope_of(dx, dy)
        to_norm[...] = norm_of(dx, dy)
        edge_dx[at] = jnp.where(core == 0, dx[:HALF], dx[rows - HALF :])
        edge_dy[at] = jnp.where(core == 0, dy[:HALF], dy[rows - HALF :])
    tabs = [tables[c] for c in range(8)]

    def block(b, carry):
        for half in range(0, BLOCK, HALF):
            here = pl.ds(pl.multiple_of(b * BLOCK + half, HALF), HALF)
            rows = slice(half, half + HALF)
            for start in range(0, cols, LANES):
                lanes = slice(start, start + LANES)
                before, after = (
                    cells[z, b, core, rows, lanes].astype(F32) for z in (near - 1, near + 1)
                )
                found = classify(before if end == near - 1 else after, tabs)
                for c in range(4):
                    kept[c, here, lanes] = found[c]
                accum, transmit = shade(
                    *nothing(), after - before, inner_slope[here, lanes], inner_norm[here, lanes],
                    classify(cells[near, b, core, rows, lanes].astype(F32), tabs),
                )
                for c in range(3):
                    inner[c, here, lanes] = accum[c]
                inner[3, here, lanes] = transmit
        return carry

    lax.fori_loop(0, blocks, block, 0)


def opening_kernel(core_ref, cells, rows_op, cols_op, tables, *refs):
    outs, (to_other, to_same, edge_same, edge_cross), inner = refs[:6], refs[6:10], refs[10:]
    slices, blocks, _, _, cols = cells.shape
    core = core_ref[0]
    outer = (slices - 1) * core
    to_other[...] = cells[outer, :, 1 - core]
    to_same[...] = cells[outer, :, core]

    @pl.when(core == 0)
    def _():
        edge_same[...] = cells[:, blocks - 1, 1, HALF:, :]
        edge_cross[...] = cells[:, 0, 0, :HALF, :]

    @pl.when(core != 0)
    def _():
        edge_same[...] = cells[:, 0, 0, :HALF, :]
        edge_cross[...] = cells[:, blocks - 1, 1, HALF:, :]

    pair_terms(cells, 0, core, rows_op, cols_op, tables, outs, *inner)


def pair_kernel(core_ref, cells, rows_op, cols_op, tables, _, *refs, end):
    pair_terms(cells, end, core_ref[0], rows_op, cols_op, tables, refs[:6], *refs[6:])


def slab_kernel(
    core_ref, own, other, outer_own, outer_other, edge_own, edge_other, tables, scales, *refs
):
    own_terms, other_terms, out = (refs[0:6], refs[6:12]), (refs[12:18], refs[18:24]), refs[24]
    slices, blocks, _, _, cols = own.shape
    core = core_ref[0]
    front = core == 0
    end = slices - 1
    opacity_scale = scales[2]

    def stacks(mine, theirs, end_own, end_other):
        own_stack = (
            [jnp.where(front, end_own, theirs[end])] + mine + [jnp.where(front, theirs[0], end_own)]
        )
        other_stack = (
            [jnp.where(front, mine[end], end_other)]
            + theirs
            + [jnp.where(front, end_other, mine[0])]
        )
        return own_stack, other_stack

    def finish(own_part, other_part):
        both = over(pick(front, own_part, other_part), pick(front, other_part, own_part))
        both[3] = (1.0 - both[3]) * opacity_scale
        return both

    def block(b, carry):
        for half in range(0, BLOCK, HALF):
            here = pl.ds(pl.multiple_of(b * BLOCK + half, HALF), HALF)
            rows = slice(half, half + HALF)
            for start in range(0, cols, LANES):
                lanes = slice(start, start + LANES)

                def half_slab(stack, terms):
                    ends, inners = [], []
                    for (kept, inner, slope, norm, _, _), z in zip(terms, (0, end)):
                        accum, transmit = shade(
                            *nothing(), stack[z + 2] - stack[z],
                            slope[here, lanes], norm[here, lanes],
                            [kept[c, here, lanes] for c in range(4)],
                        )
                        ends.append(accum + [transmit])
                        inners.append([inner[c, here, lanes] for c in range(4)])
                    return over(over(ends[0], inners[0]), over(inners[1], ends[1]))

                own_stack, other_stack = stacks(
                    [own[z, b, core, rows, lanes].astype(F32) for z in range(slices)],
                    [other[z, b, core, rows, lanes].astype(F32) for z in range(slices)],
                    outer_own[b, rows, lanes].astype(F32),
                    outer_other[b, rows, lanes].astype(F32),
                )
                both = finish(half_slab(own_stack, own_terms), half_slab(other_stack, other_terms))
                for c in range(4):
                    at = c * BLOCK + half
                    out[b, at : at + HALF, lanes] = both[c]
        return carry

    lax.fori_loop(0, blocks, block, 0)

    tabs = [tables[c] for c in range(8)]
    b = jnp.where(front, 0, blocks - 1)
    row = lax.broadcasted_iota(jnp.int32, (HALF, LANES), 0)
    at_edge = row == jnp.where(front, 0, HALF - 1)
    for start in range(0, cols, LANES):
        lanes = slice(start, start + LANES)

        def load(ref, *index):
            top = ref[(*index, slice(0, HALF), lanes)].astype(F32)
            return jnp.where(front, top, ref[(*index, slice(HALF, BLOCK), lanes)].astype(F32))

        def half_slab(stack, terms, edge):
            accum, transmit = nothing()
            for z in range(slices):
                halo = edge[z, :, lanes].astype(F32)
                halo = jnp.where(front, -halo[HALF - 1 : HALF], halo[0:1])
                _, _, _, _, edge_dx, edge_dy = terms[z // 2]
                at = 0 if z in (0, end) else 1
                dx = edge_dx[at, :, lanes] + jnp.where(at_edge, halo, 0.0)
                dy = edge_dy[at, :, lanes]
                accum, transmit = shade(
                    accum, transmit, stack[z + 2] - stack[z],
                    slope_of(dx, dy), norm_of(dx, dy), classify(stack[z + 1], tabs),
                )
            return accum + [transmit]

        own_stack, other_stack = stacks(
            [load(own, z, b, core) for z in range(slices)],
            [load(other, z, b, core) for z in range(slices)],
            load(outer_own, b),
            load(outer_other, b),
        )
        both = finish(
            half_slab(own_stack, own_terms, edge_own), half_slab(other_stack, other_terms, edge_other)
        )
        for c in range(4):
            at = pl.multiple_of(c * BLOCK + core * HALF, HALF)
            out[b, pl.ds(at, HALF), lanes] = both[c]


def merge_kernel(parts, scales, out, image):
    cols = parts.shape[2]
    colour_scale, opacity_top = scales[0], scales[1]
    for half in range(0, BLOCK, HALF):
        for start in range(0, cols, LANES):
            lanes = slice(start, start + LANES)
            accum, transmit = nothing()
            for s in range(parts.shape[0]):
                part = [
                    parts[s, c * BLOCK + half : c * BLOCK + half + HALF, lanes] for c in range(4)
                ]
                accum = [a + transmit * p for a, p in zip(accum, part[:3])]
                transmit = transmit - transmit * (part[3] * opacity_top)
            whole = [a * colour_scale for a in accum] + [1.0 - transmit]
            for c in range(4):
                at = start // LANES, slice(c * BLOCK + half, c * BLOCK + half + HALF)
                image[at] = whole[c]
    for r in range(BLOCK):
        for start in range(0, cols, LANES):
            out[:, r * cols + start : r * cols + start + LANES] = image[
                start // LANES, pl.ds(r, 4, stride=BLOCK)
            ]


def shards(volume, transfer_table):
    slices, rows, cols = volume.shape
    depth_count = lax.axis_size("depth")
    img_count = lax.axis_size("img")
    chips = depth_count // 2
    depth_total = slices * depth_count
    blocks = rows // (2 * BLOCK)
    core = lax.axis_index("depth") % 2

    def shift(x, img_step, depth_step):
        pairs = []
        for i in range(img_count):
            for d in range(depth_count):
                to_i, to_d = i + img_step(d % 2), d + depth_step(d % 2)
                if 0 <= to_i < img_count and 0 <= to_d < depth_count:
                    pairs.append((i * depth_count + d, to_i * depth_count + to_d))
        return lax.ppermute(x, ("img", "depth"), pairs)

    half = rows // 2
    split = (slices, blocks, 2, BLOCK, cols)
    core_arg = core.astype(jnp.int32).reshape(1)
    same_core = [[2 * j + c for j in range(chips)] for c in range(2)]
    vmem = pl.BlockSpec(memory_space=pltpu.MemorySpace.VMEM)
    smem = pl.BlockSpec(memory_space=pltpu.MemorySpace.SMEM)
    params = pltpu.CompilerParams(vmem_limit_bytes=16 << 20)
    quad = jax.ShapeDtypeStruct((4, half, cols), F32)
    flat = jax.ShapeDtypeStruct((half, cols), F32)
    unit = jax.ShapeDtypeStruct((2, HALF, cols), F32)
    plane = jax.ShapeDtypeStruct((blocks, BLOCK, cols), BF16)
    edge = jax.ShapeDtypeStruct((slices, HALF, cols), BF16)
    terms = (quad, quad, flat, flat, unit, unit)
    inner = [pltpu.VMEM((half, cols), F32)] * 2

    other = lax.ppermute(volume, "depth", [(d, d ^ 1) for d in range(depth_count)]).reshape(split)
    own = volume.reshape(split)
    entries = transfer_table.shape[1]
    *ops, scales = pl.pallas_call(
        functools.partial(
            prepare_kernel, slab_share=2.0 * slices / depth_total, depth_total=depth_total
        ),
        out_shape=(
            jax.ShapeDtypeStruct((half, rows), BF16),
            jax.ShapeDtypeStruct((cols, cols), BF16),
            jax.ShapeDtypeStruct((8, HALF, entries), F32),
            jax.ShapeDtypeStruct((3, HALF, LANES), F32),
        ),
        in_specs=[smem, vmem],
        out_specs=(vmem,) * 4,
        compiler_params=params,
        name="prepare",
    )(core_arg, transfer_table)
    results = pl.pallas_call(
        opening_kernel,
        out_shape=(*terms, plane, plane, edge, edge),
        in_specs=[smem] + [vmem] * 4,
        out_specs=(vmem,) * 10,
        scratch_shapes=inner,
        compiler_params=params,
        name="opening",
    )(core_arg, own, *ops)
    to_other, to_same, edge_same, edge_cross = results[6:]

    def slice_pair(cells, end, previous, name):
        return pl.pallas_call(
            functools.partial(pair_kernel, end=end),
            out_shape=terms,
            in_specs=[smem] + [vmem] * 5,
            out_specs=(vmem,) * 6,
            scratch_shapes=inner,
            compiler_params=params,
            name=name,
        )(core_arg, cells, *ops, previous[5])

    own_terms = [results[:6]]
    outer_own = shift(to_other, lambda c: 0, lambda c: 1 if c else -1)
    own_terms.append(slice_pair(own, slices - 1, own_terms[0], "own_far"))
    to_same, _ = lax.optimization_barrier((to_same, own_terms[1][5]))
    outer_other = shift(to_same, lambda c: 0, lambda c: 2 if c else -2)
    other_terms = [slice_pair(other, 0, own_terms[1], "other_near")]
    edge_same, edge_cross, _ = lax.optimization_barrier((edge_same, edge_cross, other_terms[0][5]))
    edge_own = shift(edge_same, lambda c: -1 if c else 1, lambda c: 0)
    edge_other = shift(edge_cross, lambda c: 1 if c else -1, lambda c: -1 if c else 1)
    other_terms.append(slice_pair(other, slices - 1, other_terms[0], "other_far"))
    partial_image = pl.pallas_call(
        slab_kernel,
        out_shape=jax.ShapeDtypeStruct((blocks, 4 * BLOCK, cols), F32),
        in_specs=[smem] + [vmem] * 32,
        out_specs=vmem,
        compiler_params=params,
        name="slab",
    )(
        core_arg, own, other, outer_own, outer_other, edge_own, edge_other, ops[2], scales,
        *own_terms[0], *own_terms[1], *other_terms[0], *other_terms[1],
    )
    pieces = lax.all_to_all(
        partial_image.astype(jnp.float16), "depth", split_axis=0, concat_axis=0, tiled=True,
        axis_index_groups=same_core,
    )
    return pl.pallas_call(
        merge_kernel,
        out_shape=jax.ShapeDtypeStruct((4, BLOCK * cols), F32),
        in_specs=[vmem, vmem],
        out_specs=vmem,
        scratch_shapes=[pltpu.VMEM((cols // LANES, 4 * BLOCK, LANES), F32)],
        compiler_params=params,
        name="merge",
    )(pieces.astype(F32), scales)


def solution(mesh):
    placed = (P("depth", "img", None), P())
    return jax.shard_map(
        shards, mesh=mesh, in_specs=placed, out_specs=P(None, ("img", "depth")), check_vma=False
    )
```

```python
import functools

import jax
import jax.numpy as jnp
import numpy as np
from jax import lax
from jax.experimental import pallas as pl
from jax.experimental.pallas import tpu as pltpu
from jax.sharding import PartitionSpec as P

F32 = jnp.float32
BF16 = jnp.bfloat16
BLOCK = 16
HALF = 8
LANES = 128
TINY = 1e-30
SLOPE = 1.4 / 3.0


def row_differences(rows, core):
    shape = (rows // 2, rows)
    local = lax.broadcasted_iota(jnp.int32, shape, 0)
    there = lax.broadcasted_iota(jnp.int32, shape, 1)
    step = there - (local + (local & -BLOCK) + core * BLOCK)
    return jnp.where(step == 1, 1.0, jnp.where(step == -1, -1.0, 0.0)).astype(BF16)


def column_differences(cols):
    step = lax.broadcasted_iota(jnp.int32, (cols, cols), 0) - lax.broadcasted_iota(
        jnp.int32, (cols, cols), 1
    )
    return jnp.where(step == 1, 1.0, jnp.where(step == -1, -1.0, 0.0)).astype(BF16)


def tops(table, slab_share):
    colour = jnp.max(jnp.max(table[0:3], axis=0, keepdims=True), axis=1, keepdims=True)
    extinction = jnp.max(table[3:4], axis=1, keepdims=True)
    return jnp.maximum(colour, TINY), jnp.maximum(extinction * slab_share, TINY)


def prepare_kernel(core_ref, table_ref, rows_op, cols_op, tables, scales, *, slab_share, depth_total):
    table = table_ref[...].astype(F32)
    entries = table.shape[1]
    rows_op[...] = row_differences(rows_op.shape[1], core_ref[0])
    cols_op[...] = column_differences(cols_op.shape[1])
    colour_top, opacity_top = tops(table, slab_share)
    scale = SLOPE / (colour_top * opacity_top)
    last = lax.broadcasted_iota(jnp.int32, (HALF, entries), 1) == entries - 1
    for c in range(4):
        factor = scale if c < 3 else float(-np.log2(np.e) / depth_total)
        lower = jnp.broadcast_to(table[c : c + 1] * factor, (HALF, entries))
        tables[c] = lower
        tables[c + 4] = jnp.where(last, lower, pltpu.roll(lower, entries - 1, 1))
    for at, value in enumerate((colour_top * opacity_top, opacity_top, 1.0 / opacity_top)):
        scales[at] = jnp.broadcast_to(value, (HALF, LANES))


def look_up(table, index):
    return jnp.take_along_axis(table, index, axis=1, mode="promise_in_bounds")


def classify(centre, tabs):
    position = centre * float(tabs[0].shape[1] - 1)
    knot = position.astype(jnp.int32)
    part = position - knot.astype(F32)
    upper = part.astype(BF16).astype(F32)
    lower = (1.0 - part).astype(BF16).astype(F32)
    values = [
        lower * look_up(tabs[c], knot) + upper * look_up(tabs[c + 4], knot) for c in range(4)
    ]
    return values[:3] + [jnp.exp2(values[3])]


def shade(accum, transmit, dz, slope_xy, norm_xy, found):
    shading = 0.3 / SLOPE + jnp.abs(dz + slope_xy) * lax.rsqrt(dz * dz + norm_xy)
    left = transmit * found[3]
    gain = (transmit - left) * shading
    return [a + gain * v for a, v in zip(accum, found[:3])], left


def slope_of(dx, dy):
    return 0.5 * dx + dy


def norm_of(dx, dy):
    return dx * dx + dy * dy + 0.04


def over(near, far):
    return [n + near[3] * f for n, f in zip(near[:3], far[:3])] + [near[3] * far[3]]


def nothing():
    return [jnp.zeros((HALF, LANES), F32)] * 3, jnp.ones((HALF, LANES), F32)


def pick(condition, a, b):
    return [jnp.where(condition, x, y) for x, y in zip(a, b)]


def slices_kernel(core_ref, cells, rows_op, cols_op, tables, *refs):
    first, last, middle, slope, norm, edge_dx, edge_dy, inner_slope, inner_norm = refs[-9:]
    core = core_ref[0]
    slices, blocks, _, _, cols = cells.shape
    rows = blocks * BLOCK
    ends = (0, slices - 1)
    for z in range(slices):
        dx = jnp.dot(rows_op[...], cells[z].reshape(2 * rows, cols), preferred_element_type=F32)
        dy = jnp.dot(
            cells[z, :, core].reshape(rows, cols), cols_op[...], preferred_element_type=F32
        )
        to_slope, to_norm, at = (
            (slope, norm, ends.index(z)) if z in ends else (inner_slope, inner_norm, z - 1)
        )
        to_slope[at] = slope_of(dx, dy)
        to_norm[at] = norm_of(dx, dy)
        edge_dx[z] = jnp.where(core == 0, dx[:HALF], dx[rows - HALF :])
        edge_dy[z] = jnp.where(core == 0, dy[:HALF], dy[rows - HALF :])
    tabs = [tables[c] for c in range(8)]

    def block(b, carry):
        for half in range(0, BLOCK, HALF):
            here = pl.ds(pl.multiple_of(b * BLOCK + half, HALF), HALF)
            rows = slice(half, half + HALF)
            for start in range(0, cols, LANES):
                lanes = slice(start, start + LANES)
                mine = [cells[z, b, core, rows, lanes].astype(F32) for z in range(slices)]
                accum, transmit = nothing()
                for z in range(slices):
                    found = classify(mine[z], tabs)
                    if z in ends:
                        ref = last if z else first
                        for c in range(4):
                            ref[c, here, lanes] = found[c]
                    else:
                        accum, transmit = shade(
                            accum, transmit, mine[z + 1] - mine[z - 1],
                            inner_slope[z - 1, here, lanes], inner_norm[z - 1, here, lanes], found,
                        )
                for c in range(3):
                    middle[c, here, lanes] = accum[c]
                middle[3, here, lanes] = transmit
        return carry

    lax.fori_loop(0, blocks, block, 0)


def relay_kernel(core_ref, outer, top, bottom, out):
    blocks = outer.shape[0]
    core = core_ref[0]
    out[:blocks] = outer[:, 1 - core]

    def edges(ref):
        for z in range(0, ref.shape[0], 2):
            at = blocks + z // 2
            out[at, :HALF, :] = ref[z]
            out[at, HALF:, :] = ref[z + 1]

    @pl.when(core == 0)
    def _():
        edges(bottom)

    @pl.when(core != 0)
    def _():
        edges(top)


def slab_kernel(
    core_ref, own, other, outer, relayed, top, bottom, tables, scales, *refs
):
    own_terms, other_terms, out = refs[:7], refs[7:14], refs[14]
    slices, blocks, _, _, cols = own.shape
    core = core_ref[0]
    front = core == 0
    end = slices - 1
    opacity_scale = scales[2]

    def stacks(mine, theirs, end_own, end_other):
        own_stack = (
            [jnp.where(front, end_own, theirs[end])] + mine + [jnp.where(front, theirs[0], end_own)]
        )
        other_stack = (
            [jnp.where(front, mine[end], end_other)]
            + theirs
            + [jnp.where(front, end_other, mine[0])]
        )
        return own_stack, other_stack

    def finish(own_part, other_part):
        both = over(pick(front, own_part, other_part), pick(front, other_part, own_part))
        both[3] = (1.0 - both[3]) * opacity_scale
        return both

    def block(b, carry):
        for half in range(0, BLOCK, HALF):
            here = pl.ds(pl.multiple_of(b * BLOCK + half, HALF), HALF)
            rows = slice(half, half + HALF)
            for start in range(0, cols, LANES):
                lanes = slice(start, start + LANES)

                def half_slab(stack, terms):
                    first, last, middle, slope, norm = terms[:5]
                    parts = []
                    for ref, at, z in ((first, 0, 0), (last, 1, end)):
                        accum, transmit = shade(
                            *nothing(), stack[z + 2] - stack[z],
                            slope[at, here, lanes], norm[at, here, lanes],
                            [ref[c, here, lanes] for c in range(4)],
                        )
                        parts.append(accum + [transmit])
                    inner = [middle[c, here, lanes] for c in range(4)]
                    return over(parts[0], over(inner, parts[1]))

                own_stack, other_stack = stacks(
                    [own[z, b, core, rows, lanes].astype(F32) for z in range(slices)],
                    [other[z, b, core, rows, lanes].astype(F32) for z in range(slices)],
                    outer[b, core, rows, lanes].astype(F32),
                    relayed[b, rows, lanes].astype(F32),
                )
                both = finish(half_slab(own_stack, own_terms), half_slab(other_stack, other_terms))
                for c in range(4):
                    at = c * BLOCK + half
                    out[b, at : at + HALF, lanes] = both[c]
        return carry

    lax.fori_loop(0, blocks, block, 0)

    tabs = [tables[c] for c in range(8)]
    b = jnp.where(front, 0, blocks - 1)
    row = lax.broadcasted_iota(jnp.int32, (HALF, LANES), 0)
    at_edge = row == jnp.where(front, 0, HALF - 1)
    for start in range(0, cols, LANES):
        lanes = slice(start, start + LANES)

        def load(ref, *index):
            top = ref[(*index, slice(0, HALF), lanes)].astype(F32)
            return jnp.where(front, top, ref[(*index, slice(HALF, BLOCK), lanes)].astype(F32))

        def edge_own(z):
            upper = top[z, :, lanes].astype(F32)[HALF - 1 :]
            return jnp.where(front, -upper, bottom[z, :, lanes].astype(F32)[0:1])

        def edge_other(z):
            sent = relayed[blocks + z // 2, z % 2 * HALF : (z % 2 + 1) * HALF, lanes].astype(F32)
            return jnp.where(front, -sent[HALF - 1 :], sent[0:1])

        def half_slab(stack, terms, edge):
            accum, transmit = nothing()
            for z in range(slices):
                dx = terms[5][z, :, lanes] + jnp.where(at_edge, edge(z), 0.0)
                dy = terms[6][z, :, lanes]
                accum, transmit = shade(
                    accum, transmit, stack[z + 2] - stack[z],
                    slope_of(dx, dy), norm_of(dx, dy), classify(stack[z + 1], tabs),
                )
            return accum + [transmit]

        own_stack, other_stack = stacks(
            [load(own, z, b, core) for z in range(slices)],
            [load(other, z, b, core) for z in range(slices)],
            load(outer, b, core),
            load(relayed, b),
        )
        both = finish(
            half_slab(own_stack, own_terms, edge_own), half_slab(other_stack, other_terms, edge_other)
        )
        for c in range(4):
            at = pl.multiple_of(c * BLOCK + core * HALF, HALF)
            out[b, pl.ds(at, HALF), lanes] = both[c]


def merge_kernel(parts, scales, out, image):
    cols = parts.shape[2]
    colour_scale, opacity_top = scales[0], scales[1]
    for half in range(0, BLOCK, HALF):
        for start in range(0, cols, LANES):
            lanes = slice(start, start + LANES)
            accum, transmit = nothing()
            for s in range(parts.shape[0]):
                part = [
                    parts[s, c * BLOCK + half : c * BLOCK + half + HALF, lanes] for c in range(4)
                ]
                accum = [a + transmit * p for a, p in zip(accum, part[:3])]
                transmit = transmit - transmit * (part[3] * opacity_top)
            whole = [a * colour_scale for a in accum] + [1.0 - transmit]
            for c in range(4):
                at = start // LANES, slice(c * BLOCK + half, c * BLOCK + half + HALF)
                image[at] = whole[c]
    for r in range(BLOCK):
        for start in range(0, cols, LANES):
            out[:, r * cols + start : r * cols + start + LANES] = image[
                start // LANES, pl.ds(r, 4, stride=BLOCK)
            ]


def shards(volume, transfer_table):
    slices, rows, cols = volume.shape
    depth_count = lax.axis_size("depth")
    img_count = lax.axis_size("img")
    chips = depth_count // 2
    depth_total = slices * depth_count
    blocks = rows // (2 * BLOCK)
    core = lax.axis_index("depth") % 2

    half = rows // 2
    split = (slices, blocks, 2, BLOCK, cols)
    core_arg = core.astype(jnp.int32).reshape(1)
    same_core = [[2 * j + c for j in range(chips)] for c in range(2)]
    vmem = pl.BlockSpec(memory_space=pltpu.MemorySpace.VMEM)
    smem = pl.BlockSpec(memory_space=pltpu.MemorySpace.SMEM)
    params = pltpu.CompilerParams(vmem_limit_bytes=16 << 20)
    quad = jax.ShapeDtypeStruct((4, half, cols), F32)
    two = jax.ShapeDtypeStruct((2, half, cols), F32)
    unit = jax.ShapeDtypeStruct((slices, HALF, cols), F32)
    terms = (quad, quad, quad, two, two, unit, unit)

    partner = [(d, d ^ 1) for d in range(depth_count)]
    other = lax.ppermute(volume, "depth", partner).reshape(split)
    outer = lax.ppermute(
        lax.dynamic_index_in_dim(volume, (slices - 1) * core, 0, False), "depth",
        [(d, d + 1) for d in range(1, depth_count - 1, 2)]
        + [(d + 1, d) for d in range(1, depth_count - 1, 2)],
    ).reshape(split[1:])
    down = [(i, i + 1) for i in range(img_count - 1)]
    top = lax.ppermute(volume[:, rows - HALF :], "img", down)
    bottom = lax.ppermute(volume[:, :HALF], "img", [(to, at) for at, to in down])
    own = volume.reshape(split)
    entries = transfer_table.shape[1]
    *ops, scales = pl.pallas_call(
        functools.partial(
            prepare_kernel, slab_share=2.0 * slices / depth_total, depth_total=depth_total
        ),
        out_shape=(
            jax.ShapeDtypeStruct((half, rows), BF16),
            jax.ShapeDtypeStruct((cols, cols), BF16),
            jax.ShapeDtypeStruct((8, HALF, entries), F32),
            jax.ShapeDtypeStruct((3, HALF, LANES), F32),
        ),
        in_specs=[smem, vmem],
        out_specs=(vmem,) * 4,
        compiler_params=params,
        name="prepare",
    )(core_arg, transfer_table)
    def slices_terms(cells, previous, name):
        return pl.pallas_call(
            slices_kernel,
            out_shape=terms,
            in_specs=[smem] + [vmem] * (4 + len(previous)),
            out_specs=(vmem,) * 7,
            scratch_shapes=[pltpu.VMEM((slices - 2, half, cols), F32)] * 2,
            compiler_params=params,
            name=name,
        )(core_arg, cells, *ops, *previous)

    own_terms = slices_terms(own, (), "own")
    outer, top, bottom, _ = lax.optimization_barrier((outer, top, bottom, own_terms[6]))
    relayed = pl.pallas_call(
        relay_kernel,
        out_shape=jax.ShapeDtypeStruct((blocks + slices // 2, BLOCK, cols), BF16),
        in_specs=[smem] + [vmem] * 3,
        out_specs=vmem,
        compiler_params=params,
        name="relay",
    )(core_arg, outer, top, bottom)
    other_terms = slices_terms(other, (relayed,), "other")
    relayed = lax.ppermute(relayed, "depth", partner)
    partial_image = pl.pallas_call(
        slab_kernel,
        out_shape=jax.ShapeDtypeStruct((blocks, 4 * BLOCK, cols), F32),
        in_specs=[smem] + [vmem] * 22,
        out_specs=vmem,
        compiler_params=params,
        name="slab",
    )(
        core_arg, own, other, outer, relayed, top, bottom, ops[2], scales, *own_terms, *other_terms,
    )
    pieces = lax.all_to_all(
        partial_image.astype(jnp.float16), "depth", split_axis=0, concat_axis=0, tiled=True,
        axis_index_groups=same_core,
    )
    return pl.pallas_call(
        merge_kernel,
        out_shape=jax.ShapeDtypeStruct((4, BLOCK * cols), F32),
        in_specs=[vmem, vmem],
        out_specs=vmem,
        scratch_shapes=[pltpu.VMEM((cols // LANES, 4 * BLOCK, LANES), F32)],
        compiler_params=params,
        name="merge",
    )(pieces.astype(F32), scales)


def solution(mesh):
    placed = (P("depth", "img", None), P())
    return jax.shard_map(
        shards, mesh=mesh, in_specs=placed, out_specs=P(None, ("img", "depth")), check_vma=False
    )
```

```python
import functools

import jax
import jax.numpy as jnp
import numpy as np
from jax import lax
from jax.experimental import pallas as pl
from jax.experimental.pallas import tpu as pltpu
from jax.sharding import PartitionSpec as P

F32 = jnp.float32
BF16 = jnp.bfloat16
BLOCK = 16
HALF = 8
LANES = 128
TINY = 1e-30
SLOPE = 1.4 / 3.0


def row_differences(rows, core):
    shape = (rows // 2, rows)
    local = lax.broadcasted_iota(jnp.int32, shape, 0)
    there = lax.broadcasted_iota(jnp.int32, shape, 1)
    step = there - (local + (local & -BLOCK) + core * BLOCK)
    return jnp.where(step == 1, 1.0, jnp.where(step == -1, -1.0, 0.0)).astype(BF16)


def column_differences(cols):
    step = lax.broadcasted_iota(jnp.int32, (cols, cols), 0) - lax.broadcasted_iota(
        jnp.int32, (cols, cols), 1
    )
    return jnp.where(step == 1, 1.0, jnp.where(step == -1, -1.0, 0.0)).astype(BF16)


def tops(table, slab_share):
    colour = jnp.max(jnp.max(table[0:3], axis=0, keepdims=True), axis=1, keepdims=True)
    extinction = jnp.max(table[3:4], axis=1, keepdims=True)
    return jnp.maximum(colour, TINY), jnp.maximum(extinction * slab_share, TINY)


def prepare_kernel(
    core_ref, cells, table_ref, rows_op, cols_op, tables, scales, outer, upper_edge, lower_edge,
    *, slab_share, depth_total,
):
    rows = cells.shape[1]
    outer[...] = cells[(cells.shape[0] - 1) * core_ref[0]]
    upper_edge[...] = cells[:, :HALF]
    lower_edge[...] = cells[:, rows - HALF :]
    table = table_ref[...].astype(F32)
    entries = table.shape[1]
    rows_op[...] = row_differences(rows_op.shape[1], core_ref[0])
    cols_op[...] = column_differences(cols_op.shape[1])
    colour_top, opacity_top = tops(table, slab_share)
    scale = SLOPE / (colour_top * opacity_top)
    last = lax.broadcasted_iota(jnp.int32, (HALF, entries), 1) == entries - 1
    for c in range(4):
        factor = scale if c < 3 else float(-np.log2(np.e) / depth_total)
        lower = jnp.broadcast_to(table[c : c + 1] * factor, (HALF, entries))
        tables[c] = lower
        tables[c + 4] = jnp.where(last, lower, pltpu.roll(lower, entries - 1, 1))
    for at, value in enumerate((colour_top * opacity_top, opacity_top, 1.0 / opacity_top)):
        scales[at] = jnp.broadcast_to(value, (HALF, LANES))


def look_up(table, index):
    return jnp.take_along_axis(table, index, axis=1, mode="promise_in_bounds")


def classify(centre, tabs):
    position = centre * float(tabs[0].shape[1] - 1)
    knot = position.astype(jnp.int32)
    part = position - knot.astype(F32)
    upper = part.astype(BF16).astype(F32)
    lower = (1.0 - part).astype(BF16).astype(F32)
    values = [
        lower * look_up(tabs[c], knot) + upper * look_up(tabs[c + 4], knot) for c in range(4)
    ]
    return values[:3] + [jnp.exp2(values[3])]


def shade(accum, transmit, dz, slope_xy, norm_xy, found):
    shading = 0.3 / SLOPE + jnp.abs(dz + slope_xy) * lax.rsqrt(dz * dz + norm_xy)
    left = transmit * found[3]
    gain = (transmit - left) * shading
    return [a + gain * v for a, v in zip(accum, found[:3])], left


def slope_of(dx, dy):
    return 0.5 * dx + dy


def norm_of(dx, dy):
    return dx * dx + dy * dy + 0.04


def over(near, far):
    return [n + near[3] * f for n, f in zip(near[:3], far[:3])] + [near[3] * far[3]]


def nothing():
    return [jnp.zeros((HALF, LANES), F32)] * 3, jnp.ones((HALF, LANES), F32)


def pick(condition, a, b):
    return [jnp.where(condition, x, y) for x, y in zip(a, b)]


def slices_kernel(core_ref, cells, rows_op, cols_op, tables, *refs):
    first, last, middle, slope, norm, edge_dx, edge_dy, inner_slope, inner_norm = refs[-9:]
    core = core_ref[0]
    slices, blocks, _, _, cols = cells.shape
    rows = blocks * BLOCK
    ends = (0, slices - 1)
    for z in range(slices):
        dx = jnp.dot(rows_op[...], cells[z].reshape(2 * rows, cols), preferred_element_type=F32)
        dy = jnp.dot(
            cells[z, :, core].reshape(rows, cols), cols_op[...], preferred_element_type=F32
        )
        to_slope, to_norm, at = (
            (slope, norm, ends.index(z)) if z in ends else (inner_slope, inner_norm, z - 1)
        )
        to_slope[at] = slope_of(dx, dy)
        to_norm[at] = norm_of(dx, dy)
        edge_dx[z] = jnp.where(core == 0, dx[:HALF], dx[rows - HALF :])
        edge_dy[z] = jnp.where(core == 0, dy[:HALF], dy[rows - HALF :])
    tabs = [tables[c] for c in range(8)]

    def block(bb, carry):
      for sub in range(2):
        b = bb * 2 + sub
        for half in range(0, BLOCK, HALF):
            here = pl.ds(pl.multiple_of(b * BLOCK + half, HALF), HALF)
            rows = slice(half, half + HALF)
            for start in range(0, cols, LANES):
                lanes = slice(start, start + LANES)
                mine = [cells[z, b, core, rows, lanes].astype(F32) for z in range(slices)]
                accum, transmit = nothing()
                for z in range(slices):
                    found = classify(mine[z], tabs)
                    if z in ends:
                        ref = last if z else first
                        for c in range(4):
                            ref[c, here, lanes] = found[c]
                    else:
                        accum, transmit = shade(
                            accum, transmit, mine[z + 1] - mine[z - 1],
                            inner_slope[z - 1, here, lanes], inner_norm[z - 1, here, lanes], found,
                        )
                for c in range(3):
                    middle[c, here, lanes] = accum[c]
                middle[3, here, lanes] = transmit
      return carry

    lax.fori_loop(0, blocks // 2, block, 0)


def relay_kernel(core_ref, outer, top, bottom, out):
    blocks = outer.shape[0]
    core = core_ref[0]
    out[:blocks] = outer[:, 1 - core]

    def edges(ref):
        for z in range(0, ref.shape[0], 2):
            at = blocks + z // 2
            out[at, :HALF, :] = ref[z]
            out[at, HALF:, :] = ref[z + 1]

    @pl.when(core == 0)
    def _():
        edges(bottom)

    @pl.when(core != 0)
    def _():
        edges(top)


def slab_kernel(
    core_ref, own, other, outer, relayed, top, bottom, tables, scales, *refs
):
    own_terms, other_terms, out = refs[:7], refs[7:14], refs[14]
    slices, blocks, _, _, cols = own.shape
    core = core_ref[0]
    front = core == 0
    end = slices - 1
    opacity_scale = scales[2]

    def stacks(mine, theirs, end_own, end_other):
        own_stack = (
            [jnp.where(front, end_own, theirs[end])] + mine + [jnp.where(front, theirs[0], end_own)]
        )
        other_stack = (
            [jnp.where(front, mine[end], end_other)]
            + theirs
            + [jnp.where(front, end_other, mine[0])]
        )
        return own_stack, other_stack

    def finish(own_part, other_part):
        both = over(pick(front, own_part, other_part), pick(front, other_part, own_part))
        both[3] = (1.0 - both[3]) * opacity_scale
        return both

    def block(b, carry):
        for half in range(0, BLOCK, HALF):
            here = pl.ds(pl.multiple_of(b * BLOCK + half, HALF), HALF)
            rows = slice(half, half + HALF)
            for start in range(0, cols, LANES):
                lanes = slice(start, start + LANES)

                def half_slab(stack, terms):
                    first, last, middle, slope, norm = terms[:5]
                    parts = []
                    for ref, at, z in ((first, 0, 0), (last, 1, end)):
                        accum, transmit = shade(
                            *nothing(), stack[z + 2] - stack[z],
                            slope[at, here, lanes], norm[at, here, lanes],
                            [ref[c, here, lanes] for c in range(4)],
                        )
                        parts.append(accum + [transmit])
                    inner = [middle[c, here, lanes] for c in range(4)]
                    return over(parts[0], over(inner, parts[1]))

                own_stack, other_stack = stacks(
                    [own[z, b, core, rows, lanes].astype(F32) for z in range(slices)],
                    [other[z, b, core, rows, lanes].astype(F32) for z in range(slices)],
                    outer[b, core, rows, lanes].astype(F32),
                    relayed[b, rows, lanes].astype(F32),
                )
                both = finish(half_slab(own_stack, own_terms), half_slab(other_stack, other_terms))
                for c in range(4):
                    at = c * BLOCK + half
                    out[b, at : at + HALF, lanes] = both[c]
        return carry

    lax.fori_loop(0, blocks, block, 0)

    tabs = [tables[c] for c in range(8)]
    b = jnp.where(front, 0, blocks - 1)
    row = lax.broadcasted_iota(jnp.int32, (HALF, LANES), 0)
    at_edge = row == jnp.where(front, 0, HALF - 1)
    for start in range(0, cols, LANES):
        lanes = slice(start, start + LANES)

        def load(ref, *index):
            top = ref[(*index, slice(0, HALF), lanes)].astype(F32)
            return jnp.where(front, top, ref[(*index, slice(HALF, BLOCK), lanes)].astype(F32))

        def edge_own(z):
            upper = top[z, :, lanes].astype(F32)[HALF - 1 :]
            return jnp.where(front, -upper, bottom[z, :, lanes].astype(F32)[0:1])

        def edge_other(z):
            sent = relayed[blocks + z // 2, z % 2 * HALF : (z % 2 + 1) * HALF, lanes].astype(F32)
            return jnp.where(front, -sent[HALF - 1 :], sent[0:1])

        def half_slab(stack, terms, edge):
            accum, transmit = nothing()
            for z in range(slices):
                dx = terms[5][z, :, lanes] + jnp.where(at_edge, edge(z), 0.0)
                dy = terms[6][z, :, lanes]
                accum, transmit = shade(
                    accum, transmit, stack[z + 2] - stack[z],
                    slope_of(dx, dy), norm_of(dx, dy), classify(stack[z + 1], tabs),
                )
            return accum + [transmit]

        own_stack, other_stack = stacks(
            [load(own, z, b, core) for z in range(slices)],
            [load(other, z, b, core) for z in range(slices)],
            load(outer, b, core),
            load(relayed, b),
        )
        both = finish(
            half_slab(own_stack, own_terms, edge_own), half_slab(other_stack, other_terms, edge_other)
        )
        for c in range(4):
            at = pl.multiple_of(c * BLOCK + core * HALF, HALF)
            out[b, pl.ds(at, HALF), lanes] = both[c]


def merge_kernel(parts, scales, out, image):
    cols = parts.shape[2]
    colour_scale, opacity_top = scales[0], scales[1]
    for half in range(0, BLOCK, HALF):
        for start in range(0, cols, LANES):
            lanes = slice(start, start + LANES)
            accum, transmit = nothing()
            for s in range(parts.shape[0]):
                part = [
                    parts[s, c * BLOCK + half : c * BLOCK + half + HALF, lanes] for c in range(4)
                ]
                accum = [a + transmit * p for a, p in zip(accum, part[:3])]
                transmit = transmit - transmit * (part[3] * opacity_top)
            whole = [a * colour_scale for a in accum] + [1.0 - transmit]
            for c in range(4):
                at = start // LANES, slice(c * BLOCK + half, c * BLOCK + half + HALF)
                image[at] = whole[c]
    for r in range(BLOCK):
        for start in range(0, cols, LANES):
            out[:, r * cols + start : r * cols + start + LANES] = image[
                start // LANES, pl.ds(r, 4, stride=BLOCK)
            ]


def shards(volume, transfer_table):
    slices, rows, cols = volume.shape
    depth_count = lax.axis_size("depth")
    img_count = lax.axis_size("img")
    chips = depth_count // 2
    depth_total = slices * depth_count
    blocks = rows // (2 * BLOCK)
    core = lax.axis_index("depth") % 2

    half = rows // 2
    split = (slices, blocks, 2, BLOCK, cols)
    core_arg = core.astype(jnp.int32).reshape(1)
    same_core = [[2 * j + c for j in range(chips)] for c in range(2)]
    vmem = pl.BlockSpec(memory_space=pltpu.MemorySpace.VMEM)
    smem = pl.BlockSpec(memory_space=pltpu.MemorySpace.SMEM)
    params = pltpu.CompilerParams(vmem_limit_bytes=16 << 20)
    quad = jax.ShapeDtypeStruct((4, half, cols), F32)
    two = jax.ShapeDtypeStruct((2, half, cols), F32)
    unit = jax.ShapeDtypeStruct((slices, HALF, cols), F32)
    edge = jax.ShapeDtypeStruct((slices, HALF, cols), BF16)
    terms = (quad, quad, quad, two, two, unit, unit)

    partner = [(d, d ^ 1) for d in range(depth_count)]
    other = lax.ppermute(volume, "depth", partner).reshape(split)
    own = volume.reshape(split)
    entries = transfer_table.shape[1]
    *ops, scales, outer, upper_edge, lower_edge = pl.pallas_call(
        functools.partial(
            prepare_kernel, slab_share=2.0 * slices / depth_total, depth_total=depth_total
        ),
        out_shape=(
            jax.ShapeDtypeStruct((half, rows), BF16),
            jax.ShapeDtypeStruct((cols, cols), BF16),
            jax.ShapeDtypeStruct((8, HALF, entries), F32),
            jax.ShapeDtypeStruct((3, HALF, LANES), F32),
            jax.ShapeDtypeStruct((rows, cols), BF16),
            edge,
            edge,
        ),
        in_specs=[smem, vmem, vmem],
        out_specs=(vmem,) * 7,
        compiler_params=params,
        name="prepare",
    )(core_arg, volume, transfer_table)
    outer = lax.ppermute(
        outer, "depth",
        [(d, d + 1) for d in range(1, depth_count - 1, 2)]
        + [(d + 1, d) for d in range(1, depth_count - 1, 2)],
    ).reshape(split[1:])
    down = [(i, i + 1) for i in range(img_count - 1)]
    top = lax.ppermute(lower_edge, "img", down)
    bottom = lax.ppermute(upper_edge, "img", [(to, at) for at, to in down])
    def slices_terms(cells, previous, name):
        return pl.pallas_call(
            slices_kernel,
            out_shape=terms,
            in_specs=[smem] + [vmem] * (4 + len(previous)),
            out_specs=(vmem,) * 7,
            scratch_shapes=[pltpu.VMEM((slices - 2, half, cols), F32)] * 2,
            compiler_params=params,
            name=name,
        )(core_arg, cells, *ops, *previous)

    own_terms = slices_terms(own, (), "own")
    outer, top, bottom, _ = lax.optimization_barrier((outer, top, bottom, own_terms[6]))
    relayed = pl.pallas_call(
        relay_kernel,
        out_shape=jax.ShapeDtypeStruct((blocks + slices // 2, BLOCK, cols), BF16),
        in_specs=[smem] + [vmem] * 3,
        out_specs=vmem,
        compiler_params=params,
        name="relay",
    )(core_arg, outer, top, bottom)
    other_terms = slices_terms(other, (relayed,), "other")
    relayed = lax.ppermute(relayed, "depth", partner)
    partial_image = pl.pallas_call(
        slab_kernel,
        out_shape=jax.ShapeDtypeStruct((blocks, 4 * BLOCK, cols), F32),
        in_specs=[smem] + [vmem] * 22,
        out_specs=vmem,
        compiler_params=params,
        name="slab",
    )(
        core_arg, own, other, outer, relayed, top, bottom, ops[2], scales, *own_terms, *other_terms,
    )
    pieces = lax.all_to_all(
        partial_image.astype(jnp.float16), "depth", split_axis=0, concat_axis=0, tiled=True,
        axis_index_groups=same_core,
    )
    return pl.pallas_call(
        merge_kernel,
        out_shape=jax.ShapeDtypeStruct((4, BLOCK * cols), F32),
        in_specs=[vmem, vmem],
        out_specs=vmem,
        scratch_shapes=[pltpu.VMEM((cols // LANES, 4 * BLOCK, LANES), F32)],
        compiler_params=params,
        name="merge",
    )(pieces.astype(F32), scales)


def solution(mesh):
    placed = (P("depth", "img", None), P())
    return jax.shard_map(
        shards, mesh=mesh, in_specs=placed, out_specs=P(None, ("img", "depth")), check_vma=False
    )
```

```python
import functools

import jax
import jax.numpy as jnp
import numpy as np
from jax import lax
from jax.experimental import pallas as pl
from jax.experimental.pallas import tpu as pltpu
from jax.sharding import PartitionSpec as P

F32 = jnp.float32
BF16 = jnp.bfloat16
BLOCK = 16
HALF = 8
LANES = 128
TINY = 1e-30
SLOPE = 1.4 / 3.0


def row_differences(rows, core):
    shape = (rows // 2, rows)
    local = lax.broadcasted_iota(jnp.int32, shape, 0)
    there = lax.broadcasted_iota(jnp.int32, shape, 1)
    step = there - (local + (local & -BLOCK) + core * BLOCK)
    return jnp.where(step == 1, 1.0, jnp.where(step == -1, -1.0, 0.0)).astype(BF16)


def column_differences(cols):
    step = lax.broadcasted_iota(jnp.int32, (cols, cols), 0) - lax.broadcasted_iota(
        jnp.int32, (cols, cols), 1
    )
    return jnp.where(step == 1, 1.0, jnp.where(step == -1, -1.0, 0.0)).astype(BF16)


def tops(table, slab_share):
    colour = jnp.max(jnp.max(table[0:3], axis=0, keepdims=True), axis=1, keepdims=True)
    extinction = jnp.max(table[3:4], axis=1, keepdims=True)
    return jnp.maximum(colour, TINY), jnp.maximum(extinction * slab_share, TINY)


def prepare_kernel(
    core_ref, cells, table_ref, rows_op, cols_op, tables, scales, outer,
    *, slab_share, depth_total,
):
    outer[...] = cells[(cells.shape[0] - 1) * core_ref[0]]
    table = table_ref[...].astype(F32)
    entries = table.shape[1]
    rows_op[...] = row_differences(rows_op.shape[1], core_ref[0])
    cols_op[...] = column_differences(cols_op.shape[1])
    colour_top, opacity_top = tops(table, slab_share)
    scale = SLOPE / (colour_top * opacity_top)
    last = lax.broadcasted_iota(jnp.int32, (HALF, entries), 1) == entries - 1
    for c in range(4):
        factor = scale if c < 3 else float(-np.log2(np.e) / depth_total)
        lower = jnp.broadcast_to(table[c : c + 1] * factor, (HALF, entries))
        tables[c] = lower
        tables[c + 4] = jnp.where(last, lower, pltpu.roll(lower, entries - 1, 1))
    for at, value in enumerate((colour_top * opacity_top, opacity_top, 1.0 / opacity_top)):
        scales[at] = jnp.broadcast_to(value, (HALF, LANES))


def look_up(table, index):
    return jnp.take_along_axis(table, index, axis=1, mode="promise_in_bounds")


def classify(centre, tabs):
    position = centre * float(tabs[0].shape[1] - 1)
    knot = position.astype(jnp.int32)
    part = position - knot.astype(F32)
    upper = part.astype(BF16).astype(F32)
    lower = (1.0 - part).astype(BF16).astype(F32)
    values = [
        lower * look_up(tabs[c], knot) + upper * look_up(tabs[c + 4], knot) for c in range(4)
    ]
    return values[:3] + [jnp.exp2(values[3])]


def shade(accum, transmit, dz, slope_xy, norm_xy, found):
    shading = 0.3 / SLOPE + jnp.abs(dz + slope_xy) * lax.rsqrt(dz * dz + norm_xy)
    left = transmit * found[3]
    gain = (transmit - left) * shading
    return [a + gain * v for a, v in zip(accum, found[:3])], left


def slope_of(dx, dy):
    return 0.5 * dx + dy


def norm_of(dx, dy):
    return dx * dx + dy * dy + 0.04


def over(near, far):
    return [n + near[3] * f for n, f in zip(near[:3], far[:3])] + [near[3] * far[3]]


def nothing():
    return [jnp.zeros((HALF, LANES), F32)] * 3, jnp.ones((HALF, LANES), F32)


def pick(condition, a, b):
    return [jnp.where(condition, x, y) for x, y in zip(a, b)]


def slices_kernel(core_ref, cells, rows_op, cols_op, tables, *refs):
    first, last, middle, slope, norm, edge_dx, edge_dy, inner_slope, inner_norm = refs[-9:]
    core = core_ref[0]
    slices, blocks, _, _, cols = cells.shape
    rows = blocks * BLOCK
    ends = (0, slices - 1)
    for z in range(slices):
        dx = jnp.dot(rows_op[...], cells[z].reshape(2 * rows, cols), preferred_element_type=F32)
        dy = jnp.dot(
            cells[z, :, core].reshape(rows, cols), cols_op[...], preferred_element_type=F32
        )
        to_slope, to_norm, at = (
            (slope, norm, ends.index(z)) if z in ends else (inner_slope, inner_norm, z - 1)
        )
        to_slope[at] = slope_of(dx, dy)
        to_norm[at] = norm_of(dx, dy)
        edge_dx[z] = jnp.where(core == 0, dx[:HALF], dx[rows - HALF :])
        edge_dy[z] = jnp.where(core == 0, dy[:HALF], dy[rows - HALF :])
    tabs = [tables[c] for c in range(8)]

    def block(bb, carry):
      for sub in range(2):
        b = bb * 2 + sub
        for half in range(0, BLOCK, HALF):
            here = pl.ds(pl.multiple_of(b * BLOCK + half, HALF), HALF)
            rows = slice(half, half + HALF)
            for start in range(0, cols, LANES):
                lanes = slice(start, start + LANES)
                mine = [cells[z, b, core, rows, lanes].astype(F32) for z in range(slices)]
                accum, transmit = nothing()
                for z in range(slices):
                    found = classify(mine[z], tabs)
                    if z in ends:
                        ref = last if z else first
                        for c in range(4):
                            ref[c, here, lanes] = found[c]
                    else:
                        accum, transmit = shade(
                            accum, transmit, mine[z + 1] - mine[z - 1],
                            inner_slope[z - 1, here, lanes], inner_norm[z - 1, here, lanes], found,
                        )
                for c in range(3):
                    middle[c, here, lanes] = accum[c]
                middle[3, here, lanes] = transmit
      return carry

    lax.fori_loop(0, blocks // 2, block, 0)


def relay_kernel(core_ref, own, other, outer, relayed, edge):
    slices, blocks, _, _, _ = own.shape
    core = core_ref[0]
    relayed[...] = outer[:, 1 - core]

    @pl.when(core == 0)
    def _():
        edge[:slices] = own[:, blocks - 1, 1, HALF:, :]
        edge[slices:] = other[:, blocks - 1, 1, HALF:, :]

    @pl.when(core != 0)
    def _():
        edge[:slices] = own[:, 0, 0, :HALF, :]
        edge[slices:] = other[:, 0, 0, :HALF, :]


def slab_kernel(
    core_ref, own, other, outer, relayed, edges, tables, scales, *refs
):
    own_terms, other_terms, out = refs[:7], refs[7:14], refs[14]
    slices, blocks, _, _, cols = own.shape
    core = core_ref[0]
    front = core == 0
    end = slices - 1
    opacity_scale = scales[2]

    def stacks(mine, theirs, end_own, end_other):
        own_stack = (
            [jnp.where(front, end_own, theirs[end])] + mine + [jnp.where(front, theirs[0], end_own)]
        )
        other_stack = (
            [jnp.where(front, mine[end], end_other)]
            + theirs
            + [jnp.where(front, end_other, mine[0])]
        )
        return own_stack, other_stack

    def finish(own_part, other_part):
        both = over(pick(front, own_part, other_part), pick(front, other_part, own_part))
        both[3] = (1.0 - both[3]) * opacity_scale
        return both

    def block(b, carry):
        for half in range(0, BLOCK, HALF):
            here = pl.ds(pl.multiple_of(b * BLOCK + half, HALF), HALF)
            rows = slice(half, half + HALF)
            for start in range(0, cols, LANES):
                lanes = slice(start, start + LANES)

                def half_slab(stack, terms):
                    first, last, middle, slope, norm = terms[:5]
                    parts = []
                    for ref, at, z in ((first, 0, 0), (last, 1, end)):
                        accum, transmit = shade(
                            *nothing(), stack[z + 2] - stack[z],
                            slope[at, here, lanes], norm[at, here, lanes],
                            [ref[c, here, lanes] for c in range(4)],
                        )
                        parts.append(accum + [transmit])
                    inner = [middle[c, here, lanes] for c in range(4)]
                    return over(parts[0], over(inner, parts[1]))

                own_stack, other_stack = stacks(
                    [own[z, b, core, rows, lanes].astype(F32) for z in range(slices)],
                    [other[z, b, core, rows, lanes].astype(F32) for z in range(slices)],
                    outer[b, core, rows, lanes].astype(F32),
                    relayed[b, rows, lanes].astype(F32),
                )
                both = finish(half_slab(own_stack, own_terms), half_slab(other_stack, other_terms))
                for c in range(4):
                    at = c * BLOCK + half
                    out[b, at : at + HALF, lanes] = both[c]
        return carry

    lax.fori_loop(0, blocks, block, 0)

    tabs = [tables[c] for c in range(8)]
    b = jnp.where(front, 0, blocks - 1)
    row = lax.broadcasted_iota(jnp.int32, (HALF, LANES), 0)
    at_edge = row == jnp.where(front, 0, HALF - 1)
    for start in range(0, cols, LANES):
        lanes = slice(start, start + LANES)

        def load(ref, *index):
            top = ref[(*index, slice(0, HALF), lanes)].astype(F32)
            return jnp.where(front, top, ref[(*index, slice(HALF, BLOCK), lanes)].astype(F32))

        def half_slab(stack, terms, at):
            accum, transmit = nothing()
            for z in range(slices):
                halo = edges[at + z, :, lanes].astype(F32)
                halo = jnp.where(front, -halo[HALF - 1 :], halo[0:1])
                dx = terms[5][z, :, lanes] + jnp.where(at_edge, halo, 0.0)
                dy = terms[6][z, :, lanes]
                accum, transmit = shade(
                    accum, transmit, stack[z + 2] - stack[z],
                    slope_of(dx, dy), norm_of(dx, dy), classify(stack[z + 1], tabs),
                )
            return accum + [transmit]

        own_stack, other_stack = stacks(
            [load(own, z, b, core) for z in range(slices)],
            [load(other, z, b, core) for z in range(slices)],
            load(outer, b, core),
            load(relayed, b),
        )
        both = finish(
            half_slab(own_stack, own_terms, 0), half_slab(other_stack, other_terms, slices)
        )
        for c in range(4):
            at = pl.multiple_of(c * BLOCK + core * HALF, HALF)
            out[b, pl.ds(at, HALF), lanes] = both[c]


def merge_kernel(parts, scales, out, image):
    cols = parts.shape[2]
    colour_scale, opacity_top = scales[0], scales[1]
    for half in range(0, BLOCK, HALF):
        for start in range(0, cols, LANES):
            lanes = slice(start, start + LANES)
            accum, transmit = nothing()
            for s in range(parts.shape[0]):
                part = [
                    parts[s, c * BLOCK + half : c * BLOCK + half + HALF, lanes] for c in range(4)
                ]
                accum = [a + transmit * p for a, p in zip(accum, part[:3])]
                transmit = transmit - transmit * (part[3] * opacity_top)
            whole = [a * colour_scale for a in accum] + [1.0 - transmit]
            for c in range(4):
                at = start // LANES, slice(c * BLOCK + half, c * BLOCK + half + HALF)
                image[at] = whole[c]
    for r in range(BLOCK):
        for start in range(0, cols, LANES):
            out[:, r * cols + start : r * cols + start + LANES] = image[
                start // LANES, pl.ds(r, 4, stride=BLOCK)
            ]


def shards(volume, transfer_table):
    slices, rows, cols = volume.shape
    depth_count = lax.axis_size("depth")
    img_count = lax.axis_size("img")
    chips = depth_count // 2
    depth_total = slices * depth_count
    blocks = rows // (2 * BLOCK)
    core = lax.axis_index("depth") % 2

    half = rows // 2
    split = (slices, blocks, 2, BLOCK, cols)
    core_arg = core.astype(jnp.int32).reshape(1)
    same_core = [[2 * j + c for j in range(chips)] for c in range(2)]
    vmem = pl.BlockSpec(memory_space=pltpu.MemorySpace.VMEM)
    smem = pl.BlockSpec(memory_space=pltpu.MemorySpace.SMEM)
    params = pltpu.CompilerParams(vmem_limit_bytes=16 << 20)
    quad = jax.ShapeDtypeStruct((4, half, cols), F32)
    two = jax.ShapeDtypeStruct((2, half, cols), F32)
    unit = jax.ShapeDtypeStruct((slices, HALF, cols), F32)
    plane = jax.ShapeDtypeStruct((blocks, BLOCK, cols), BF16)
    edge = jax.ShapeDtypeStruct((2 * slices, HALF, cols), BF16)
    terms = (quad, quad, quad, two, two, unit, unit)

    partner = [(d, d ^ 1) for d in range(depth_count)]
    own = volume.reshape(split)
    entries = transfer_table.shape[1]
    *ops, scales, outer = pl.pallas_call(
        functools.partial(
            prepare_kernel, slab_share=2.0 * slices / depth_total, depth_total=depth_total
        ),
        out_shape=(
            jax.ShapeDtypeStruct((half, rows), BF16),
            jax.ShapeDtypeStruct((cols, cols), BF16),
            jax.ShapeDtypeStruct((8, HALF, entries), F32),
            jax.ShapeDtypeStruct((3, HALF, LANES), F32),
            jax.ShapeDtypeStruct((rows, cols), BF16),
        ),
        in_specs=[smem, vmem, vmem],
        out_specs=(vmem,) * 5,
        compiler_params=params,
        name="prepare",
    )(core_arg, volume, transfer_table)
    outer = lax.ppermute(
        outer, "depth",
        [(d, d + 1) for d in range(1, depth_count - 1, 2)]
        + [(d + 1, d) for d in range(1, depth_count - 1, 2)],
    ).reshape(split[1:])
    other = lax.ppermute(volume, "depth", partner).reshape(split)

    def slices_terms(cells, previous, name):
        return pl.pallas_call(
            slices_kernel,
            out_shape=terms,
            in_specs=[smem] + [vmem] * (4 + len(previous)),
            out_specs=(vmem,) * 7,
            scratch_shapes=[pltpu.VMEM((slices - 2, half, cols), F32)] * 2,
            compiler_params=params,
            name=name,
        )(core_arg, cells, *ops, *previous)

    own_terms = slices_terms(own, (), "own")
    outer, _ = lax.optimization_barrier((outer, own_terms[6]))
    relayed, edges = pl.pallas_call(
        relay_kernel,
        out_shape=(plane, edge),
        in_specs=[smem] + [vmem] * 3,
        out_specs=(vmem, vmem),
        compiler_params=params,
        name="relay",
    )(core_arg, own, other, outer)
    other_terms = slices_terms(other, (relayed,), "other")
    relayed = lax.ppermute(relayed, "depth", partner)
    edges = lax.ppermute(
        edges, ("img", "depth"),
        [
            (at * depth_count + d, to * depth_count + d)
            for i in range(img_count - 1)
            for d in range(depth_count)
            for at, to in [((i + 1, i) if d % 2 else (i, i + 1))]
        ],
    )
    partial_image = pl.pallas_call(
        slab_kernel,
        out_shape=jax.ShapeDtypeStruct((blocks, 4 * BLOCK, cols), F32),
        in_specs=[smem] + [vmem] * 21,
        out_specs=vmem,
        compiler_params=params,
        name="slab",
    )(
        core_arg, own, other, outer, relayed, edges, ops[2], scales, *own_terms, *other_terms,
    )
    pieces = lax.all_to_all(
        partial_image.astype(jnp.float16), "depth", split_axis=0, concat_axis=0, tiled=True,
        axis_index_groups=same_core,
    )
    return pl.pallas_call(
        merge_kernel,
        out_shape=jax.ShapeDtypeStruct((4, BLOCK * cols), F32),
        in_specs=[vmem, vmem],
        out_specs=vmem,
        scratch_shapes=[pltpu.VMEM((cols // LANES, 4 * BLOCK, LANES), F32)],
        compiler_params=params,
        name="merge",
    )(pieces.astype(F32), scales)


def solution(mesh):
    placed = (P("depth", "img", None), P())
    return jax.shard_map(
        shards, mesh=mesh, in_specs=placed, out_specs=P(None, ("img", "depth")), check_vma=False
    )
```

```python
import functools

import jax
import jax.numpy as jnp
import numpy as np
from jax import lax
from jax.experimental import pallas as pl
from jax.experimental.pallas import tpu as pltpu
from jax.sharding import PartitionSpec as P

F32 = jnp.float32
BF16 = jnp.bfloat16
BLOCK = 16
HALF = 8
LANES = 128
TINY = 1e-30
SLOPE = 1.4 / 3.0


def row_differences(rows, core):
    shape = (rows // 2, rows)
    local = lax.broadcasted_iota(jnp.int32, shape, 0)
    there = lax.broadcasted_iota(jnp.int32, shape, 1)
    step = there - (local + (local & -BLOCK) + core * BLOCK)
    return jnp.where(step == 1, 1.0, jnp.where(step == -1, -1.0, 0.0)).astype(BF16)


def column_differences(cols):
    step = lax.broadcasted_iota(jnp.int32, (cols, cols), 0) - lax.broadcasted_iota(
        jnp.int32, (cols, cols), 1
    )
    return jnp.where(step == 1, 1.0, jnp.where(step == -1, -1.0, 0.0)).astype(BF16)


def tops(table, slab_share):
    colour = jnp.max(jnp.max(table[0:3], axis=0, keepdims=True), axis=1, keepdims=True)
    extinction = jnp.max(table[3:4], axis=1, keepdims=True)
    return jnp.maximum(colour, TINY), jnp.maximum(extinction * slab_share, TINY)


def prepare_kernel(
    core_ref, cells, table_ref, rows_op, cols_op, tables, scales, outer,
    *, slab_share, depth_total,
):
    outer[...] = cells[(cells.shape[0] - 1) * core_ref[0]]
    table = table_ref[...].astype(F32)
    entries = table.shape[1]
    rows_op[...] = row_differences(rows_op.shape[1], core_ref[0])
    cols_op[...] = column_differences(cols_op.shape[1])
    colour_top, opacity_top = tops(table, slab_share)
    scale = SLOPE / (colour_top * opacity_top)
    last = lax.broadcasted_iota(jnp.int32, (HALF, entries), 1) == entries - 1
    for c in range(4):
        factor = scale if c < 3 else float(-np.log2(np.e) / depth_total)
        lower = jnp.broadcast_to(table[c : c + 1] * factor, (HALF, entries))
        tables[c] = lower
        tables[c + 4] = jnp.where(last, lower, pltpu.roll(lower, entries - 1, 1))
    for at, value in enumerate((colour_top * opacity_top, opacity_top, 1.0 / opacity_top)):
        scales[at] = jnp.broadcast_to(value, (HALF, LANES))


def look_up(table, index):
    return jnp.take_along_axis(table, index, axis=1, mode="promise_in_bounds")


def classify(centre, tabs):
    position = centre * float(tabs[0].shape[1] - 1)
    knot = position.astype(jnp.int32)
    part = position - knot.astype(F32)
    upper = part.astype(BF16).astype(F32)
    lower = (1.0 - part).astype(BF16).astype(F32)
    values = [
        lower * look_up(tabs[c], knot) + upper * look_up(tabs[c + 4], knot) for c in range(4)
    ]
    return values[:3] + [jnp.exp2(values[3])]


def shade(accum, transmit, dz, slope_xy, norm_xy, found):
    shading = 0.3 / SLOPE + jnp.abs(dz + slope_xy) * lax.rsqrt(dz * dz + norm_xy)
    left = transmit * found[3]
    gain = (transmit - left) * shading
    return [a + gain * v for a, v in zip(accum, found[:3])], left


def slope_of(dx, dy):
    return 0.5 * dx + dy


def norm_of(dx, dy):
    return dx * dx + dy * dy + 0.04


def over(near, far):
    return [n + near[3] * f for n, f in zip(near[:3], far[:3])] + [near[3] * far[3]]


def nothing():
    return [jnp.zeros((HALF, LANES), F32)] * 3, jnp.ones((HALF, LANES), F32)


def pick(condition, a, b):
    return [jnp.where(condition, x, y) for x, y in zip(a, b)]


def slices_kernel(core_ref, cells, rows_op, cols_op, tables, *refs):
    first, last, middle, slope, norm, edge_dx, edge_dy, inner_slope, inner_norm = refs[-9:]
    core = core_ref[0]
    slices, blocks, _, _, cols = cells.shape
    rows = blocks * BLOCK
    ends = (0, slices - 1)
    for z in range(slices):
        dx = jnp.dot(rows_op[...], cells[z].reshape(2 * rows, cols), preferred_element_type=F32)
        dy = jnp.dot(
            cells[z, :, core].reshape(rows, cols), cols_op[...], preferred_element_type=F32
        )
        to_slope, to_norm, at = (
            (slope, norm, ends.index(z)) if z in ends else (inner_slope, inner_norm, z - 1)
        )
        to_slope[at] = slope_of(dx, dy)
        to_norm[at] = norm_of(dx, dy)
        edge_dx[z] = jnp.where(core == 0, dx[:HALF], dx[rows - HALF :])
        edge_dy[z] = jnp.where(core == 0, dy[:HALF], dy[rows - HALF :])
    tabs = [tables[c] for c in range(8)]

    def block(bb, carry):
      for sub in range(2):
        b = bb * 2 + sub
        for half in range(0, BLOCK, HALF):
            here = pl.ds(pl.multiple_of(b * BLOCK + half, HALF), HALF)
            rows = slice(half, half + HALF)
            for start in range(0, cols, LANES):
                lanes = slice(start, start + LANES)
                mine = [cells[z, b, core, rows, lanes].astype(F32) for z in range(slices)]
                accum, transmit = nothing()
                for z in range(slices):
                    found = classify(mine[z], tabs)
                    if z in ends:
                        ref = last if z else first
                        for c in range(4):
                            ref[c, here, lanes] = found[c]
                    else:
                        accum, transmit = shade(
                            accum, transmit, mine[z + 1] - mine[z - 1],
                            inner_slope[z - 1, here, lanes], inner_norm[z - 1, here, lanes], found,
                        )
                for c in range(3):
                    middle[c, here, lanes] = accum[c]
                middle[3, here, lanes] = transmit
      return carry

    lax.fori_loop(0, blocks // 2, block, 0)


def relay_kernel(core_ref, own, other, outer, relayed, edge):
    slices, blocks, _, _, _ = own.shape
    core = core_ref[0]
    relayed[...] = outer[:, 1 - core]

    @pl.when(core == 0)
    def _():
        edge[:slices] = own[:, blocks - 1, 1, HALF:, :]
        edge[slices:] = other[:, blocks - 1, 1, HALF:, :]

    @pl.when(core != 0)
    def _():
        edge[:slices] = own[:, 0, 0, :HALF, :]
        edge[slices:] = other[:, 0, 0, :HALF, :]


def slab_kernel(
    core_ref, own, other, outer, relayed, edges, tables, scales, *refs
):
    own_terms, other_terms, out = refs[:7], refs[7:14], refs[14]
    slices, blocks, _, _, cols = own.shape
    core = core_ref[0]
    front = core == 0
    end = slices - 1
    opacity_scale = scales[2]

    def stacks(mine, theirs, end_own, end_other):
        own_stack = (
            [jnp.where(front, end_own, theirs[end])] + mine + [jnp.where(front, theirs[0], end_own)]
        )
        other_stack = (
            [jnp.where(front, mine[end], end_other)]
            + theirs
            + [jnp.where(front, end_other, mine[0])]
        )
        return own_stack, other_stack

    def finish(own_part, other_part):
        both = over(pick(front, own_part, other_part), pick(front, other_part, own_part))
        both[3] = (1.0 - both[3]) * opacity_scale
        return both

    def block(b, carry):
        for half in range(0, BLOCK, HALF):
            here = pl.ds(pl.multiple_of(b * BLOCK + half, HALF), HALF)
            rows = slice(half, half + HALF)
            for start in range(0, cols, LANES):
                lanes = slice(start, start + LANES)

                def half_slab(stack, terms):
                    first, last, middle, slope, norm = terms[:5]
                    parts = []
                    for ref, at, z in ((first, 0, 0), (last, 1, end)):
                        accum, transmit = shade(
                            *nothing(), stack[z + 2] - stack[z],
                            slope[at, here, lanes], norm[at, here, lanes],
                            [ref[c, here, lanes] for c in range(4)],
                        )
                        parts.append(accum + [transmit])
                    inner = [middle[c, here, lanes] for c in range(4)]
                    return over(parts[0], over(inner, parts[1]))

                own_stack, other_stack = stacks(
                    [own[z, b, core, rows, lanes].astype(F32) for z in range(slices)],
                    [other[z, b, core, rows, lanes].astype(F32) for z in range(slices)],
                    outer[b, core, rows, lanes].astype(F32),
                    relayed[b, rows, lanes].astype(F32),
                )
                both = finish(half_slab(own_stack, own_terms), half_slab(other_stack, other_terms))
                for c in range(4):
                    at = c * BLOCK + half
                    out[b, at : at + HALF, lanes] = both[c]
        return carry

    lax.fori_loop(0, blocks, block, 0)

    tabs = [tables[c] for c in range(8)]
    b = jnp.where(front, 0, blocks - 1)
    row = lax.broadcasted_iota(jnp.int32, (HALF, LANES), 0)
    at_edge = row == jnp.where(front, 0, HALF - 1)
    for start in range(0, cols, LANES):
        lanes = slice(start, start + LANES)

        def load(ref, *index):
            top = ref[(*index, slice(0, HALF), lanes)].astype(F32)
            return jnp.where(front, top, ref[(*index, slice(HALF, BLOCK), lanes)].astype(F32))

        def half_slab(stack, terms, at):
            accum, transmit = nothing()
            for z in range(slices):
                halo = edges[at + z, :, lanes].astype(F32)
                halo = jnp.where(front, -halo[HALF - 1 :], halo[0:1])
                dx = terms[5][z, :, lanes] + jnp.where(at_edge, halo, 0.0)
                dy = terms[6][z, :, lanes]
                accum, transmit = shade(
                    accum, transmit, stack[z + 2] - stack[z],
                    slope_of(dx, dy), norm_of(dx, dy), classify(stack[z + 1], tabs),
                )
            return accum + [transmit]

        own_stack, other_stack = stacks(
            [load(own, z, b, core) for z in range(slices)],
            [load(other, z, b, core) for z in range(slices)],
            load(outer, b, core),
            load(relayed, b),
        )
        both = finish(
            half_slab(own_stack, own_terms, 0), half_slab(other_stack, other_terms, slices)
        )
        for c in range(4):
            at = pl.multiple_of(c * BLOCK + core * HALF, HALF)
            out[b, pl.ds(at, HALF), lanes] = both[c]


def merge_kernel(parts, scales, out, image):
    cols = parts.shape[2]
    colour_scale, opacity_top = scales[0], scales[1]
    for half in range(0, BLOCK, HALF):
        for start in range(0, cols, LANES):
            lanes = slice(start, start + LANES)
            accum, transmit = nothing()
            for s in range(parts.shape[0]):
                part = [
                    parts[s, c * BLOCK + half : c * BLOCK + half + HALF, lanes] for c in range(4)
                ]
                accum = [a + transmit * p for a, p in zip(accum, part[:3])]
                transmit = transmit - transmit * (part[3] * opacity_top)
            whole = [a * colour_scale for a in accum] + [1.0 - transmit]
            for c in range(4):
                at = start // LANES, slice(c * BLOCK + half, c * BLOCK + half + HALF)
                image[at] = whole[c]
    for r in range(BLOCK):
        for start in range(0, cols, LANES):
            out[:, r * cols + start : r * cols + start + LANES] = image[
                start // LANES, pl.ds(r, 4, stride=BLOCK)
            ]


def shards(volume, transfer_table):
    slices, rows, cols = volume.shape
    depth_count = lax.axis_size("depth")
    img_count = lax.axis_size("img")
    chips = depth_count // 2
    depth_total = slices * depth_count
    blocks = rows // (2 * BLOCK)
    core = lax.axis_index("depth") % 2

    half = rows // 2
    split = (slices, blocks, 2, BLOCK, cols)
    core_arg = core.astype(jnp.int32).reshape(1)
    same_core = [[2 * j + c for j in range(chips)] for c in range(2)]
    vmem = pl.BlockSpec(memory_space=pltpu.MemorySpace.VMEM)
    smem = pl.BlockSpec(memory_space=pltpu.MemorySpace.SMEM)
    params = pltpu.CompilerParams(vmem_limit_bytes=16 << 20)
    quad = jax.ShapeDtypeStruct((4, half, cols), F32)
    two = jax.ShapeDtypeStruct((2, half, cols), F32)
    unit = jax.ShapeDtypeStruct((slices, HALF, cols), F32)
    plane = jax.ShapeDtypeStruct((blocks, BLOCK, cols), BF16)
    edge = jax.ShapeDtypeStruct((2 * slices, HALF, cols), BF16)
    terms = (quad, quad, quad, two, two, unit, unit)

    partner = [(d, d ^ 1) for d in range(depth_count)]
    own = volume.reshape(split)
    entries = transfer_table.shape[1]
    *ops, scales, outer = pl.pallas_call(
        functools.partial(
            prepare_kernel, slab_share=2.0 * slices / depth_total, depth_total=depth_total
        ),
        out_shape=(
            jax.ShapeDtypeStruct((half, rows), BF16),
            jax.ShapeDtypeStruct((cols, cols), BF16),
            jax.ShapeDtypeStruct((8, HALF, entries), F32),
            jax.ShapeDtypeStruct((3, HALF, LANES), F32),
            jax.ShapeDtypeStruct((rows, cols), BF16),
        ),
        in_specs=[smem, vmem, vmem],
        out_specs=(vmem,) * 5,
        compiler_params=params,
        name="prepare",
    )(core_arg, volume, transfer_table)
    outer = lax.ppermute(
        outer, "depth",
        [(d, d + 1) for d in range(1, depth_count - 1, 2)]
        + [(d + 1, d) for d in range(1, depth_count - 1, 2)],
    ).reshape(split[1:])
    held = lax.optimization_barrier((volume, scales))[0]
    other = lax.ppermute(held, "depth", partner).reshape(split)

    def slices_terms(cells, previous, name):
        return pl.pallas_call(
            slices_kernel,
            out_shape=terms,
            in_specs=[smem] + [vmem] * (4 + len(previous)),
            out_specs=(vmem,) * 7,
            scratch_shapes=[pltpu.VMEM((slices - 2, half, cols), F32)] * 2,
            compiler_params=params,
            name=name,
        )(core_arg, cells, *ops, *previous)

    own_terms = slices_terms(own, (), "own")
    outer, _ = lax.optimization_barrier((outer, own_terms[6]))
    relayed, edges = pl.pallas_call(
        relay_kernel,
        out_shape=(plane, edge),
        in_specs=[smem] + [vmem] * 3,
        out_specs=(vmem, vmem),
        compiler_params=params,
        name="relay",
    )(core_arg, own, other, outer)
    other_terms = slices_terms(other, (relayed,), "other")
    relayed = lax.ppermute(relayed, "depth", partner)
    edges = lax.ppermute(
        edges, ("img", "depth"),
        [
            (at * depth_count + d, to * depth_count + d)
            for i in range(img_count - 1)
            for d in range(depth_count)
            for at, to in [((i + 1, i) if d % 2 else (i, i + 1))]
        ],
    )
    partial_image = pl.pallas_call(
        slab_kernel,
        out_shape=jax.ShapeDtypeStruct((blocks, 4 * BLOCK, cols), F32),
        in_specs=[smem] + [vmem] * 21,
        out_specs=vmem,
        compiler_params=params,
        name="slab",
    )(
        core_arg, own, other, outer, relayed, edges, ops[2], scales, *own_terms, *other_terms,
    )
    pieces = lax.all_to_all(
        partial_image.astype(jnp.float16), "depth", split_axis=0, concat_axis=0, tiled=True,
        axis_index_groups=same_core,
    )
    return pl.pallas_call(
        merge_kernel,
        out_shape=jax.ShapeDtypeStruct((4, BLOCK * cols), F32),
        in_specs=[vmem, vmem],
        out_specs=vmem,
        scratch_shapes=[pltpu.VMEM((cols // LANES, 4 * BLOCK, LANES), F32)],
        compiler_params=params,
        name="merge",
    )(pieces.astype(F32), scales)


def solution(mesh):
    placed = (P("depth", "img", None), P())
    return jax.shard_map(
        shards, mesh=mesh, in_specs=placed, out_specs=P(None, ("img", "depth")), check_vma=False
    )
```

```python
import functools

import jax
import jax.numpy as jnp
import numpy as np
from jax import lax
from jax.experimental import pallas as pl
from jax.experimental.pallas import tpu as pltpu
from jax.sharding import PartitionSpec as P

F32 = jnp.float32
BF16 = jnp.bfloat16
BLOCK = 16
HALF = 8
LANES = 128
TINY = 1e-30
SLOPE = 1.4 / 3.0


def row_differences(rows, core):
    shape = (rows // 2, rows)
    local = lax.broadcasted_iota(jnp.int32, shape, 0)
    there = lax.broadcasted_iota(jnp.int32, shape, 1)
    step = there - (local + (local & -BLOCK) + core * BLOCK)
    return jnp.where(step == 1, 1.0, jnp.where(step == -1, -1.0, 0.0)).astype(BF16)


def column_differences(cols):
    step = lax.broadcasted_iota(jnp.int32, (cols, cols), 0) - lax.broadcasted_iota(
        jnp.int32, (cols, cols), 1
    )
    return jnp.where(step == 1, 1.0, jnp.where(step == -1, -1.0, 0.0)).astype(BF16)


def tops(table, slab_share):
    colour = jnp.max(jnp.max(table[0:3], axis=0, keepdims=True), axis=1, keepdims=True)
    extinction = jnp.max(table[3:4], axis=1, keepdims=True)
    return jnp.maximum(colour, TINY), jnp.maximum(extinction * slab_share, TINY)


def prepare_kernel(
    core_ref, volume, table_hbm, rows_op, cols_op, tables, scales, outer, table_ref, sems,
    *, slab_share, depth_total,
):
    outer_slice = (volume.shape[0] - 1) * core_ref[0]
    table_copy = pltpu.make_async_copy(table_hbm, table_ref, sems.at[0])
    outer_copy = pltpu.make_async_copy(volume.at[outer_slice], outer, sems.at[1])
    table_copy.start()
    outer_copy.start()
    rows_op[...] = row_differences(rows_op.shape[1], core_ref[0])
    cols_op[...] = column_differences(cols_op.shape[1])
    table_copy.wait()
    table = table_ref[...].astype(F32)
    entries = table.shape[1]
    colour_top, opacity_top = tops(table, slab_share)
    scale = SLOPE / (colour_top * opacity_top)
    last = lax.broadcasted_iota(jnp.int32, (HALF, entries), 1) == entries - 1
    for c in range(4):
        factor = scale if c < 3 else float(-np.log2(np.e) / depth_total)
        lower = jnp.broadcast_to(table[c : c + 1] * factor, (HALF, entries))
        tables[c] = lower
        tables[c + 4] = jnp.where(last, lower, pltpu.roll(lower, entries - 1, 1))
    for at, value in enumerate((colour_top * opacity_top, opacity_top, 1.0 / opacity_top)):
        scales[at] = jnp.broadcast_to(value, (HALF, LANES))
    outer_copy.wait()


def look_up(table, index):
    return jnp.take_along_axis(table, index, axis=1, mode="promise_in_bounds")


def classify(centre, tabs):
    position = centre * float(tabs[0].shape[1] - 1)
    knot = position.astype(jnp.int32)
    part = position - knot.astype(F32)
    upper = part.astype(BF16).astype(F32)
    lower = (1.0 - part).astype(BF16).astype(F32)
    values = [
        lower * look_up(tabs[c], knot) + upper * look_up(tabs[c + 4], knot) for c in range(4)
    ]
    return values[:3] + [jnp.exp2(values[3])]


def shade(accum, transmit, dz, slope_xy, norm_xy, found):
    shading = 0.3 / SLOPE + jnp.abs(dz + slope_xy) * lax.rsqrt(dz * dz + norm_xy)
    left = transmit * found[3]
    gain = (transmit - left) * shading
    return [a + gain * v for a, v in zip(accum, found[:3])], left


def slope_of(dx, dy):
    return 0.5 * dx + dy


def norm_of(dx, dy):
    return dx * dx + dy * dy + 0.04


def over(near, far):
    return [n + near[3] * f for n, f in zip(near[:3], far[:3])] + [near[3] * far[3]]


def nothing():
    return [jnp.zeros((HALF, LANES), F32)] * 3, jnp.ones((HALF, LANES), F32)


def pick(condition, a, b):
    return [jnp.where(condition, x, y) for x, y in zip(a, b)]


def own_kernel(core_ref, volume, rows_op, cols_op, tables, *refs):
    cells, sems = refs[7], refs[-1]
    copies = [
        pltpu.make_async_copy(volume.at[z], cells.at[z], sems.at[z]) for z in range(cells.shape[0])
    ]
    for copy in copies:
        copy.start()
    slices_kernel(core_ref, cells, rows_op, cols_op, tables, *refs[:7], *refs[8:10], copies=copies)


def slices_kernel(core_ref, cells, rows_op, cols_op, tables, *refs, copies=()):
    first, last, middle, slope, norm, edge_dx, edge_dy, inner_slope, inner_norm = refs[-9:]
    core = core_ref[0]
    slices, blocks, _, _, cols = cells.shape
    rows = blocks * BLOCK
    ends = (0, slices - 1)
    for z in range(slices):
        if copies:
            copies[z].wait()
        dx = jnp.dot(rows_op[...], cells[z].reshape(2 * rows, cols), preferred_element_type=F32)
        dy = jnp.dot(
            cells[z, :, core].reshape(rows, cols), cols_op[...], preferred_element_type=F32
        )
        to_slope, to_norm, at = (
            (slope, norm, ends.index(z)) if z in ends else (inner_slope, inner_norm, z - 1)
        )
        to_slope[at] = slope_of(dx, dy)
        to_norm[at] = norm_of(dx, dy)
        edge_dx[z] = jnp.where(core == 0, dx[:HALF], dx[rows - HALF :])
        edge_dy[z] = jnp.where(core == 0, dy[:HALF], dy[rows - HALF :])
    tabs = [tables[c] for c in range(8)]

    def block(bb, carry):
      for sub in range(2):
        b = bb * 2 + sub
        for half in range(0, BLOCK, HALF):
            here = pl.ds(pl.multiple_of(b * BLOCK + half, HALF), HALF)
            rows = slice(half, half + HALF)
            for start in range(0, cols, LANES):
                lanes = slice(start, start + LANES)
                mine = [cells[z, b, core, rows, lanes].astype(F32) for z in range(slices)]
                accum, transmit = nothing()
                for z in range(slices):
                    found = classify(mine[z], tabs)
                    if z in ends:
                        ref = last if z else first
                        for c in range(4):
                            ref[c, here, lanes] = found[c]
                    else:
                        accum, transmit = shade(
                            accum, transmit, mine[z + 1] - mine[z - 1],
                            inner_slope[z - 1, here, lanes], inner_norm[z - 1, here, lanes], found,
                        )
                for c in range(3):
                    middle[c, here, lanes] = accum[c]
                middle[3, here, lanes] = transmit
      return carry

    lax.fori_loop(0, blocks // 2, block, 0)


def relay_kernel(core_ref, own, other, outer, relayed, edge):
    slices, blocks, _, _, _ = own.shape
    core = core_ref[0]
    relayed[...] = outer[:, 1 - core]

    @pl.when(core == 0)
    def _():
        edge[:slices] = own[:, blocks - 1, 1, HALF:, :]
        edge[slices:] = other[:, blocks - 1, 1, HALF:, :]

    @pl.when(core != 0)
    def _():
        edge[:slices] = own[:, 0, 0, :HALF, :]
        edge[slices:] = other[:, 0, 0, :HALF, :]


def slab_kernel(
    core_ref, own, other, outer, relayed, edges, tables, scales, *refs
):
    own_terms, other_terms, out = refs[:7], refs[7:14], refs[14]
    slices, blocks, _, _, cols = own.shape
    core = core_ref[0]
    front = core == 0
    end = slices - 1
    opacity_scale = scales[2]

    def stacks(mine, theirs, end_own, end_other):
        own_stack = (
            [jnp.where(front, end_own, theirs[end])] + mine + [jnp.where(front, theirs[0], end_own)]
        )
        other_stack = (
            [jnp.where(front, mine[end], end_other)]
            + theirs
            + [jnp.where(front, end_other, mine[0])]
        )
        return own_stack, other_stack

    def finish(own_part, other_part):
        both = over(pick(front, own_part, other_part), pick(front, other_part, own_part))
        both[3] = (1.0 - both[3]) * opacity_scale
        return both

    def block(b, carry):
        for half in range(0, BLOCK, HALF):
            here = pl.ds(pl.multiple_of(b * BLOCK + half, HALF), HALF)
            rows = slice(half, half + HALF)
            for start in range(0, cols, LANES):
                lanes = slice(start, start + LANES)

                def half_slab(stack, terms):
                    first, last, middle, slope, norm = terms[:5]
                    parts = []
                    for ref, at, z in ((first, 0, 0), (last, 1, end)):
                        accum, transmit = shade(
                            *nothing(), stack[z + 2] - stack[z],
                            slope[at, here, lanes], norm[at, here, lanes],
                            [ref[c, here, lanes] for c in range(4)],
                        )
                        parts.append(accum + [transmit])
                    inner = [middle[c, here, lanes] for c in range(4)]
                    return over(parts[0], over(inner, parts[1]))

                own_stack, other_stack = stacks(
                    [own[z, b, core, rows, lanes].astype(F32) for z in range(slices)],
                    [other[z, b, core, rows, lanes].astype(F32) for z in range(slices)],
                    outer[b, core, rows, lanes].astype(F32),
                    relayed[b, rows, lanes].astype(F32),
                )
                both = finish(half_slab(own_stack, own_terms), half_slab(other_stack, other_terms))
                for c in range(4):
                    at = c * BLOCK + half
                    out[b, at : at + HALF, lanes] = both[c]
        return carry

    lax.fori_loop(0, blocks, block, 0)

    tabs = [tables[c] for c in range(8)]
    b = jnp.where(front, 0, blocks - 1)
    row = lax.broadcasted_iota(jnp.int32, (HALF, LANES), 0)
    at_edge = row == jnp.where(front, 0, HALF - 1)
    for start in range(0, cols, LANES):
        lanes = slice(start, start + LANES)

        def load(ref, *index):
            top = ref[(*index, slice(0, HALF), lanes)].astype(F32)
            return jnp.where(front, top, ref[(*index, slice(HALF, BLOCK), lanes)].astype(F32))

        def half_slab(stack, terms, at):
            accum, transmit = nothing()
            for z in range(slices):
                halo = edges[at + z, :, lanes].astype(F32)
                halo = jnp.where(front, -halo[HALF - 1 :], halo[0:1])
                dx = terms[5][z, :, lanes] + jnp.where(at_edge, halo, 0.0)
                dy = terms[6][z, :, lanes]
                accum, transmit = shade(
                    accum, transmit, stack[z + 2] - stack[z],
                    slope_of(dx, dy), norm_of(dx, dy), classify(stack[z + 1], tabs),
                )
            return accum + [transmit]

        own_stack, other_stack = stacks(
            [load(own, z, b, core) for z in range(slices)],
            [load(other, z, b, core) for z in range(slices)],
            load(outer, b, core),
            load(relayed, b),
        )
        both = finish(
            half_slab(own_stack, own_terms, 0), half_slab(other_stack, other_terms, slices)
        )
        for c in range(4):
            at = pl.multiple_of(c * BLOCK + core * HALF, HALF)
            out[b, pl.ds(at, HALF), lanes] = both[c]


def merge_kernel(parts, scales, out, image):
    cols = parts.shape[2]
    colour_scale, opacity_top = scales[0], scales[1]
    for half in range(0, BLOCK, HALF):
        for start in range(0, cols, LANES):
            lanes = slice(start, start + LANES)
            accum, transmit = nothing()
            for s in range(parts.shape[0]):
                part = [
                    parts[s, c * BLOCK + half : c * BLOCK + half + HALF, lanes] for c in range(4)
                ]
                accum = [a + transmit * p for a, p in zip(accum, part[:3])]
                transmit = transmit - transmit * (part[3] * opacity_top)
            whole = [a * colour_scale for a in accum] + [1.0 - transmit]
            for c in range(4):
                at = start // LANES, slice(c * BLOCK + half, c * BLOCK + half + HALF)
                image[at] = whole[c]
    for r in range(BLOCK):
        for start in range(0, cols, LANES):
            out[:, r * cols + start : r * cols + start + LANES] = image[
                start // LANES, pl.ds(r, 4, stride=BLOCK)
            ]


def shards(volume, transfer_table):
    slices, rows, cols = volume.shape
    depth_count = lax.axis_size("depth")
    img_count = lax.axis_size("img")
    chips = depth_count // 2
    depth_total = slices * depth_count
    blocks = rows // (2 * BLOCK)
    core = lax.axis_index("depth") % 2

    half = rows // 2
    split = (slices, blocks, 2, BLOCK, cols)
    core_arg = core.astype(jnp.int32).reshape(1)
    same_core = [[2 * j + c for j in range(chips)] for c in range(2)]
    vmem = pl.BlockSpec(memory_space=pltpu.MemorySpace.VMEM)
    hbm = pl.BlockSpec(memory_space=pltpu.MemorySpace.HBM)
    in_hbm = functools.partial(pltpu.with_memory_space_constraint, memory_space=pltpu.MemorySpace.HBM)
    smem = pl.BlockSpec(memory_space=pltpu.MemorySpace.SMEM)
    params = pltpu.CompilerParams(vmem_limit_bytes=16 << 20)
    quad = jax.ShapeDtypeStruct((4, half, cols), F32)
    two = jax.ShapeDtypeStruct((2, half, cols), F32)
    unit = jax.ShapeDtypeStruct((slices, HALF, cols), F32)
    plane = jax.ShapeDtypeStruct((blocks, BLOCK, cols), BF16)
    edge = jax.ShapeDtypeStruct((2 * slices, HALF, cols), BF16)
    terms = (quad, quad, quad, two, two, unit, unit)

    partner = [(d, d ^ 1) for d in range(depth_count)]
    entries = transfer_table.shape[1]
    *ops, scales, outer = pl.pallas_call(
        functools.partial(
            prepare_kernel, slab_share=2.0 * slices / depth_total, depth_total=depth_total
        ),
        out_shape=(
            jax.ShapeDtypeStruct((half, rows), BF16),
            jax.ShapeDtypeStruct((cols, cols), BF16),
            jax.ShapeDtypeStruct((8, HALF, entries), F32),
            jax.ShapeDtypeStruct((3, HALF, LANES), F32),
            jax.ShapeDtypeStruct((rows, cols), BF16),
        ),
        in_specs=[smem, hbm, hbm],
        out_specs=(vmem,) * 5,
        scratch_shapes=[
            pltpu.VMEM(transfer_table.shape, BF16), pltpu.SemaphoreType.DMA((2,)),
        ],
        compiler_params=params,
        name="prepare",
    )(
        core_arg, in_hbm(volume), in_hbm(transfer_table)
    )
    outer = lax.ppermute(
        outer, "depth",
        [(d, d + 1) for d in range(1, depth_count - 1, 2)]
        + [(d + 1, d) for d in range(1, depth_count - 1, 2)],
    ).reshape(split[1:])
    other = lax.ppermute(volume, "depth", partner).reshape(split)

    def slices_terms(cells, previous, name):
        return pl.pallas_call(
            slices_kernel,
            out_shape=terms,
            in_specs=[smem] + [vmem] * (4 + len(previous)),
            out_specs=(vmem,) * 7,
            scratch_shapes=[pltpu.VMEM((slices - 2, half, cols), F32)] * 2,
            compiler_params=params,
            name=name,
        )(core_arg, cells, *ops, *previous)

    *own_terms, own = pl.pallas_call(
        own_kernel,
        out_shape=(*terms, jax.ShapeDtypeStruct(split, BF16)),
        in_specs=[smem, hbm] + [vmem] * 3,
        out_specs=(vmem,) * 8,
        scratch_shapes=[pltpu.VMEM((slices - 2, half, cols), F32)] * 2
        + [pltpu.SemaphoreType.DMA((slices,))],
        compiler_params=params,
        name="own",
    )(core_arg, in_hbm(volume.reshape(split)), *ops)
    outer, _ = lax.optimization_barrier((outer, own_terms[6]))
    relayed, edges = pl.pallas_call(
        relay_kernel,
        out_shape=(plane, edge),
        in_specs=[smem] + [vmem] * 3,
        out_specs=(vmem, vmem),
        compiler_params=params,
        name="relay",
    )(core_arg, own, other, outer)
    other_terms = slices_terms(other, (relayed,), "other")
    relayed = lax.ppermute(relayed, "depth", partner)
    edges = lax.ppermute(
        edges, ("img", "depth"),
        [
            (at * depth_count + d, to * depth_count + d)
            for i in range(img_count - 1)
            for d in range(depth_count)
            for at, to in [((i + 1, i) if d % 2 else (i, i + 1))]
        ],
    )
    partial_image = pl.pallas_call(
        slab_kernel,
        out_shape=jax.ShapeDtypeStruct((blocks, 4 * BLOCK, cols), F32),
        in_specs=[smem] + [vmem] * 21,
        out_specs=vmem,
        compiler_params=params,
        name="slab",
    )(
        core_arg, own, other, outer, relayed, edges, ops[2], scales, *own_terms, *other_terms,
    )
    pieces = lax.all_to_all(
        partial_image.astype(jnp.float16), "depth", split_axis=0, concat_axis=0, tiled=True,
        axis_index_groups=same_core,
    )
    return pl.pallas_call(
        merge_kernel,
        out_shape=jax.ShapeDtypeStruct((4, BLOCK * cols), F32),
        in_specs=[vmem, vmem],
        out_specs=vmem,
        scratch_shapes=[pltpu.VMEM((cols // LANES, 4 * BLOCK, LANES), F32)],
        compiler_params=params,
        name="merge",
    )(pieces.astype(F32), scales)


def solution(mesh):
    placed = (P("depth", "img", None), P())
    return jax.shard_map(
        shards, mesh=mesh, in_specs=placed, out_specs=P(None, ("img", "depth")), check_vma=False
    )
```

```python
import functools

import jax
import jax.numpy as jnp
import numpy as np
from jax import lax
from jax.experimental import pallas as pl
from jax.experimental.pallas import tpu as pltpu
from jax.sharding import PartitionSpec as P

F32 = jnp.float32
BF16 = jnp.bfloat16
BLOCK = 16
HALF = 8
LANES = 128
TINY = 1e-30
SLOPE = 1.4 / 3.0


def row_differences(rows, core):
    shape = (rows // 2, rows)
    local = lax.broadcasted_iota(jnp.int32, shape, 0)
    there = lax.broadcasted_iota(jnp.int32, shape, 1)
    step = there - (local + (local & -BLOCK) + core * BLOCK)
    return jnp.where(step == 1, 1.0, jnp.where(step == -1, -1.0, 0.0)).astype(BF16)


def column_differences(cols):
    step = lax.broadcasted_iota(jnp.int32, (cols, cols), 0) - lax.broadcasted_iota(
        jnp.int32, (cols, cols), 1
    )
    return jnp.where(step == 1, 1.0, jnp.where(step == -1, -1.0, 0.0)).astype(BF16)


def tops(table, slab_share):
    colour = jnp.max(jnp.max(table[0:3], axis=0, keepdims=True), axis=1, keepdims=True)
    extinction = jnp.max(table[3:4], axis=1, keepdims=True)
    return jnp.maximum(colour, TINY), jnp.maximum(extinction * slab_share, TINY)


def prepare_kernel(
    core_ref, volume, table_hbm, rows_op, cols_op, tables, scales, outer, table_ref, sems,
    *, slab_share, depth_total,
):
    outer_slice = (volume.shape[0] - 1) * core_ref[0]
    table_copy = pltpu.make_async_copy(table_hbm, table_ref, sems.at[0])
    outer_copy = pltpu.make_async_copy(volume.at[outer_slice], outer, sems.at[1])
    table_copy.start()
    outer_copy.start()
    rows_op[...] = row_differences(rows_op.shape[1], core_ref[0])
    cols_op[...] = column_differences(cols_op.shape[1])
    table_copy.wait()
    table = table_ref[...].astype(F32)
    entries = table.shape[1]
    colour_top, opacity_top = tops(table, slab_share)
    scale = SLOPE / (colour_top * opacity_top)
    last = lax.broadcasted_iota(jnp.int32, (HALF, entries), 1) == entries - 1
    for c in range(4):
        factor = scale if c < 3 else float(-np.log2(np.e) / depth_total)
        lower = jnp.broadcast_to(table[c : c + 1] * factor, (HALF, entries))
        tables[c] = lower
        tables[c + 4] = jnp.where(last, lower, pltpu.roll(lower, entries - 1, 1))
    for at, value in enumerate((colour_top * opacity_top, opacity_top, 1.0 / opacity_top)):
        scales[at] = jnp.broadcast_to(value, (HALF, LANES))
    outer_copy.wait()


def look_up(table, index):
    return jnp.take_along_axis(table, index, axis=1, mode="promise_in_bounds")


def classify(centre, tabs):
    position = centre * float(tabs[0].shape[1] - 1)
    knot = position.astype(jnp.int32)
    part = position - knot.astype(F32)
    upper = part.astype(BF16).astype(F32)
    lower = (1.0 - part).astype(BF16).astype(F32)
    values = [
        lower * look_up(tabs[c], knot) + upper * look_up(tabs[c + 4], knot) for c in range(4)
    ]
    return values[:3] + [jnp.exp2(values[3])]


def shade(accum, transmit, dz, slope_xy, norm_xy, found):
    shading = 0.3 / SLOPE + jnp.abs(dz + slope_xy) * lax.rsqrt(dz * dz + norm_xy)
    left = transmit * found[3]
    gain = (transmit - left) * shading
    return [a + gain * v for a, v in zip(accum, found[:3])], left


def slope_of(dx, dy):
    return 0.5 * dx + dy


def norm_of(dx, dy):
    return dx * dx + dy * dy + 0.04


def over(near, far):
    return [n + near[3] * f for n, f in zip(near[:3], far[:3])] + [near[3] * far[3]]


def nothing():
    return [jnp.zeros((HALF, LANES), F32)] * 3, jnp.ones((HALF, LANES), F32)


def pick(condition, a, b):
    return [jnp.where(condition, x, y) for x, y in zip(a, b)]


def each_block(blocks, unroll, body):
    def step(at, carry):
        for sub in range(unroll):
            body(at * unroll + sub)
        return carry

    lax.fori_loop(0, blocks // unroll, step, 0)


def each_unit(cols):
    for half in range(0, BLOCK, HALF):
        for start in range(0, cols, LANES):
            yield half, slice(half, half + HALF), slice(start, start + LANES)


def keep(ref, centre, tabs, here, lanes):
    for c, value in enumerate(classify(centre, tabs)):
        ref[c, here, lanes] = value


def own_kernel(core_ref, volume, rows_op, cols_op, tables, *refs):
    first, cells, sems = refs[0], refs[7], refs[-1]
    slices, blocks, _, _, cols = cells.shape
    copies = [
        pltpu.make_async_copy(volume.at[z], cells.at[z], sems.at[z]) for z in range(slices)
    ]
    for copy in copies:
        copy.start()
    copies[0].wait()
    tabs = [tables[c] for c in range(8)]

    def look_up_first(b):
        for half, rows, lanes in each_unit(cols):
            here = pl.ds(pl.multiple_of(b * BLOCK + half, HALF), HALF)
            keep(first, cells[0, b, core_ref[0], rows, lanes].astype(F32), tabs, here, lanes)

    each_block(blocks, 4, look_up_first)
    for copy in copies[1:]:
        copy.wait()
    later_slices(core_ref, cells, rows_op, cols_op, tables, *refs[:7], *refs[8:10], first_done=True)


def slices_kernel(*refs):
    later_slices(*refs[:5], *refs[-9:], first_done=False)


def later_slices(
    core_ref, cells, rows_op, cols_op, tables,
    first, last, middle, slope, norm, edge_dx, edge_dy, inner_slope, inner_norm, *, first_done,
):
    core = core_ref[0]
    slices, blocks, _, _, cols = cells.shape
    rows = blocks * BLOCK
    end = slices - 1
    for z in range(slices):
        dx = jnp.dot(rows_op[...], cells[z].reshape(2 * rows, cols), preferred_element_type=F32)
        dy = jnp.dot(
            cells[z, :, core].reshape(rows, cols), cols_op[...], preferred_element_type=F32
        )
        to_slope, to_norm, at = (
            (slope, norm, z // end) if z in (0, end) else (inner_slope, inner_norm, z - 1)
        )
        to_slope[at] = slope_of(dx, dy)
        to_norm[at] = norm_of(dx, dy)
        edge_dx[z] = jnp.where(core == 0, dx[:HALF], dx[rows - HALF :])
        edge_dy[z] = jnp.where(core == 0, dy[:HALF], dy[rows - HALF :])
    tabs = [tables[c] for c in range(8)]

    def block(b):
        for half, rows, lanes in each_unit(cols):
            here = pl.ds(pl.multiple_of(b * BLOCK + half, HALF), HALF)
            mine = [cells[z, b, core, rows, lanes].astype(F32) for z in range(slices)]
            if not first_done:
                keep(first, mine[0], tabs, here, lanes)
            accum, transmit = nothing()
            for z in range(1, end):
                accum, transmit = shade(
                    accum, transmit, mine[z + 1] - mine[z - 1],
                    inner_slope[z - 1, here, lanes], inner_norm[z - 1, here, lanes],
                    classify(mine[z], tabs),
                )
            keep(last, mine[end], tabs, here, lanes)
            for c, value in enumerate(accum + [transmit]):
                middle[c, here, lanes] = value

    each_block(blocks, 2, block)


def relay_kernel(core_ref, own, other, outer, relayed, edge):
    slices, blocks, _, _, _ = own.shape
    core = core_ref[0]
    relayed[...] = outer[:, 1 - core]

    @pl.when(core == 0)
    def _():
        edge[:slices] = own[:, blocks - 1, 1, HALF:, :]
        edge[slices:] = other[:, blocks - 1, 1, HALF:, :]

    @pl.when(core != 0)
    def _():
        edge[:slices] = own[:, 0, 0, :HALF, :]
        edge[slices:] = other[:, 0, 0, :HALF, :]


def slab_kernel(
    core_ref, own, other, outer, relayed, edges, tables, scales, *refs
):
    own_terms, other_terms, out = refs[:7], refs[7:14], refs[14]
    slices, blocks, _, _, cols = own.shape
    core = core_ref[0]
    front = core == 0
    end = slices - 1
    opacity_scale = scales[2]

    def stacks(mine, theirs, end_own, end_other):
        own_stack = (
            [jnp.where(front, end_own, theirs[end])] + mine + [jnp.where(front, theirs[0], end_own)]
        )
        other_stack = (
            [jnp.where(front, mine[end], end_other)]
            + theirs
            + [jnp.where(front, end_other, mine[0])]
        )
        return own_stack, other_stack

    def finish(own_part, other_part):
        both = over(pick(front, own_part, other_part), pick(front, other_part, own_part))
        both[3] = (1.0 - both[3]) * opacity_scale
        return both

    def block(b):
        for half, rows, lanes in each_unit(cols):
            here = pl.ds(pl.multiple_of(b * BLOCK + half, HALF), HALF)

            def half_slab(stack, terms):
                first, last, middle, slope, norm = terms[:5]
                parts = []
                for ref, at, z in ((first, 0, 0), (last, 1, end)):
                    accum, transmit = shade(
                        *nothing(), stack[z + 2] - stack[z],
                        slope[at, here, lanes], norm[at, here, lanes],
                        [ref[c, here, lanes] for c in range(4)],
                    )
                    parts.append(accum + [transmit])
                inner = [middle[c, here, lanes] for c in range(4)]
                return over(parts[0], over(inner, parts[1]))

            own_stack, other_stack = stacks(
                [own[z, b, core, rows, lanes].astype(F32) for z in range(slices)],
                [other[z, b, core, rows, lanes].astype(F32) for z in range(slices)],
                outer[b, core, rows, lanes].astype(F32),
                relayed[b, rows, lanes].astype(F32),
            )
            both = finish(half_slab(own_stack, own_terms), half_slab(other_stack, other_terms))
            for c in range(4):
                at = c * BLOCK + half
                out[b, at : at + HALF, lanes] = both[c]

    each_block(blocks, 2, block)

    tabs = [tables[c] for c in range(8)]
    b = jnp.where(front, 0, blocks - 1)
    row = lax.broadcasted_iota(jnp.int32, (HALF, LANES), 0)
    at_edge = row == jnp.where(front, 0, HALF - 1)
    for start in range(0, cols, LANES):
        lanes = slice(start, start + LANES)

        def load(ref, *index):
            top = ref[(*index, slice(0, HALF), lanes)].astype(F32)
            return jnp.where(front, top, ref[(*index, slice(HALF, BLOCK), lanes)].astype(F32))

        def half_slab(stack, terms, at):
            accum, transmit = nothing()
            for z in range(slices):
                halo = edges[at + z, :, lanes].astype(F32)
                halo = jnp.where(front, -halo[HALF - 1 :], halo[0:1])
                dx = terms[5][z, :, lanes] + jnp.where(at_edge, halo, 0.0)
                dy = terms[6][z, :, lanes]
                accum, transmit = shade(
                    accum, transmit, stack[z + 2] - stack[z],
                    slope_of(dx, dy), norm_of(dx, dy), classify(stack[z + 1], tabs),
                )
            return accum + [transmit]

        own_stack, other_stack = stacks(
            [load(own, z, b, core) for z in range(slices)],
            [load(other, z, b, core) for z in range(slices)],
            load(outer, b, core),
            load(relayed, b),
        )
        both = finish(
            half_slab(own_stack, own_terms, 0), half_slab(other_stack, other_terms, slices)
        )
        for c in range(4):
            at = pl.multiple_of(c * BLOCK + core * HALF, HALF)
            out[b, pl.ds(at, HALF), lanes] = both[c]


def merge_kernel(parts, scales, out, image):
    cols = parts.shape[2]
    colour_scale, opacity_top = scales[0], scales[1]
    for half in range(0, BLOCK, HALF):
        for start in range(0, cols, LANES):
            lanes = slice(start, start + LANES)
            accum, transmit = nothing()
            for s in range(parts.shape[0]):
                part = [
                    parts[s, c * BLOCK + half : c * BLOCK + half + HALF, lanes] for c in range(4)
                ]
                accum = [a + transmit * p for a, p in zip(accum, part[:3])]
                transmit = transmit - transmit * (part[3] * opacity_top)
            whole = [a * colour_scale for a in accum] + [1.0 - transmit]
            for c in range(4):
                at = start // LANES, slice(c * BLOCK + half, c * BLOCK + half + HALF)
                image[at] = whole[c]
    for r in range(BLOCK):
        for start in range(0, cols, LANES):
            out[:, r * cols + start : r * cols + start + LANES] = image[
                start // LANES, pl.ds(r, 4, stride=BLOCK)
            ]


def shards(volume, transfer_table):
    slices, rows, cols = volume.shape
    depth_count = lax.axis_size("depth")
    img_count = lax.axis_size("img")
    chips = depth_count // 2
    depth_total = slices * depth_count
    blocks = rows // (2 * BLOCK)
    core = lax.axis_index("depth") % 2

    half = rows // 2
    split = (slices, blocks, 2, BLOCK, cols)
    core_arg = core.astype(jnp.int32).reshape(1)
    same_core = [[2 * j + c for j in range(chips)] for c in range(2)]
    vmem = pl.BlockSpec(memory_space=pltpu.MemorySpace.VMEM)
    hbm = pl.BlockSpec(memory_space=pltpu.MemorySpace.HBM)
    in_hbm = functools.partial(pltpu.with_memory_space_constraint, memory_space=pltpu.MemorySpace.HBM)
    smem = pl.BlockSpec(memory_space=pltpu.MemorySpace.SMEM)
    params = pltpu.CompilerParams(vmem_limit_bytes=16 << 20)
    quad = jax.ShapeDtypeStruct((4, half, cols), F32)
    two = jax.ShapeDtypeStruct((2, half, cols), F32)
    unit = jax.ShapeDtypeStruct((slices, HALF, cols), F32)
    plane = jax.ShapeDtypeStruct((blocks, BLOCK, cols), BF16)
    edge = jax.ShapeDtypeStruct((2 * slices, HALF, cols), BF16)
    terms = (quad, quad, quad, two, two, unit, unit)

    partner = [(d, d ^ 1) for d in range(depth_count)]
    entries = transfer_table.shape[1]
    *ops, scales, outer = pl.pallas_call(
        functools.partial(
            prepare_kernel, slab_share=2.0 * slices / depth_total, depth_total=depth_total
        ),
        out_shape=(
            jax.ShapeDtypeStruct((half, rows), BF16),
            jax.ShapeDtypeStruct((cols, cols), BF16),
            jax.ShapeDtypeStruct((8, HALF, entries), F32),
            jax.ShapeDtypeStruct((3, HALF, LANES), F32),
            jax.ShapeDtypeStruct((rows, cols), BF16),
        ),
        in_specs=[smem, hbm, hbm],
        out_specs=(vmem,) * 5,
        scratch_shapes=[
            pltpu.VMEM(transfer_table.shape, BF16), pltpu.SemaphoreType.DMA((2,)),
        ],
        compiler_params=params,
        name="prepare",
    )(
        core_arg, in_hbm(volume), in_hbm(transfer_table)
    )
    outer = lax.ppermute(
        outer, "depth",
        [(d, d + 1) for d in range(1, depth_count - 1, 2)]
        + [(d + 1, d) for d in range(1, depth_count - 1, 2)],
    ).reshape(split[1:])
    other = lax.ppermute(volume, "depth", partner).reshape(split)

    def slices_terms(cells, previous, name):
        return pl.pallas_call(
            slices_kernel,
            out_shape=terms,
            in_specs=[smem] + [vmem] * (4 + len(previous)),
            out_specs=(vmem,) * 7,
            scratch_shapes=[pltpu.VMEM((slices - 2, half, cols), F32)] * 2,
            compiler_params=params,
            name=name,
        )(core_arg, cells, *ops, *previous)

    *own_terms, own = pl.pallas_call(
        own_kernel,
        out_shape=(*terms, jax.ShapeDtypeStruct(split, BF16)),
        in_specs=[smem, hbm] + [vmem] * 3,
        out_specs=(vmem,) * 8,
        scratch_shapes=[pltpu.VMEM((slices - 2, half, cols), F32)] * 2
        + [pltpu.SemaphoreType.DMA((slices,))],
        compiler_params=params,
        name="own",
    )(core_arg, in_hbm(volume.reshape(split)), *ops)
    outer, _ = lax.optimization_barrier((outer, own_terms[6]))
    relayed, edges = pl.pallas_call(
        relay_kernel,
        out_shape=(plane, edge),
        in_specs=[smem] + [vmem] * 3,
        out_specs=(vmem, vmem),
        compiler_params=params,
        name="relay",
    )(core_arg, own, other, outer)
    other_terms = slices_terms(other, (relayed,), "other")
    relayed = lax.ppermute(relayed, "depth", partner)
    edges = lax.ppermute(
        edges, ("img", "depth"),
        [
            (at * depth_count + d, to * depth_count + d)
            for i in range(img_count - 1)
            for d in range(depth_count)
            for at, to in [((i + 1, i) if d % 2 else (i, i + 1))]
        ],
    )
    partial_image = pl.pallas_call(
        slab_kernel,
        out_shape=jax.ShapeDtypeStruct((blocks, 4 * BLOCK, cols), F32),
        in_specs=[smem] + [vmem] * 21,
        out_specs=vmem,
        compiler_params=params,
        name="slab",
    )(
        core_arg, own, other, outer, relayed, edges, ops[2], scales, *own_terms, *other_terms,
    )
    pieces = lax.all_to_all(
        partial_image.astype(jnp.float16), "depth", split_axis=0, concat_axis=0, tiled=True,
        axis_index_groups=same_core,
    )
    return pl.pallas_call(
        merge_kernel,
        out_shape=jax.ShapeDtypeStruct((4, BLOCK * cols), F32),
        in_specs=[vmem, vmem],
        out_specs=vmem,
        scratch_shapes=[pltpu.VMEM((cols // LANES, 4 * BLOCK, LANES), F32)],
        compiler_params=params,
        name="merge",
    )(pieces.astype(F32), scales)


def solution(mesh):
    placed = (P("depth", "img", None), P())
    return jax.shard_map(
        shards, mesh=mesh, in_specs=placed, out_specs=P(None, ("img", "depth")), check_vma=False
    )
```

```python
import functools

import jax
import jax.numpy as jnp
import numpy as np
from jax import lax
from jax.experimental import pallas as pl
from jax.experimental.pallas import tpu as pltpu
from jax.sharding import PartitionSpec as P

F32 = jnp.float32
BF16 = jnp.bfloat16
BLOCK = 16
HALF = 8
LANES = 128
TINY = 1e-30
SLOPE = 1.4 / 3.0


def row_differences(rows, core):
    shape = (rows // 2, rows)
    local = lax.broadcasted_iota(jnp.int32, shape, 0)
    there = lax.broadcasted_iota(jnp.int32, shape, 1)
    step = there - (local + (local & -BLOCK) + core * BLOCK)
    return jnp.where(step == 1, 1.0, jnp.where(step == -1, -1.0, 0.0)).astype(BF16)


def column_differences(cols):
    step = lax.broadcasted_iota(jnp.int32, (cols, cols), 0) - lax.broadcasted_iota(
        jnp.int32, (cols, cols), 1
    )
    return jnp.where(step == 1, 1.0, jnp.where(step == -1, -1.0, 0.0)).astype(BF16)


def tops(table, slab_share):
    colour = jnp.max(jnp.max(table[0:3], axis=0, keepdims=True), axis=1, keepdims=True)
    extinction = jnp.max(table[3:4], axis=1, keepdims=True)
    return jnp.maximum(colour, TINY), jnp.maximum(extinction * slab_share, TINY)


def prepare_kernel(
    core_ref, volume, table_hbm, rows_op, cols_op, tables, scales, outer, table_ref, sems,
    *, slab_share, depth_total,
):
    outer_slice = (volume.shape[0] - 1) * core_ref[0]
    table_copy = pltpu.make_async_copy(table_hbm, table_ref, sems.at[0])
    outer_copy = pltpu.make_async_copy(volume.at[outer_slice], outer, sems.at[1])
    table_copy.start()
    outer_copy.start()
    rows_op[...] = row_differences(rows_op.shape[1], core_ref[0])
    cols_op[...] = column_differences(cols_op.shape[1])
    table_copy.wait()
    table = table_ref[...].astype(F32)
    entries = table.shape[1]
    colour_top, opacity_top = tops(table, slab_share)
    scale = SLOPE / (colour_top * opacity_top)
    last = lax.broadcasted_iota(jnp.int32, (HALF, entries), 1) == entries - 1
    for c in range(4):
        factor = scale if c < 3 else float(-np.log2(np.e) / depth_total)
        lower = jnp.broadcast_to(table[c : c + 1] * factor, (HALF, entries))
        tables[c] = lower
        tables[c + 4] = jnp.where(last, lower, pltpu.roll(lower, entries - 1, 1))
    for at, value in enumerate((colour_top * opacity_top, opacity_top, 1.0 / opacity_top)):
        scales[at] = jnp.broadcast_to(value, (HALF, LANES))
    outer_copy.wait()


def look_up(table, index):
    return jnp.take_along_axis(table, index, axis=1, mode="promise_in_bounds")


def classify(centre, tabs):
    position = centre * float(tabs[0].shape[1] - 1)
    knot = position.astype(jnp.int32)
    part = position - knot.astype(F32)
    upper = part.astype(BF16).astype(F32)
    lower = (1.0 - part).astype(BF16).astype(F32)
    values = [
        lower * look_up(tabs[c], knot) + upper * look_up(tabs[c + 4], knot) for c in range(4)
    ]
    return values[:3] + [jnp.exp2(values[3])]


def shade(accum, transmit, dz, slope_xy, norm_xy, found):
    shading = 0.3 / SLOPE + jnp.abs(dz + slope_xy) * lax.rsqrt(dz * dz + norm_xy)
    left = transmit * found[3]
    gain = (transmit - left) * shading
    return [a + gain * v for a, v in zip(accum, found[:3])], left


def slope_of(dx, dy):
    return 0.5 * dx + dy


def norm_of(dx, dy):
    return dx * dx + dy * dy + 0.04


def over(near, far):
    return [n + near[3] * f for n, f in zip(near[:3], far[:3])] + [near[3] * far[3]]


def nothing():
    return [jnp.zeros((HALF, LANES), F32)] * 3, jnp.ones((HALF, LANES), F32)


def pick(condition, a, b):
    return [jnp.where(condition, x, y) for x, y in zip(a, b)]


def each_block(blocks, unroll, body):
    def step(at, carry):
        for sub in range(unroll):
            body(at * unroll + sub)
        return carry

    lax.fori_loop(0, blocks // unroll, step, 0)


def each_unit(cols):
    for half in range(0, BLOCK, HALF):
        for start in range(0, cols, LANES):
            yield half, slice(half, half + HALF), slice(start, start + LANES)


def keep(ref, centre, tabs, here, lanes):
    for c, value in enumerate(classify(centre, tabs)):
        ref[c, here, lanes] = value


def own_kernel(core_ref, volume, rows_op, cols_op, tables, *refs):
    first, cells, sems = refs[0], refs[7], refs[-1]
    slices, blocks, _, _, cols = cells.shape
    copies = [
        pltpu.make_async_copy(volume.at[z], cells.at[z], sems.at[z]) for z in range(slices)
    ]
    copies[0].start()
    copies[0].wait()
    for copy in copies[1:]:
        copy.start()
    tabs = [tables[c] for c in range(8)]

    def look_up_first(b):
        for half, rows, lanes in each_unit(cols):
            here = pl.ds(pl.multiple_of(b * BLOCK + half, HALF), HALF)
            keep(first, cells[0, b, core_ref[0], rows, lanes].astype(F32), tabs, here, lanes)

    each_block(blocks, 4, look_up_first)
    for copy in copies[1:]:
        copy.wait()
    later_slices(core_ref, cells, rows_op, cols_op, tables, *refs[:7], *refs[8:10], first_done=True)


def slices_kernel(*refs):
    later_slices(*refs[:5], *refs[-9:], first_done=False)


def later_slices(
    core_ref, cells, rows_op, cols_op, tables,
    first, last, middle, slope, norm, edge_dx, edge_dy, inner_slope, inner_norm, *, first_done,
):
    core = core_ref[0]
    slices, blocks, _, _, cols = cells.shape
    rows = blocks * BLOCK
    end = slices - 1
    for z in range(slices):
        dx = jnp.dot(rows_op[...], cells[z].reshape(2 * rows, cols), preferred_element_type=F32)
        dy = jnp.dot(
            cells[z, :, core].reshape(rows, cols), cols_op[...], preferred_element_type=F32
        )
        to_slope, to_norm, at = (
            (slope, norm, z // end) if z in (0, end) else (inner_slope, inner_norm, z - 1)
        )
        to_slope[at] = slope_of(dx, dy)
        to_norm[at] = norm_of(dx, dy)
        edge_dx[z] = jnp.where(core == 0, dx[:HALF], dx[rows - HALF :])
        edge_dy[z] = jnp.where(core == 0, dy[:HALF], dy[rows - HALF :])
    tabs = [tables[c] for c in range(8)]

    def block(b):
        for half, rows, lanes in each_unit(cols):
            here = pl.ds(pl.multiple_of(b * BLOCK + half, HALF), HALF)
            mine = [cells[z, b, core, rows, lanes].astype(F32) for z in range(slices)]
            if not first_done:
                keep(first, mine[0], tabs, here, lanes)
            accum, transmit = nothing()
            for z in range(1, end):
                accum, transmit = shade(
                    accum, transmit, mine[z + 1] - mine[z - 1],
                    inner_slope[z - 1, here, lanes], inner_norm[z - 1, here, lanes],
                    classify(mine[z], tabs),
                )
            keep(last, mine[end], tabs, here, lanes)
            for c, value in enumerate(accum + [transmit]):
                middle[c, here, lanes] = value

    each_block(blocks, 2, block)


def relay_kernel(core_ref, own, other, outer, relayed, edge):
    slices, blocks, _, _, _ = own.shape
    core = core_ref[0]
    relayed[...] = outer[:, 1 - core]

    @pl.when(core == 0)
    def _():
        edge[:slices] = own[:, blocks - 1, 1, HALF:, :]
        edge[slices:] = other[:, blocks - 1, 1, HALF:, :]

    @pl.when(core != 0)
    def _():
        edge[:slices] = own[:, 0, 0, :HALF, :]
        edge[slices:] = other[:, 0, 0, :HALF, :]


def slab_kernel(
    core_ref, own, other, outer, relayed, edges, tables, scales, *refs
):
    own_terms, other_terms, out = refs[:7], refs[7:14], refs[14]
    slices, blocks, _, _, cols = own.shape
    core = core_ref[0]
    front = core == 0
    end = slices - 1
    opacity_scale = scales[2]

    def stacks(mine, theirs, end_own, end_other):
        own_stack = (
            [jnp.where(front, end_own, theirs[end])] + mine + [jnp.where(front, theirs[0], end_own)]
        )
        other_stack = (
            [jnp.where(front, mine[end], end_other)]
            + theirs
            + [jnp.where(front, end_other, mine[0])]
        )
        return own_stack, other_stack

    def finish(own_part, other_part):
        both = over(pick(front, own_part, other_part), pick(front, other_part, own_part))
        both[3] = (1.0 - both[3]) * opacity_scale
        return both

    def block(b):
        for half, rows, lanes in each_unit(cols):
            here = pl.ds(pl.multiple_of(b * BLOCK + half, HALF), HALF)

            def half_slab(stack, terms):
                first, last, middle, slope, norm = terms[:5]
                parts = []
                for ref, at, z in ((first, 0, 0), (last, 1, end)):
                    accum, transmit = shade(
                        *nothing(), stack[z + 2] - stack[z],
                        slope[at, here, lanes], norm[at, here, lanes],
                        [ref[c, here, lanes] for c in range(4)],
                    )
                    parts.append(accum + [transmit])
                inner = [middle[c, here, lanes] for c in range(4)]
                return over(parts[0], over(inner, parts[1]))

            own_stack, other_stack = stacks(
                [own[z, b, core, rows, lanes].astype(F32) for z in range(slices)],
                [other[z, b, core, rows, lanes].astype(F32) for z in range(slices)],
                outer[b, core, rows, lanes].astype(F32),
                relayed[b, rows, lanes].astype(F32),
            )
            both = finish(half_slab(own_stack, own_terms), half_slab(other_stack, other_terms))
            for c in range(4):
                at = c * BLOCK + half
                out[b, at : at + HALF, lanes] = both[c]

    each_block(blocks, 2, block)

    tabs = [tables[c] for c in range(8)]
    b = jnp.where(front, 0, blocks - 1)
    row = lax.broadcasted_iota(jnp.int32, (HALF, LANES), 0)
    at_edge = row == jnp.where(front, 0, HALF - 1)
    for start in range(0, cols, LANES):
        lanes = slice(start, start + LANES)

        def load(ref, *index):
            top = ref[(*index, slice(0, HALF), lanes)].astype(F32)
            return jnp.where(front, top, ref[(*index, slice(HALF, BLOCK), lanes)].astype(F32))

        def half_slab(stack, terms, at):
            accum, transmit = nothing()
            for z in range(slices):
                halo = edges[at + z, :, lanes].astype(F32)
                halo = jnp.where(front, -halo[HALF - 1 :], halo[0:1])
                dx = terms[5][z, :, lanes] + jnp.where(at_edge, halo, 0.0)
                dy = terms[6][z, :, lanes]
                accum, transmit = shade(
                    accum, transmit, stack[z + 2] - stack[z],
                    slope_of(dx, dy), norm_of(dx, dy), classify(stack[z + 1], tabs),
                )
            return accum + [transmit]

        own_stack, other_stack = stacks(
            [load(own, z, b, core) for z in range(slices)],
            [load(other, z, b, core) for z in range(slices)],
            load(outer, b, core),
            load(relayed, b),
        )
        both = finish(
            half_slab(own_stack, own_terms, 0), half_slab(other_stack, other_terms, slices)
        )
        for c in range(4):
            at = pl.multiple_of(c * BLOCK + core * HALF, HALF)
            out[b, pl.ds(at, HALF), lanes] = both[c]


def merge_kernel(parts, scales, out, image):
    cols = parts.shape[2]
    colour_scale, opacity_top = scales[0], scales[1]
    for half in range(0, BLOCK, HALF):
        for start in range(0, cols, LANES):
            lanes = slice(start, start + LANES)
            accum, transmit = nothing()
            for s in range(parts.shape[0]):
                part = [
                    parts[s, c * BLOCK + half : c * BLOCK + half + HALF, lanes] for c in range(4)
                ]
                accum = [a + transmit * p for a, p in zip(accum, part[:3])]
                transmit = transmit - transmit * (part[3] * opacity_top)
            whole = [a * colour_scale for a in accum] + [1.0 - transmit]
            for c in range(4):
                at = start // LANES, slice(c * BLOCK + half, c * BLOCK + half + HALF)
                image[at] = whole[c]
    for r in range(BLOCK):
        for start in range(0, cols, LANES):
            out[:, r * cols + start : r * cols + start + LANES] = image[
                start // LANES, pl.ds(r, 4, stride=BLOCK)
            ]


def shards(volume, transfer_table):
    slices, rows, cols = volume.shape
    depth_count = lax.axis_size("depth")
    img_count = lax.axis_size("img")
    chips = depth_count // 2
    depth_total = slices * depth_count
    blocks = rows // (2 * BLOCK)
    core = lax.axis_index("depth") % 2

    half = rows // 2
    split = (slices, blocks, 2, BLOCK, cols)
    core_arg = core.astype(jnp.int32).reshape(1)
    same_core = [[2 * j + c for j in range(chips)] for c in range(2)]
    vmem = pl.BlockSpec(memory_space=pltpu.MemorySpace.VMEM)
    hbm = pl.BlockSpec(memory_space=pltpu.MemorySpace.HBM)
    in_hbm = functools.partial(pltpu.with_memory_space_constraint, memory_space=pltpu.MemorySpace.HBM)
    smem = pl.BlockSpec(memory_space=pltpu.MemorySpace.SMEM)
    params = pltpu.CompilerParams(vmem_limit_bytes=16 << 20)
    quad = jax.ShapeDtypeStruct((4, half, cols), F32)
    two = jax.ShapeDtypeStruct((2, half, cols), F32)
    unit = jax.ShapeDtypeStruct((slices, HALF, cols), F32)
    plane = jax.ShapeDtypeStruct((blocks, BLOCK, cols), BF16)
    edge = jax.ShapeDtypeStruct((2 * slices, HALF, cols), BF16)
    terms = (quad, quad, quad, two, two, unit, unit)

    partner = [(d, d ^ 1) for d in range(depth_count)]
    entries = transfer_table.shape[1]
    *ops, scales, outer = pl.pallas_call(
        functools.partial(
            prepare_kernel, slab_share=2.0 * slices / depth_total, depth_total=depth_total
        ),
        out_shape=(
            jax.ShapeDtypeStruct((half, rows), BF16),
            jax.ShapeDtypeStruct((cols, cols), BF16),
            jax.ShapeDtypeStruct((8, HALF, entries), F32),
            jax.ShapeDtypeStruct((3, HALF, LANES), F32),
            jax.ShapeDtypeStruct((rows, cols), BF16),
        ),
        in_specs=[smem, hbm, hbm],
        out_specs=(vmem,) * 5,
        scratch_shapes=[
            pltpu.VMEM(transfer_table.shape, BF16), pltpu.SemaphoreType.DMA((2,)),
        ],
        compiler_params=params,
        name="prepare",
    )(
        core_arg, in_hbm(volume), in_hbm(transfer_table)
    )
    outer = lax.ppermute(
        outer, "depth",
        [(d, d + 1) for d in range(1, depth_count - 1, 2)]
        + [(d + 1, d) for d in range(1, depth_count - 1, 2)],
    ).reshape(split[1:])
    other = lax.ppermute(volume, "depth", partner).reshape(split)

    def slices_terms(cells, previous, name):
        return pl.pallas_call(
            slices_kernel,
            out_shape=terms,
            in_specs=[smem] + [vmem] * (4 + len(previous)),
            out_specs=(vmem,) * 7,
            scratch_shapes=[pltpu.VMEM((slices - 2, half, cols), F32)] * 2,
            compiler_params=params,
            name=name,
        )(core_arg, cells, *ops, *previous)

    *own_terms, own = pl.pallas_call(
        own_kernel,
        out_shape=(*terms, jax.ShapeDtypeStruct(split, BF16)),
        in_specs=[smem, hbm] + [vmem] * 3,
        out_specs=(vmem,) * 8,
        scratch_shapes=[pltpu.VMEM((slices - 2, half, cols), F32)] * 2
        + [pltpu.SemaphoreType.DMA((slices,))],
        compiler_params=params,
        name="own",
    )(core_arg, in_hbm(volume.reshape(split)), *ops)
    outer, _ = lax.optimization_barrier((outer, own_terms[6]))
    relayed, edges = pl.pallas_call(
        relay_kernel,
        out_shape=(plane, edge),
        in_specs=[smem] + [vmem] * 3,
        out_specs=(vmem, vmem),
        compiler_params=params,
        name="relay",
    )(core_arg, own, other, outer)
    other_terms = slices_terms(other, (relayed,), "other")
    relayed = lax.ppermute(relayed, "depth", partner)
    edges = lax.ppermute(
        edges, ("img", "depth"),
        [
            (at * depth_count + d, to * depth_count + d)
            for i in range(img_count - 1)
            for d in range(depth_count)
            for at, to in [((i + 1, i) if d % 2 else (i, i + 1))]
        ],
    )
    partial_image = pl.pallas_call(
        slab_kernel,
        out_shape=jax.ShapeDtypeStruct((blocks, 4 * BLOCK, cols), F32),
        in_specs=[smem] + [vmem] * 21,
        out_specs=vmem,
        compiler_params=params,
        name="slab",
    )(
        core_arg, own, other, outer, relayed, edges, ops[2], scales, *own_terms, *other_terms,
    )
    pieces = lax.all_to_all(
        partial_image.astype(jnp.float16), "depth", split_axis=0, concat_axis=0, tiled=True,
        axis_index_groups=same_core,
    )
    return pl.pallas_call(
        merge_kernel,
        out_shape=jax.ShapeDtypeStruct((4, BLOCK * cols), F32),
        in_specs=[vmem, vmem],
        out_specs=vmem,
        scratch_shapes=[pltpu.VMEM((cols // LANES, 4 * BLOCK, LANES), F32)],
        compiler_params=params,
        name="merge",
    )(pieces.astype(F32), scales)


def solution(mesh):
    placed = (P("depth", "img", None), P())
    return jax.shard_map(
        shards, mesh=mesh, in_specs=placed, out_specs=P(None, ("img", "depth")), check_vma=False
    )
```

```python
import functools

import jax
import jax.numpy as jnp
import numpy as np
from jax import lax
from jax.experimental import pallas as pl
from jax.experimental.pallas import tpu as pltpu
from jax.sharding import PartitionSpec as P

F32 = jnp.float32
BF16 = jnp.bfloat16
BLOCK = 16
HALF = 8
LANES = 128
TINY = 1e-30
SLOPE = 1.4 / 3.0


def row_differences(rows, core):
    shape = (rows // 2, rows)
    local = lax.broadcasted_iota(jnp.int32, shape, 0)
    there = lax.broadcasted_iota(jnp.int32, shape, 1)
    step = there - (local + (local & -BLOCK) + core * BLOCK)
    return jnp.where(step == 1, 1.0, jnp.where(step == -1, -1.0, 0.0)).astype(BF16)


def column_differences(cols):
    step = lax.broadcasted_iota(jnp.int32, (cols, cols), 0) - lax.broadcasted_iota(
        jnp.int32, (cols, cols), 1
    )
    return jnp.where(step == 1, 1.0, jnp.where(step == -1, -1.0, 0.0)).astype(BF16)


def tops(table, slab_share):
    colour = jnp.max(jnp.max(table[0:3], axis=0, keepdims=True), axis=1, keepdims=True)
    extinction = jnp.max(table[3:4], axis=1, keepdims=True)
    return jnp.maximum(colour, TINY), jnp.maximum(extinction * slab_share, TINY)


def prepare_kernel(
    core_ref, volume, table_hbm, rows_op, cols_op, tables, scales, outer, cells, table_ref, sems,
    *, slab_share, depth_total,
):
    slices = volume.shape[0]
    table_copy = pltpu.make_async_copy(table_hbm, table_ref, sems.at[slices])
    copies = [pltpu.make_async_copy(volume.at[z], cells.at[z], sems.at[z]) for z in range(slices)]
    table_copy.start()
    for copy in copies:
        copy.start()
    rows_op[...] = row_differences(rows_op.shape[1], core_ref[0])
    cols_op[...] = column_differences(cols_op.shape[1])
    table_copy.wait()
    table = table_ref[...].astype(F32)
    entries = table.shape[1]
    colour_top, opacity_top = tops(table, slab_share)
    scale = SLOPE / (colour_top * opacity_top)
    last = lax.broadcasted_iota(jnp.int32, (HALF, entries), 1) == entries - 1
    for c in range(4):
        factor = scale if c < 3 else float(-np.log2(np.e) / depth_total)
        lower = jnp.broadcast_to(table[c : c + 1] * factor, (HALF, entries))
        tables[c] = lower
        tables[c + 4] = jnp.where(last, lower, pltpu.roll(lower, entries - 1, 1))
    for at, value in enumerate((colour_top * opacity_top, opacity_top, 1.0 / opacity_top)):
        scales[at] = jnp.broadcast_to(value, (HALF, LANES))
    for copy in copies:
        copy.wait()
    outer[...] = cells[(slices - 1) * core_ref[0]]


def look_up(table, index):
    return jnp.take_along_axis(table, index, axis=1, mode="promise_in_bounds")


def classify(centre, tabs):
    position = centre * float(tabs[0].shape[1] - 1)
    knot = position.astype(jnp.int32)
    part = position - knot.astype(F32)
    upper = part.astype(BF16).astype(F32)
    lower = (1.0 - part).astype(BF16).astype(F32)
    values = [
        lower * look_up(tabs[c], knot) + upper * look_up(tabs[c + 4], knot) for c in range(4)
    ]
    return values[:3] + [jnp.exp2(values[3])]


def shade(accum, transmit, dz, slope_xy, norm_xy, found):
    shading = 0.3 / SLOPE + jnp.abs(dz + slope_xy) * lax.rsqrt(dz * dz + norm_xy)
    left = transmit * found[3]
    gain = (transmit - left) * shading
    return [a + gain * v for a, v in zip(accum, found[:3])], left


def slope_of(dx, dy):
    return 0.5 * dx + dy


def norm_of(dx, dy):
    return dx * dx + dy * dy + 0.04


def over(near, far):
    return [n + near[3] * f for n, f in zip(near[:3], far[:3])] + [near[3] * far[3]]


def nothing():
    return [jnp.zeros((HALF, LANES), F32)] * 3, jnp.ones((HALF, LANES), F32)


def pick(condition, a, b):
    return [jnp.where(condition, x, y) for x, y in zip(a, b)]


def each_block(blocks, unroll, body):
    def step(at, carry):
        for sub in range(unroll):
            body(at * unroll + sub)
        return carry

    lax.fori_loop(0, blocks // unroll, step, 0)


def each_unit(cols):
    for half in range(0, BLOCK, HALF):
        for start in range(0, cols, LANES):
            yield half, slice(half, half + HALF), slice(start, start + LANES)


def keep(ref, centre, tabs, here, lanes):
    for c, value in enumerate(classify(centre, tabs)):
        ref[c, here, lanes] = value


def slices_kernel(
    core_ref, cells, rows_op, cols_op, tables, *refs
):
    first, last, middle, slope, norm, edge_dx, edge_dy, inner_slope, inner_norm = refs[-9:]
    core = core_ref[0]
    slices, blocks, _, _, cols = cells.shape
    rows = blocks * BLOCK
    end = slices - 1
    for z in range(slices):
        dx = jnp.dot(rows_op[...], cells[z].reshape(2 * rows, cols), preferred_element_type=F32)
        dy = jnp.dot(
            cells[z, :, core].reshape(rows, cols), cols_op[...], preferred_element_type=F32
        )
        to_slope, to_norm, at = (
            (slope, norm, z // end) if z in (0, end) else (inner_slope, inner_norm, z - 1)
        )
        to_slope[at] = slope_of(dx, dy)
        to_norm[at] = norm_of(dx, dy)
        edge_dx[z] = jnp.where(core == 0, dx[:HALF], dx[rows - HALF :])
        edge_dy[z] = jnp.where(core == 0, dy[:HALF], dy[rows - HALF :])
    tabs = [tables[c] for c in range(8)]

    def block(b):
        for half, rows, lanes in each_unit(cols):
            here = pl.ds(pl.multiple_of(b * BLOCK + half, HALF), HALF)
            mine = [cells[z, b, core, rows, lanes].astype(F32) for z in range(slices)]
            keep(first, mine[0], tabs, here, lanes)
            accum, transmit = nothing()
            for z in range(1, end):
                accum, transmit = shade(
                    accum, transmit, mine[z + 1] - mine[z - 1],
                    inner_slope[z - 1, here, lanes], inner_norm[z - 1, here, lanes],
                    classify(mine[z], tabs),
                )
            keep(last, mine[end], tabs, here, lanes)
            for c, value in enumerate(accum + [transmit]):
                middle[c, here, lanes] = value

    each_block(blocks, 4, block)


def relay_kernel(core_ref, own, other, outer, relayed, edge):
    slices, blocks, _, _, _ = own.shape
    core = core_ref[0]
    relayed[...] = outer[:, 1 - core]

    @pl.when(core == 0)
    def _():
        edge[:slices] = own[:, blocks - 1, 1, HALF:, :]
        edge[slices:] = other[:, blocks - 1, 1, HALF:, :]

    @pl.when(core != 0)
    def _():
        edge[:slices] = own[:, 0, 0, :HALF, :]
        edge[slices:] = other[:, 0, 0, :HALF, :]


def slab_kernel(
    core_ref, own, other, outer, relayed, edges, tables, scales, *refs
):
    own_terms, other_terms, out = refs[:7], refs[7:14], refs[14]
    slices, blocks, _, _, cols = own.shape
    core = core_ref[0]
    front = core == 0
    end = slices - 1
    opacity_scale = scales[2]

    def stacks(mine, theirs, end_own, end_other):
        own_stack = (
            [jnp.where(front, end_own, theirs[end])] + mine + [jnp.where(front, theirs[0], end_own)]
        )
        other_stack = (
            [jnp.where(front, mine[end], end_other)]
            + theirs
            + [jnp.where(front, end_other, mine[0])]
        )
        return own_stack, other_stack

    def finish(own_part, other_part):
        both = over(pick(front, own_part, other_part), pick(front, other_part, own_part))
        both[3] = (1.0 - both[3]) * opacity_scale
        return both

    def block(b):
        for half, rows, lanes in each_unit(cols):
            here = pl.ds(pl.multiple_of(b * BLOCK + half, HALF), HALF)

            def half_slab(stack, terms):
                first, last, middle, slope, norm = terms[:5]
                parts = []
                for ref, at, z in ((first, 0, 0), (last, 1, end)):
                    accum, transmit = shade(
                        *nothing(), stack[z + 2] - stack[z],
                        slope[at, here, lanes], norm[at, here, lanes],
                        [ref[c, here, lanes] for c in range(4)],
                    )
                    parts.append(accum + [transmit])
                inner = [middle[c, here, lanes] for c in range(4)]
                return over(parts[0], over(inner, parts[1]))

            own_stack, other_stack = stacks(
                [own[z, b, core, rows, lanes].astype(F32) for z in range(slices)],
                [other[z, b, core, rows, lanes].astype(F32) for z in range(slices)],
                outer[b, core, rows, lanes].astype(F32),
                relayed[b, rows, lanes].astype(F32),
            )
            both = finish(half_slab(own_stack, own_terms), half_slab(other_stack, other_terms))
            for c in range(4):
                at = c * BLOCK + half
                out[b, at : at + HALF, lanes] = both[c]

    each_block(blocks, 2, block)

    tabs = [tables[c] for c in range(8)]
    b = jnp.where(front, 0, blocks - 1)
    row = lax.broadcasted_iota(jnp.int32, (HALF, LANES), 0)
    at_edge = row == jnp.where(front, 0, HALF - 1)
    for start in range(0, cols, LANES):
        lanes = slice(start, start + LANES)

        def load(ref, *index):
            top = ref[(*index, slice(0, HALF), lanes)].astype(F32)
            return jnp.where(front, top, ref[(*index, slice(HALF, BLOCK), lanes)].astype(F32))

        def half_slab(stack, terms, at):
            accum, transmit = nothing()
            for z in range(slices):
                halo = edges[at + z, :, lanes].astype(F32)
                halo = jnp.where(front, -halo[HALF - 1 :], halo[0:1])
                dx = terms[5][z, :, lanes] + jnp.where(at_edge, halo, 0.0)
                dy = terms[6][z, :, lanes]
                accum, transmit = shade(
                    accum, transmit, stack[z + 2] - stack[z],
                    slope_of(dx, dy), norm_of(dx, dy), classify(stack[z + 1], tabs),
                )
            return accum + [transmit]

        own_stack, other_stack = stacks(
            [load(own, z, b, core) for z in range(slices)],
            [load(other, z, b, core) for z in range(slices)],
            load(outer, b, core),
            load(relayed, b),
        )
        both = finish(
            half_slab(own_stack, own_terms, 0), half_slab(other_stack, other_terms, slices)
        )
        for c in range(4):
            at = pl.multiple_of(c * BLOCK + core * HALF, HALF)
            out[b, pl.ds(at, HALF), lanes] = both[c]


def merge_kernel(parts, scales, out, image):
    cols = parts.shape[2]
    colour_scale, opacity_top = scales[0], scales[1]
    for half in range(0, BLOCK, HALF):
        for start in range(0, cols, LANES):
            lanes = slice(start, start + LANES)
            accum, transmit = nothing()
            for s in range(parts.shape[0]):
                part = [
                    parts[s, c * BLOCK + half : c * BLOCK + half + HALF, lanes] for c in range(4)
                ]
                accum = [a + transmit * p for a, p in zip(accum, part[:3])]
                transmit = transmit - transmit * (part[3] * opacity_top)
            whole = [a * colour_scale for a in accum] + [1.0 - transmit]
            for c in range(4):
                at = start // LANES, slice(c * BLOCK + half, c * BLOCK + half + HALF)
                image[at] = whole[c]
    for r in range(BLOCK):
        for start in range(0, cols, LANES):
            out[:, r * cols + start : r * cols + start + LANES] = image[
                start // LANES, pl.ds(r, 4, stride=BLOCK)
            ]


def shards(volume, transfer_table):
    slices, rows, cols = volume.shape
    depth_count = lax.axis_size("depth")
    img_count = lax.axis_size("img")
    chips = depth_count // 2
    depth_total = slices * depth_count
    blocks = rows // (2 * BLOCK)
    core = lax.axis_index("depth") % 2

    half = rows // 2
    split = (slices, blocks, 2, BLOCK, cols)
    core_arg = core.astype(jnp.int32).reshape(1)
    same_core = [[2 * j + c for j in range(chips)] for c in range(2)]
    vmem = pl.BlockSpec(memory_space=pltpu.MemorySpace.VMEM)
    hbm = pl.BlockSpec(memory_space=pltpu.MemorySpace.HBM)
    in_hbm = functools.partial(pltpu.with_memory_space_constraint, memory_space=pltpu.MemorySpace.HBM)
    smem = pl.BlockSpec(memory_space=pltpu.MemorySpace.SMEM)
    params = pltpu.CompilerParams(vmem_limit_bytes=16 << 20)
    quad = jax.ShapeDtypeStruct((4, half, cols), F32)
    two = jax.ShapeDtypeStruct((2, half, cols), F32)
    unit = jax.ShapeDtypeStruct((slices, HALF, cols), F32)
    plane = jax.ShapeDtypeStruct((blocks, BLOCK, cols), BF16)
    edge = jax.ShapeDtypeStruct((2 * slices, HALF, cols), BF16)
    terms = (quad, quad, quad, two, two, unit, unit)

    partner = [(d, d ^ 1) for d in range(depth_count)]
    entries = transfer_table.shape[1]
    *ops, scales, outer, own = pl.pallas_call(
        functools.partial(
            prepare_kernel, slab_share=2.0 * slices / depth_total, depth_total=depth_total
        ),
        out_shape=(
            jax.ShapeDtypeStruct((half, rows), BF16),
            jax.ShapeDtypeStruct((cols, cols), BF16),
            jax.ShapeDtypeStruct((8, HALF, entries), F32),
            jax.ShapeDtypeStruct((3, HALF, LANES), F32),
            jax.ShapeDtypeStruct((rows, cols), BF16),
            jax.ShapeDtypeStruct(volume.shape, BF16),
        ),
        in_specs=[smem, hbm, hbm],
        out_specs=(vmem,) * 6,
        scratch_shapes=[
            pltpu.VMEM(transfer_table.shape, BF16), pltpu.SemaphoreType.DMA((slices + 1,)),
        ],
        compiler_params=params,
        name="prepare",
    )(
        core_arg, in_hbm(volume), in_hbm(transfer_table)
    )
    outer = lax.ppermute(
        outer, "depth",
        [(d, d + 1) for d in range(1, depth_count - 1, 2)]
        + [(d + 1, d) for d in range(1, depth_count - 1, 2)],
    ).reshape(split[1:])
    other = lax.ppermute(volume, "depth", partner).reshape(split)

    def slices_terms(cells, previous, name):
        return pl.pallas_call(
            slices_kernel,
            out_shape=terms,
            in_specs=[smem] + [vmem] * (4 + len(previous)),
            out_specs=(vmem,) * 7,
            scratch_shapes=[pltpu.VMEM((slices - 2, half, cols), F32)] * 2,
            compiler_params=params,
            name=name,
        )(core_arg, cells, *ops, *previous)

    own = own.reshape(split)
    own_terms = slices_terms(own, (), "own")
    outer, _ = lax.optimization_barrier((outer, own_terms[6]))
    relayed, edges = pl.pallas_call(
        relay_kernel,
        out_shape=(plane, edge),
        in_specs=[smem] + [vmem] * 3,
        out_specs=(vmem, vmem),
        compiler_params=params,
        name="relay",
    )(core_arg, own, other, outer)
    other_terms = slices_terms(other, (relayed,), "other")
    relayed = lax.ppermute(relayed, "depth", partner)
    edges = lax.ppermute(
        edges, ("img", "depth"),
        [
            (at * depth_count + d, to * depth_count + d)
            for i in range(img_count - 1)
            for d in range(depth_count)
            for at, to in [((i + 1, i) if d % 2 else (i, i + 1))]
        ],
    )
    partial_image = pl.pallas_call(
        slab_kernel,
        out_shape=jax.ShapeDtypeStruct((blocks, 4 * BLOCK, cols), F32),
        in_specs=[smem] + [vmem] * 21,
        out_specs=vmem,
        compiler_params=params,
        name="slab",
    )(
        core_arg, own, other, outer, relayed, edges, ops[2], scales, *own_terms, *other_terms,
    )
    pieces = lax.all_to_all(
        partial_image.astype(jnp.float16), "depth", split_axis=0, concat_axis=0, tiled=True,
        axis_index_groups=same_core,
    )
    return pl.pallas_call(
        merge_kernel,
        out_shape=jax.ShapeDtypeStruct((4, BLOCK * cols), F32),
        in_specs=[vmem, vmem],
        out_specs=vmem,
        scratch_shapes=[pltpu.VMEM((cols // LANES, 4 * BLOCK, LANES), F32)],
        compiler_params=params,
        name="merge",
    )(pieces.astype(F32), scales)


def solution(mesh):
    placed = (P("depth", "img", None), P())
    return jax.shard_map(
        shards, mesh=mesh, in_specs=placed, out_specs=P(None, ("img", "depth")), check_vma=False
    )
```

```python
import functools

import jax
import jax.numpy as jnp
import numpy as np
from jax import lax
from jax.experimental import pallas as pl
from jax.experimental.pallas import tpu as pltpu
from jax.sharding import PartitionSpec as P

F32 = jnp.float32
BF16 = jnp.bfloat16
BLOCK = 16
HALF = 8
LANES = 128
TINY = 1e-30
SLOPE = 1.4 / 3.0


def row_differences(rows, core):
    shape = (rows // 2, rows)
    local = lax.broadcasted_iota(jnp.int32, shape, 0)
    there = lax.broadcasted_iota(jnp.int32, shape, 1)
    step = there - (local + (local & -BLOCK) + core * BLOCK)
    return jnp.where(step == 1, 1.0, jnp.where(step == -1, -1.0, 0.0)).astype(BF16)


def column_differences(cols):
    step = lax.broadcasted_iota(jnp.int32, (cols, cols), 0) - lax.broadcasted_iota(
        jnp.int32, (cols, cols), 1
    )
    return jnp.where(step == 1, 1.0, jnp.where(step == -1, -1.0, 0.0)).astype(BF16)


def tops(table, slab_share):
    colour = jnp.max(jnp.max(table[0:3], axis=0, keepdims=True), axis=1, keepdims=True)
    extinction = jnp.max(table[3:4], axis=1, keepdims=True)
    return jnp.maximum(colour, TINY), jnp.maximum(extinction * slab_share, TINY)


def plane_kernel(core_ref, volume, outer, sem):
    at = (volume.shape[0] - 1) * core_ref[0]
    copy = pltpu.make_async_copy(volume.at[at], outer, sem.at[0])
    copy.start()
    copy.wait()


def prepare_kernel(
    core_ref, volume, table_hbm, _, rows_op, cols_op, tables, scales, cells, table_ref, sems,
    *, slab_share, depth_total,
):
    slices = volume.shape[0]
    table_copy = pltpu.make_async_copy(table_hbm, table_ref, sems.at[slices])
    copies = [pltpu.make_async_copy(volume.at[z], cells.at[z], sems.at[z]) for z in range(slices)]
    table_copy.start()
    for copy in copies:
        copy.start()
    rows_op[...] = row_differences(rows_op.shape[1], core_ref[0])
    cols_op[...] = column_differences(cols_op.shape[1])
    table_copy.wait()
    table = table_ref[...].astype(F32)
    entries = table.shape[1]
    colour_top, opacity_top = tops(table, slab_share)
    scale = SLOPE / (colour_top * opacity_top)
    last = lax.broadcasted_iota(jnp.int32, (HALF, entries), 1) == entries - 1
    for c in range(4):
        factor = scale if c < 3 else float(-np.log2(np.e) / depth_total)
        lower = jnp.broadcast_to(table[c : c + 1] * factor, (HALF, entries))
        tables[c] = lower
        tables[c + 4] = jnp.where(last, lower, pltpu.roll(lower, entries - 1, 1))
    for at, value in enumerate((colour_top * opacity_top, opacity_top, 1.0 / opacity_top)):
        scales[at] = jnp.broadcast_to(value, (HALF, LANES))
    for copy in copies:
        copy.wait()


def look_up(table, index):
    return jnp.take_along_axis(table, index, axis=1, mode="promise_in_bounds")


def classify(centre, tabs):
    position = centre * float(tabs[0].shape[1] - 1)
    knot = position.astype(jnp.int32)
    part = position - knot.astype(F32)
    upper = part.astype(BF16).astype(F32)
    lower = (1.0 - part).astype(BF16).astype(F32)
    values = [
        lower * look_up(tabs[c], knot) + upper * look_up(tabs[c + 4], knot) for c in range(4)
    ]
    return values[:3] + [jnp.exp2(values[3])]


def shade(accum, transmit, dz, slope_xy, norm_xy, found):
    shading = 0.3 / SLOPE + jnp.abs(dz + slope_xy) * lax.rsqrt(dz * dz + norm_xy)
    left = transmit * found[3]
    gain = (transmit - left) * shading
    return [a + gain * v for a, v in zip(accum, found[:3])], left


def slope_of(dx, dy):
    return 0.5 * dx + dy


def norm_of(dx, dy):
    return dx * dx + dy * dy + 0.04


def over(near, far):
    return [n + near[3] * f for n, f in zip(near[:3], far[:3])] + [near[3] * far[3]]


def nothing():
    return [jnp.zeros((HALF, LANES), F32)] * 3, jnp.ones((HALF, LANES), F32)


def pick(condition, a, b):
    return [jnp.where(condition, x, y) for x, y in zip(a, b)]


def each_block(blocks, unroll, body):
    def step(at, carry):
        for sub in range(unroll):
            body(at * unroll + sub)
        return carry

    lax.fori_loop(0, blocks // unroll, step, 0)


def each_unit(cols):
    for half in range(0, BLOCK, HALF):
        for start in range(0, cols, LANES):
            yield half, slice(half, half + HALF), slice(start, start + LANES)


def keep(ref, centre, tabs, here, lanes):
    for c, value in enumerate(classify(centre, tabs)):
        ref[c, here, lanes] = value


def slices_kernel(
    core_ref, cells, rows_op, cols_op, tables, *refs
):
    first, last, middle, slope, norm, edge_dx, edge_dy, inner_slope, inner_norm = refs[-9:]
    core = core_ref[0]
    slices, blocks, _, _, cols = cells.shape
    rows = blocks * BLOCK
    end = slices - 1
    for z in range(slices):
        dx = jnp.dot(rows_op[...], cells[z].reshape(2 * rows, cols), preferred_element_type=F32)
        dy = jnp.dot(
            cells[z, :, core].reshape(rows, cols), cols_op[...], preferred_element_type=F32
        )
        to_slope, to_norm, at = (
            (slope, norm, z // end) if z in (0, end) else (inner_slope, inner_norm, z - 1)
        )
        to_slope[at] = slope_of(dx, dy)
        to_norm[at] = norm_of(dx, dy)
        edge_dx[z] = jnp.where(core == 0, dx[:HALF], dx[rows - HALF :])
        edge_dy[z] = jnp.where(core == 0, dy[:HALF], dy[rows - HALF :])
    tabs = [tables[c] for c in range(8)]

    def block(b):
        for half, rows, lanes in each_unit(cols):
            here = pl.ds(pl.multiple_of(b * BLOCK + half, HALF), HALF)
            mine = [cells[z, b, core, rows, lanes].astype(F32) for z in range(slices)]
            keep(first, mine[0], tabs, here, lanes)
            accum, transmit = nothing()
            for z in range(1, end):
                accum, transmit = shade(
                    accum, transmit, mine[z + 1] - mine[z - 1],
                    inner_slope[z - 1, here, lanes], inner_norm[z - 1, here, lanes],
                    classify(mine[z], tabs),
                )
            keep(last, mine[end], tabs, here, lanes)
            for c, value in enumerate(accum + [transmit]):
                middle[c, here, lanes] = value

    each_block(blocks, 4, block)


def relay_kernel(core_ref, own, other, outer, relayed, edge):
    slices, blocks, _, _, _ = own.shape
    core = core_ref[0]
    relayed[...] = outer[:, 1 - core]

    @pl.when(core == 0)
    def _():
        edge[:slices] = own[:, blocks - 1, 1, HALF:, :]
        edge[slices:] = other[:, blocks - 1, 1, HALF:, :]

    @pl.when(core != 0)
    def _():
        edge[:slices] = own[:, 0, 0, :HALF, :]
        edge[slices:] = other[:, 0, 0, :HALF, :]


def slab_kernel(
    core_ref, own, other, outer, relayed, edges, tables, scales, *refs
):
    own_terms, other_terms, out = refs[:7], refs[7:14], refs[14]
    slices, blocks, _, _, cols = own.shape
    core = core_ref[0]
    front = core == 0
    end = slices - 1
    opacity_scale = scales[2]

    def stacks(mine, theirs, end_own, end_other):
        own_stack = (
            [jnp.where(front, end_own, theirs[end])] + mine + [jnp.where(front, theirs[0], end_own)]
        )
        other_stack = (
            [jnp.where(front, mine[end], end_other)]
            + theirs
            + [jnp.where(front, end_other, mine[0])]
        )
        return own_stack, other_stack

    def finish(own_part, other_part):
        both = over(pick(front, own_part, other_part), pick(front, other_part, own_part))
        both[3] = (1.0 - both[3]) * opacity_scale
        return both

    def block(b):
        for half, rows, lanes in each_unit(cols):
            here = pl.ds(pl.multiple_of(b * BLOCK + half, HALF), HALF)

            def half_slab(stack, terms):
                first, last, middle, slope, norm = terms[:5]
                parts = []
                for ref, at, z in ((first, 0, 0), (last, 1, end)):
                    accum, transmit = shade(
                        *nothing(), stack[z + 2] - stack[z],
                        slope[at, here, lanes], norm[at, here, lanes],
                        [ref[c, here, lanes] for c in range(4)],
                    )
                    parts.append(accum + [transmit])
                inner = [middle[c, here, lanes] for c in range(4)]
                return over(parts[0], over(inner, parts[1]))

            own_stack, other_stack = stacks(
                [own[z, b, core, rows, lanes].astype(F32) for z in range(slices)],
                [other[z, b, core, rows, lanes].astype(F32) for z in range(slices)],
                outer[b, core, rows, lanes].astype(F32),
                relayed[b, rows, lanes].astype(F32),
            )
            both = finish(half_slab(own_stack, own_terms), half_slab(other_stack, other_terms))
            for c in range(4):
                at = c * BLOCK + half
                out[b, at : at + HALF, lanes] = both[c]

    each_block(blocks, 2, block)

    tabs = [tables[c] for c in range(8)]
    b = jnp.where(front, 0, blocks - 1)
    row = lax.broadcasted_iota(jnp.int32, (HALF, LANES), 0)
    at_edge = row == jnp.where(front, 0, HALF - 1)
    for start in range(0, cols, LANES):
        lanes = slice(start, start + LANES)

        def load(ref, *index):
            top = ref[(*index, slice(0, HALF), lanes)].astype(F32)
            return jnp.where(front, top, ref[(*index, slice(HALF, BLOCK), lanes)].astype(F32))

        def half_slab(stack, terms, at):
            accum, transmit = nothing()
            for z in range(slices):
                halo = edges[at + z, :, lanes].astype(F32)
                halo = jnp.where(front, -halo[HALF - 1 :], halo[0:1])
                dx = terms[5][z, :, lanes] + jnp.where(at_edge, halo, 0.0)
                dy = terms[6][z, :, lanes]
                accum, transmit = shade(
                    accum, transmit, stack[z + 2] - stack[z],
                    slope_of(dx, dy), norm_of(dx, dy), classify(stack[z + 1], tabs),
                )
            return accum + [transmit]

        own_stack, other_stack = stacks(
            [load(own, z, b, core) for z in range(slices)],
            [load(other, z, b, core) for z in range(slices)],
            load(outer, b, core),
            load(relayed, b),
        )
        both = finish(
            half_slab(own_stack, own_terms, 0), half_slab(other_stack, other_terms, slices)
        )
        for c in range(4):
            at = pl.multiple_of(c * BLOCK + core * HALF, HALF)
            out[b, pl.ds(at, HALF), lanes] = both[c]


def merge_kernel(parts, scales, out, image):
    cols = parts.shape[2]
    colour_scale, opacity_top = scales[0], scales[1]
    for half in range(0, BLOCK, HALF):
        for start in range(0, cols, LANES):
            lanes = slice(start, start + LANES)
            accum, transmit = nothing()
            for s in range(parts.shape[0]):
                part = [
                    parts[s, c * BLOCK + half : c * BLOCK + half + HALF, lanes] for c in range(4)
                ]
                accum = [a + transmit * p for a, p in zip(accum, part[:3])]
                transmit = transmit - transmit * (part[3] * opacity_top)
            whole = [a * colour_scale for a in accum] + [1.0 - transmit]
            for c in range(4):
                at = start // LANES, slice(c * BLOCK + half, c * BLOCK + half + HALF)
                image[at] = whole[c]
    for r in range(BLOCK):
        for start in range(0, cols, LANES):
            out[:, r * cols + start : r * cols + start + LANES] = image[
                start // LANES, pl.ds(r, 4, stride=BLOCK)
            ]


def shards(volume, transfer_table):
    slices, rows, cols = volume.shape
    depth_count = lax.axis_size("depth")
    img_count = lax.axis_size("img")
    chips = depth_count // 2
    depth_total = slices * depth_count
    blocks = rows // (2 * BLOCK)
    core = lax.axis_index("depth") % 2

    half = rows // 2
    split = (slices, blocks, 2, BLOCK, cols)
    core_arg = core.astype(jnp.int32).reshape(1)
    same_core = [[2 * j + c for j in range(chips)] for c in range(2)]
    vmem = pl.BlockSpec(memory_space=pltpu.MemorySpace.VMEM)
    hbm = pl.BlockSpec(memory_space=pltpu.MemorySpace.HBM)
    in_hbm = functools.partial(pltpu.with_memory_space_constraint, memory_space=pltpu.MemorySpace.HBM)
    smem = pl.BlockSpec(memory_space=pltpu.MemorySpace.SMEM)
    params = pltpu.CompilerParams(vmem_limit_bytes=16 << 20)
    quad = jax.ShapeDtypeStruct((4, half, cols), F32)
    two = jax.ShapeDtypeStruct((2, half, cols), F32)
    unit = jax.ShapeDtypeStruct((slices, HALF, cols), F32)
    plane = jax.ShapeDtypeStruct((blocks, BLOCK, cols), BF16)
    edge = jax.ShapeDtypeStruct((2 * slices, HALF, cols), BF16)
    terms = (quad, quad, quad, two, two, unit, unit)

    partner = [(d, d ^ 1) for d in range(depth_count)]
    entries = transfer_table.shape[1]
    outer = pl.pallas_call(
        plane_kernel,
        out_shape=jax.ShapeDtypeStruct((rows, cols), BF16),
        in_specs=[smem, hbm],
        out_specs=vmem,
        scratch_shapes=[pltpu.SemaphoreType.DMA((1,))],
        compiler_params=params,
        name="plane",
    )(core_arg, in_hbm(volume))
    *ops, scales, own = pl.pallas_call(
        functools.partial(
            prepare_kernel, slab_share=2.0 * slices / depth_total, depth_total=depth_total
        ),
        out_shape=(
            jax.ShapeDtypeStruct((half, rows), BF16),
            jax.ShapeDtypeStruct((cols, cols), BF16),
            jax.ShapeDtypeStruct((8, HALF, entries), F32),
            jax.ShapeDtypeStruct((3, HALF, LANES), F32),
            jax.ShapeDtypeStruct(volume.shape, BF16),
        ),
        in_specs=[smem, hbm, hbm, vmem],
        out_specs=(vmem,) * 5,
        scratch_shapes=[
            pltpu.VMEM(transfer_table.shape, BF16), pltpu.SemaphoreType.DMA((slices + 1,)),
        ],
        compiler_params=params,
        name="prepare",
    )(
        core_arg, in_hbm(volume), in_hbm(transfer_table), outer
    )
    outer = lax.ppermute(
        outer, "depth",
        [(d, d + 1) for d in range(1, depth_count - 1, 2)]
        + [(d + 1, d) for d in range(1, depth_count - 1, 2)],
    ).reshape(split[1:])
    other = lax.ppermute(volume, "depth", partner).reshape(split)

    def slices_terms(cells, previous, name):
        return pl.pallas_call(
            slices_kernel,
            out_shape=terms,
            in_specs=[smem] + [vmem] * (4 + len(previous)),
            out_specs=(vmem,) * 7,
            scratch_shapes=[pltpu.VMEM((slices - 2, half, cols), F32)] * 2,
            compiler_params=params,
            name=name,
        )(core_arg, cells, *ops, *previous)

    own = own.reshape(split)
    own_terms = slices_terms(own, (), "own")
    outer, _ = lax.optimization_barrier((outer, own_terms[6]))
    relayed, edges = pl.pallas_call(
        relay_kernel,
        out_shape=(plane, edge),
        in_specs=[smem] + [vmem] * 3,
        out_specs=(vmem, vmem),
        compiler_params=params,
        name="relay",
    )(core_arg, own, other, outer)
    other_terms = slices_terms(other, (relayed,), "other")
    relayed = lax.ppermute(relayed, "depth", partner)
    edges = lax.ppermute(
        edges, ("img", "depth"),
        [
            (at * depth_count + d, to * depth_count + d)
            for i in range(img_count - 1)
            for d in range(depth_count)
            for at, to in [((i + 1, i) if d % 2 else (i, i + 1))]
        ],
    )
    partial_image = pl.pallas_call(
        slab_kernel,
        out_shape=jax.ShapeDtypeStruct((blocks, 4 * BLOCK, cols), F32),
        in_specs=[smem] + [vmem] * 21,
        out_specs=vmem,
        compiler_params=params,
        name="slab",
    )(
        core_arg, own, other, outer, relayed, edges, ops[2], scales, *own_terms, *other_terms,
    )
    pieces = lax.all_to_all(
        partial_image.astype(jnp.float16), "depth", split_axis=0, concat_axis=0, tiled=True,
        axis_index_groups=same_core,
    )
    return pl.pallas_call(
        merge_kernel,
        out_shape=jax.ShapeDtypeStruct((4, BLOCK * cols), F32),
        in_specs=[vmem, vmem],
        out_specs=vmem,
        scratch_shapes=[pltpu.VMEM((cols // LANES, 4 * BLOCK, LANES), F32)],
        compiler_params=params,
        name="merge",
    )(pieces.astype(F32), scales)


def solution(mesh):
    placed = (P("depth", "img", None), P())
    return jax.shard_map(
        shards, mesh=mesh, in_specs=placed, out_specs=P(None, ("img", "depth")), check_vma=False
    )
```

```python
import functools

import jax
import jax.numpy as jnp
import numpy as np
from jax import lax
from jax.experimental import pallas as pl
from jax.experimental.pallas import tpu as pltpu
from jax.sharding import PartitionSpec as P

F32 = jnp.float32
BF16 = jnp.bfloat16
BLOCK = 16
HALF = 8
LANES = 128
TINY = 1e-30
SLOPE = 1.4 / 3.0


def row_differences(rows, core):
    shape = (rows // 2, rows)
    local = lax.broadcasted_iota(jnp.int32, shape, 0)
    there = lax.broadcasted_iota(jnp.int32, shape, 1)
    step = there - (local + (local & -BLOCK) + core * BLOCK)
    return jnp.where(step == 1, 1.0, jnp.where(step == -1, -1.0, 0.0)).astype(BF16)


def column_differences(cols):
    step = lax.broadcasted_iota(jnp.int32, (cols, cols), 0) - lax.broadcasted_iota(
        jnp.int32, (cols, cols), 1
    )
    return jnp.where(step == 1, 1.0, jnp.where(step == -1, -1.0, 0.0)).astype(BF16)


def tops(table, slab_share):
    colour = jnp.max(jnp.max(table[0:3], axis=0, keepdims=True), axis=1, keepdims=True)
    extinction = jnp.max(table[3:4], axis=1, keepdims=True)
    return jnp.maximum(colour, TINY), jnp.maximum(extinction * slab_share, TINY)


def plane_kernel(core_ref, volume, outer, sem):
    at = (volume.shape[0] - 1) * core_ref[0]
    copy = pltpu.make_async_copy(volume.at[at], outer, sem.at[0])
    copy.start()
    copy.wait()


def prepare_kernel(
    core_ref, volume, table_hbm, _, rows_op, cols_op, tables, scales, cells, table_ref, sems,
    *, slab_share, depth_total,
):
    slices = volume.shape[0]
    table_copy = pltpu.make_async_copy(table_hbm, table_ref, sems.at[slices])
    copies = [pltpu.make_async_copy(volume.at[z], cells.at[z], sems.at[z]) for z in range(slices)]
    table_copy.start()
    for copy in copies:
        copy.start()
    rows_op[...] = row_differences(rows_op.shape[1], core_ref[0])
    cols_op[...] = column_differences(cols_op.shape[1])
    table_copy.wait()
    table = table_ref[...].astype(F32)
    entries = table.shape[1]
    colour_top, opacity_top = tops(table, slab_share)
    scale = SLOPE / (colour_top * opacity_top)
    last = lax.broadcasted_iota(jnp.int32, (HALF, entries), 1) == entries - 1
    for c in range(4):
        factor = scale if c < 3 else float(-np.log2(np.e) / depth_total)
        lower = jnp.broadcast_to(table[c : c + 1] * factor, (HALF, entries))
        tables[c] = lower
        tables[c + 4] = jnp.where(last, lower, pltpu.roll(lower, entries - 1, 1))
    for at, value in enumerate((colour_top * opacity_top, opacity_top, 1.0 / opacity_top)):
        scales[at] = jnp.broadcast_to(value, (HALF, LANES))
    for copy in copies:
        copy.wait()


def look_up(table, index):
    return jnp.take_along_axis(table, index, axis=1, mode="promise_in_bounds")


def classify(centre, tabs):
    position = centre * float(tabs[0].shape[1] - 1)
    knot = position.astype(jnp.int32)
    part = position - knot.astype(F32)
    upper = part.astype(BF16).astype(F32)
    lower = (1.0 - part).astype(BF16).astype(F32)
    values = [
        lower * look_up(tabs[c], knot) + upper * look_up(tabs[c + 4], knot) for c in range(4)
    ]
    return values[:3] + [jnp.exp2(values[3])]


def shade(accum, transmit, dz, slope_xy, norm_xy, found):
    shading = 0.3 / SLOPE + jnp.abs(dz + slope_xy) * lax.rsqrt(dz * dz + norm_xy)
    left = transmit * found[3]
    gain = (transmit - left) * shading
    return [a + gain * v for a, v in zip(accum, found[:3])], left


def slope_of(dx, dy):
    return 0.5 * dx + dy


def norm_of(dx, dy):
    return dx * dx + dy * dy + 0.04


def over(near, far):
    return [n + near[3] * f for n, f in zip(near[:3], far[:3])] + [near[3] * far[3]]


def nothing():
    return [jnp.zeros((HALF, LANES), F32)] * 3, jnp.ones((HALF, LANES), F32)


def pick(condition, a, b):
    return [jnp.where(condition, x, y) for x, y in zip(a, b)]


def each_block(blocks, unroll, body):
    def step(at, carry):
        for sub in range(unroll):
            body(at * unroll + sub)
        return carry

    lax.fori_loop(0, blocks // unroll, step, 0)


def each_unit(cols):
    for half in range(0, BLOCK, HALF):
        for start in range(0, cols, LANES):
            yield half, slice(half, half + HALF), slice(start, start + LANES)


def keep(ref, centre, tabs, here, lanes):
    for c, value in enumerate(classify(centre, tabs)):
        ref[c, here, lanes] = value


def slices_kernel(
    core_ref, cells, rows_op, cols_op, tables, *refs
):
    first, last, middle, slope, norm, edge_dx, edge_dy, inner_slope, inner_norm = refs[-9:]
    core = core_ref[0]
    slices, blocks, _, _, cols = cells.shape
    rows = blocks * BLOCK
    end = slices - 1
    for z in range(slices):
        dx = jnp.dot(rows_op[...], cells[z].reshape(2 * rows, cols), preferred_element_type=F32)
        dy = jnp.dot(
            cells[z, :, core].reshape(rows, cols), cols_op[...], preferred_element_type=F32
        )
        to_slope, to_norm, at = (
            (slope, norm, z // end) if z in (0, end) else (inner_slope, inner_norm, z - 1)
        )
        to_slope[at] = slope_of(dx, dy)
        to_norm[at] = norm_of(dx, dy)
        edge_dx[z] = jnp.where(core == 0, dx[:HALF], dx[rows - HALF :])
        edge_dy[z] = jnp.where(core == 0, dy[:HALF], dy[rows - HALF :])
    tabs = [tables[c] for c in range(8)]

    def block(b):
        for half, rows, lanes in each_unit(cols):
            here = pl.ds(pl.multiple_of(b * BLOCK + half, HALF), HALF)
            mine = [cells[z, b, core, rows, lanes].astype(F32) for z in range(slices)]
            keep(first, mine[0], tabs, here, lanes)
            accum, transmit = nothing()
            for z in range(1, end):
                accum, transmit = shade(
                    accum, transmit, mine[z + 1] - mine[z - 1],
                    inner_slope[z - 1, here, lanes], inner_norm[z - 1, here, lanes],
                    classify(mine[z], tabs),
                )
            keep(last, mine[end], tabs, here, lanes)
            for c, value in enumerate(accum + [transmit]):
                middle[c, here, lanes] = value

    each_block(blocks, 4, block)


def relay_kernel(core_ref, own, other, outer, relayed, edge):
    slices, blocks, _, _, _ = own.shape
    core = core_ref[0]
    relayed[...] = outer[:, 1 - core]

    @pl.when(core == 0)
    def _():
        edge[:slices] = own[:, blocks - 1, 1, HALF:, :]
        edge[slices:] = other[:, blocks - 1, 1, HALF:, :]

    @pl.when(core != 0)
    def _():
        edge[:slices] = own[:, 0, 0, :HALF, :]
        edge[slices:] = other[:, 0, 0, :HALF, :]


def slab_kernel(
    core_ref, own, other, outer, relayed, edges, tables, scales, *refs
):
    own_terms, other_terms, out = refs[:7], refs[7:14], refs[14]
    slices, blocks, _, _, cols = own.shape
    core = core_ref[0]
    front = core == 0
    end = slices - 1
    opacity_scale = scales[2]

    def stacks(mine, theirs, end_own, end_other):
        own_stack = (
            [jnp.where(front, end_own, theirs[end])] + mine + [jnp.where(front, theirs[0], end_own)]
        )
        other_stack = (
            [jnp.where(front, mine[end], end_other)]
            + theirs
            + [jnp.where(front, end_other, mine[0])]
        )
        return own_stack, other_stack

    def finish(own_part, other_part):
        both = over(pick(front, own_part, other_part), pick(front, other_part, own_part))
        both[3] = (1.0 - both[3]) * opacity_scale
        return both

    def block(b):
        for half, rows, lanes in each_unit(cols):
            here = pl.ds(pl.multiple_of(b * BLOCK + half, HALF), HALF)

            def half_slab(stack, terms):
                first, last, middle, slope, norm = terms[:5]
                parts = []
                for ref, at, z in ((first, 0, 0), (last, 1, end)):
                    accum, transmit = shade(
                        *nothing(), stack[z + 2] - stack[z],
                        slope[at, here, lanes], norm[at, here, lanes],
                        [ref[c, here, lanes] for c in range(4)],
                    )
                    parts.append(accum + [transmit])
                inner = [middle[c, here, lanes] for c in range(4)]
                return over(parts[0], over(inner, parts[1]))

            own_stack, other_stack = stacks(
                [own[z, b, core, rows, lanes].astype(F32) for z in range(slices)],
                [other[z, b, core, rows, lanes].astype(F32) for z in range(slices)],
                outer[b, core, rows, lanes].astype(F32),
                relayed[b, rows, lanes].astype(F32),
            )
            both = finish(half_slab(own_stack, own_terms), half_slab(other_stack, other_terms))
            for c in range(4):
                at = c * BLOCK + half
                out[b, at : at + HALF, lanes] = both[c]

    each_block(blocks, 2, block)

    tabs = [tables[c] for c in range(8)]
    b = jnp.where(front, 0, blocks - 1)
    row = lax.broadcasted_iota(jnp.int32, (HALF, LANES), 0)
    at_edge = row == jnp.where(front, 0, HALF - 1)
    for start in range(0, cols, LANES):
        lanes = slice(start, start + LANES)

        def load(ref, *index):
            top = ref[(*index, slice(0, HALF), lanes)].astype(F32)
            return jnp.where(front, top, ref[(*index, slice(HALF, BLOCK), lanes)].astype(F32))

        def half_slab(stack, terms, at):
            accum, transmit = nothing()
            for z in range(slices):
                halo = edges[at + z, :, lanes].astype(F32)
                halo = jnp.where(front, -halo[HALF - 1 :], halo[0:1])
                dx = terms[5][z, :, lanes] + jnp.where(at_edge, halo, 0.0)
                dy = terms[6][z, :, lanes]
                accum, transmit = shade(
                    accum, transmit, stack[z + 2] - stack[z],
                    slope_of(dx, dy), norm_of(dx, dy), classify(stack[z + 1], tabs),
                )
            return accum + [transmit]

        own_stack, other_stack = stacks(
            [load(own, z, b, core) for z in range(slices)],
            [load(other, z, b, core) for z in range(slices)],
            load(outer, b, core),
            load(relayed, b),
        )
        both = finish(
            half_slab(own_stack, own_terms, 0), half_slab(other_stack, other_terms, slices)
        )
        for c in range(4):
            at = pl.multiple_of(c * BLOCK + core * HALF, HALF)
            out[b, pl.ds(at, HALF), lanes] = both[c]


def merge_kernel(parts, scales, out, image):
    cols = parts.shape[2]
    colour_scale, opacity_top = scales[0], scales[1]
    for half in range(0, BLOCK, HALF):
        for start in range(0, cols, LANES):
            lanes = slice(start, start + LANES)
            accum, transmit = nothing()
            for s in range(parts.shape[0]):
                part = [
                    parts[s, c * BLOCK + half : c * BLOCK + half + HALF, lanes] for c in range(4)
                ]
                accum = [a + transmit * p for a, p in zip(accum, part[:3])]
                transmit = transmit - transmit * (part[3] * opacity_top)
            whole = [a * colour_scale for a in accum] + [1.0 - transmit]
            for c in range(4):
                at = start // LANES, slice(c * BLOCK + half, c * BLOCK + half + HALF)
                image[at] = whole[c]
    for r in range(BLOCK):
        for start in range(0, cols, LANES):
            out[:, r * cols + start : r * cols + start + LANES] = image[
                start // LANES, pl.ds(r, 4, stride=BLOCK)
            ]


def shards(volume, transfer_table):
    slices, rows, cols = volume.shape
    depth_count = lax.axis_size("depth")
    img_count = lax.axis_size("img")
    chips = depth_count // 2
    depth_total = slices * depth_count
    blocks = rows // (2 * BLOCK)
    core = lax.axis_index("depth") % 2

    half = rows // 2
    split = (slices, blocks, 2, BLOCK, cols)
    core_arg = core.astype(jnp.int32).reshape(1)
    same_core = [[2 * j + c for j in range(chips)] for c in range(2)]
    vmem = pl.BlockSpec(memory_space=pltpu.MemorySpace.VMEM)
    hbm = pl.BlockSpec(memory_space=pltpu.MemorySpace.HBM)
    in_hbm = functools.partial(pltpu.with_memory_space_constraint, memory_space=pltpu.MemorySpace.HBM)
    smem = pl.BlockSpec(memory_space=pltpu.MemorySpace.SMEM)
    params = pltpu.CompilerParams(vmem_limit_bytes=16 << 20)
    quad = jax.ShapeDtypeStruct((4, half, cols), F32)
    two = jax.ShapeDtypeStruct((2, half, cols), F32)
    unit = jax.ShapeDtypeStruct((slices, HALF, cols), F32)
    plane = jax.ShapeDtypeStruct((blocks, BLOCK, cols), BF16)
    edge = jax.ShapeDtypeStruct((2 * slices, HALF, cols), BF16)
    terms = (quad, quad, quad, two, two, unit, unit)

    partner = [(d, d ^ 1) for d in range(depth_count)]
    entries = transfer_table.shape[1]
    outer = pl.pallas_call(
        plane_kernel,
        out_shape=jax.ShapeDtypeStruct((rows, cols), BF16),
        in_specs=[smem, hbm],
        out_specs=vmem,
        scratch_shapes=[pltpu.SemaphoreType.DMA((1,))],
        compiler_params=params,
        name="plane",
    )(core_arg, in_hbm(volume))
    held = lax.optimization_barrier((volume, outer))[0]
    other = lax.ppermute(held, "depth", partner).reshape(split)
    *ops, scales, own = pl.pallas_call(
        functools.partial(
            prepare_kernel, slab_share=2.0 * slices / depth_total, depth_total=depth_total
        ),
        out_shape=(
            jax.ShapeDtypeStruct((half, rows), BF16),
            jax.ShapeDtypeStruct((cols, cols), BF16),
            jax.ShapeDtypeStruct((8, HALF, entries), F32),
            jax.ShapeDtypeStruct((3, HALF, LANES), F32),
            jax.ShapeDtypeStruct(volume.shape, BF16),
        ),
        in_specs=[smem, hbm, hbm, vmem],
        out_specs=(vmem,) * 5,
        scratch_shapes=[
            pltpu.VMEM(transfer_table.shape, BF16), pltpu.SemaphoreType.DMA((slices + 1,)),
        ],
        compiler_params=params,
        name="prepare",
    )(
        core_arg, in_hbm(volume), in_hbm(transfer_table), outer
    )
    outer = lax.ppermute(
        outer, "depth",
        [(d, d + 1) for d in range(1, depth_count - 1, 2)]
        + [(d + 1, d) for d in range(1, depth_count - 1, 2)],
    ).reshape(split[1:])

    def slices_terms(cells, previous, name):
        return pl.pallas_call(
            slices_kernel,
            out_shape=terms,
            in_specs=[smem] + [vmem] * (4 + len(previous)),
            out_specs=(vmem,) * 7,
            scratch_shapes=[pltpu.VMEM((slices - 2, half, cols), F32)] * 2,
            compiler_params=params,
            name=name,
        )(core_arg, cells, *ops, *previous)

    own = own.reshape(split)
    own_terms = slices_terms(own, (), "own")
    outer, _ = lax.optimization_barrier((outer, own_terms[6]))
    relayed, edges = pl.pallas_call(
        relay_kernel,
        out_shape=(plane, edge),
        in_specs=[smem] + [vmem] * 3,
        out_specs=(vmem, vmem),
        compiler_params=params,
        name="relay",
    )(core_arg, own, other, outer)
    other_terms = slices_terms(other, (relayed,), "other")
    relayed = lax.ppermute(relayed, "depth", partner)
    edges = lax.ppermute(
        edges, ("img", "depth"),
        [
            (at * depth_count + d, to * depth_count + d)
            for i in range(img_count - 1)
            for d in range(depth_count)
            for at, to in [((i + 1, i) if d % 2 else (i, i + 1))]
        ],
    )
    partial_image = pl.pallas_call(
        slab_kernel,
        out_shape=jax.ShapeDtypeStruct((blocks, 4 * BLOCK, cols), F32),
        in_specs=[smem] + [vmem] * 21,
        out_specs=vmem,
        compiler_params=params,
        name="slab",
    )(
        core_arg, own, other, outer, relayed, edges, ops[2], scales, *own_terms, *other_terms,
    )
    pieces = lax.all_to_all(
        partial_image.astype(jnp.float16), "depth", split_axis=0, concat_axis=0, tiled=True,
        axis_index_groups=same_core,
    )
    return pl.pallas_call(
        merge_kernel,
        out_shape=jax.ShapeDtypeStruct((4, BLOCK * cols), F32),
        in_specs=[vmem, vmem],
        out_specs=vmem,
        scratch_shapes=[pltpu.VMEM((cols // LANES, 4 * BLOCK, LANES), F32)],
        compiler_params=params,
        name="merge",
    )(pieces.astype(F32), scales)


def solution(mesh):
    placed = (P("depth", "img", None), P())
    return jax.shard_map(
        shards, mesh=mesh, in_specs=placed, out_specs=P(None, ("img", "depth")), check_vma=False
    )
```

```python
import functools

import jax
import jax.numpy as jnp
import numpy as np
from jax import lax
from jax.experimental import pallas as pl
from jax.experimental.pallas import tpu as pltpu
from jax.sharding import PartitionSpec as P

F32 = jnp.float32
BF16 = jnp.bfloat16
BLOCK = 16
HALF = 8
LANES = 128
PARTS = 4
TINY = 1e-30
SLOPE = 1.4 / 3.0


def row_differences(rows, core):
    shape = (rows // 2, rows)
    local = lax.broadcasted_iota(jnp.int32, shape, 0)
    there = lax.broadcasted_iota(jnp.int32, shape, 1)
    step = there - (local + (local & -BLOCK) + core * BLOCK)
    return jnp.where(step == 1, 1.0, jnp.where(step == -1, -1.0, 0.0)).astype(BF16)


def column_differences(cols):
    step = lax.broadcasted_iota(jnp.int32, (cols, cols), 0) - lax.broadcasted_iota(
        jnp.int32, (cols, cols), 1
    )
    return jnp.where(step == 1, 1.0, jnp.where(step == -1, -1.0, 0.0)).astype(BF16)


def tops(table, slab_share):
    colour = jnp.max(jnp.max(table[0:3], axis=0, keepdims=True), axis=1, keepdims=True)
    extinction = jnp.max(table[3:4], axis=1, keepdims=True)
    return jnp.maximum(colour, TINY), jnp.maximum(extinction * slab_share, TINY)


def plane_kernel(core_ref, volume, outer, sems):
    at = (volume.shape[0] - 1) * core_ref[0]
    parts = sems.shape[0]
    size = outer.shape[0] // parts
    copies = [
        pltpu.make_async_copy(
            volume.at[at, pl.ds(p * size, size)], outer.at[pl.ds(p * size, size)], sems.at[p]
        )
        for p in range(parts)
    ]
    for copy in copies:
        copy.start()
    for copy in copies:
        copy.wait()


def prepare_kernel(
    core_ref, volume, table_hbm, _, rows_op, cols_op, tables, scales, cells, table_ref, sems,
    *, slab_share, depth_total,
):
    slices = volume.shape[0]
    table_copy = pltpu.make_async_copy(table_hbm, table_ref, sems.at[slices * PARTS])
    size = volume.shape[1] // PARTS
    copies = [
        pltpu.make_async_copy(
            volume.at[z, pl.ds(p * size, size)],
            cells.at[z, pl.ds(p * size, size)],
            sems.at[z * PARTS + p],
        )
        for z in range(slices)
        for p in range(PARTS)
    ]
    table_copy.start()
    for copy in copies:
        copy.start()
    rows_op[...] = row_differences(rows_op.shape[1], core_ref[0])
    cols_op[...] = column_differences(cols_op.shape[1])
    table_copy.wait()
    table = table_ref[...].astype(F32)
    entries = table.shape[1]
    colour_top, opacity_top = tops(table, slab_share)
    scale = SLOPE / (colour_top * opacity_top)
    last = lax.broadcasted_iota(jnp.int32, (HALF, entries), 1) == entries - 1
    for c in range(4):
        factor = scale if c < 3 else float(-np.log2(np.e) / depth_total)
        lower = jnp.broadcast_to(table[c : c + 1] * factor, (HALF, entries))
        tables[c] = lower
        tables[c + 4] = jnp.where(last, lower, pltpu.roll(lower, entries - 1, 1))
    for at, value in enumerate((colour_top * opacity_top, opacity_top, 1.0 / opacity_top)):
        scales[at] = jnp.broadcast_to(value, (HALF, LANES))
    for copy in copies:
        copy.wait()


def look_up(table, index):
    return jnp.take_along_axis(table, index, axis=1, mode="promise_in_bounds")


def classify(centre, tabs):
    position = centre * float(tabs[0].shape[1] - 1)
    knot = position.astype(jnp.int32)
    part = position - knot.astype(F32)
    upper = part.astype(BF16).astype(F32)
    lower = (1.0 - part).astype(BF16).astype(F32)
    values = [
        lower * look_up(tabs[c], knot) + upper * look_up(tabs[c + 4], knot) for c in range(4)
    ]
    return values[:3] + [jnp.exp2(values[3])]


def shade(accum, transmit, dz, slope_xy, norm_xy, found):
    shading = 0.3 / SLOPE + jnp.abs(dz + slope_xy) * lax.rsqrt(dz * dz + norm_xy)
    left = transmit * found[3]
    gain = (transmit - left) * shading
    return [a + gain * v for a, v in zip(accum, found[:3])], left


def slope_of(dx, dy):
    return 0.5 * dx + dy


def norm_of(dx, dy):
    return dx * dx + dy * dy + 0.04


def over(near, far):
    return [n + near[3] * f for n, f in zip(near[:3], far[:3])] + [near[3] * far[3]]


def nothing():
    return [jnp.zeros((HALF, LANES), F32)] * 3, jnp.ones((HALF, LANES), F32)


def pick(condition, a, b):
    return [jnp.where(condition, x, y) for x, y in zip(a, b)]


def each_block(blocks, unroll, body):
    def step(at, carry):
        for sub in range(unroll):
            body(at * unroll + sub)
        return carry

    lax.fori_loop(0, blocks // unroll, step, 0)


def each_unit(cols):
    for half in range(0, BLOCK, HALF):
        for start in range(0, cols, LANES):
            yield half, slice(half, half + HALF), slice(start, start + LANES)


def keep(ref, centre, tabs, here, lanes):
    for c, value in enumerate(classify(centre, tabs)):
        ref[c, here, lanes] = value


def slices_kernel(
    core_ref, cells, rows_op, cols_op, tables, *refs
):
    first, last, middle, slope, norm, edge_dx, edge_dy, inner_slope, inner_norm = refs[-9:]
    core = core_ref[0]
    slices, blocks, _, _, cols = cells.shape
    rows = blocks * BLOCK
    end = slices - 1
    for z in range(slices):
        dx = jnp.dot(rows_op[...], cells[z].reshape(2 * rows, cols), preferred_element_type=F32)
        dy = jnp.dot(
            cells[z, :, core].reshape(rows, cols), cols_op[...], preferred_element_type=F32
        )
        to_slope, to_norm, at = (
            (slope, norm, z // end) if z in (0, end) else (inner_slope, inner_norm, z - 1)
        )
        to_slope[at] = slope_of(dx, dy)
        to_norm[at] = norm_of(dx, dy)
        edge_dx[z] = jnp.where(core == 0, dx[:HALF], dx[rows - HALF :])
        edge_dy[z] = jnp.where(core == 0, dy[:HALF], dy[rows - HALF :])
    tabs = [tables[c] for c in range(8)]

    def block(b):
        for half, rows, lanes in each_unit(cols):
            here = pl.ds(pl.multiple_of(b * BLOCK + half, HALF), HALF)
            mine = [cells[z, b, core, rows, lanes].astype(F32) for z in range(slices)]
            keep(first, mine[0], tabs, here, lanes)
            accum, transmit = nothing()
            for z in range(1, end):
                accum, transmit = shade(
                    accum, transmit, mine[z + 1] - mine[z - 1],
                    inner_slope[z - 1, here, lanes], inner_norm[z - 1, here, lanes],
                    classify(mine[z], tabs),
                )
            keep(last, mine[end], tabs, here, lanes)
            for c, value in enumerate(accum + [transmit]):
                middle[c, here, lanes] = value

    each_block(blocks, 4, block)


def relay_kernel(core_ref, own, other, outer, relayed, edge):
    slices, blocks, _, _, _ = own.shape
    core = core_ref[0]
    relayed[...] = outer[:, 1 - core]

    @pl.when(core == 0)
    def _():
        edge[:slices] = own[:, blocks - 1, 1, HALF:, :]
        edge[slices:] = other[:, blocks - 1, 1, HALF:, :]

    @pl.when(core != 0)
    def _():
        edge[:slices] = own[:, 0, 0, :HALF, :]
        edge[slices:] = other[:, 0, 0, :HALF, :]


def slab_kernel(
    core_ref, own, other, outer, relayed, edges, tables, scales, *refs
):
    own_terms, other_terms, out = refs[:7], refs[7:14], refs[14]
    slices, blocks, _, _, cols = own.shape
    core = core_ref[0]
    front = core == 0
    end = slices - 1
    opacity_scale = scales[2]

    def stacks(mine, theirs, end_own, end_other):
        own_stack = (
            [jnp.where(front, end_own, theirs[end])] + mine + [jnp.where(front, theirs[0], end_own)]
        )
        other_stack = (
            [jnp.where(front, mine[end], end_other)]
            + theirs
            + [jnp.where(front, end_other, mine[0])]
        )
        return own_stack, other_stack

    def finish(own_part, other_part):
        both = over(pick(front, own_part, other_part), pick(front, other_part, own_part))
        both[3] = (1.0 - both[3]) * opacity_scale
        return both

    def block(b):
        for half, rows, lanes in each_unit(cols):
            here = pl.ds(pl.multiple_of(b * BLOCK + half, HALF), HALF)

            def half_slab(stack, terms):
                first, last, middle, slope, norm = terms[:5]
                parts = []
                for ref, at, z in ((first, 0, 0), (last, 1, end)):
                    accum, transmit = shade(
                        *nothing(), stack[z + 2] - stack[z],
                        slope[at, here, lanes], norm[at, here, lanes],
                        [ref[c, here, lanes] for c in range(4)],
                    )
                    parts.append(accum + [transmit])
                inner = [middle[c, here, lanes] for c in range(4)]
                return over(parts[0], over(inner, parts[1]))

            own_stack, other_stack = stacks(
                [own[z, b, core, rows, lanes].astype(F32) for z in range(slices)],
                [other[z, b, core, rows, lanes].astype(F32) for z in range(slices)],
                outer[b, core, rows, lanes].astype(F32),
                relayed[b, rows, lanes].astype(F32),
            )
            both = finish(half_slab(own_stack, own_terms), half_slab(other_stack, other_terms))
            for c in range(4):
                at = c * BLOCK + half
                out[b, at : at + HALF, lanes] = both[c]

    each_block(blocks, 2, block)

    tabs = [tables[c] for c in range(8)]
    b = jnp.where(front, 0, blocks - 1)
    row = lax.broadcasted_iota(jnp.int32, (HALF, LANES), 0)
    at_edge = row == jnp.where(front, 0, HALF - 1)
    for start in range(0, cols, LANES):
        lanes = slice(start, start + LANES)

        def load(ref, *index):
            top = ref[(*index, slice(0, HALF), lanes)].astype(F32)
            return jnp.where(front, top, ref[(*index, slice(HALF, BLOCK), lanes)].astype(F32))

        def half_slab(stack, terms, at):
            accum, transmit = nothing()
            for z in range(slices):
                halo = edges[at + z, :, lanes].astype(F32)
                halo = jnp.where(front, -halo[HALF - 1 :], halo[0:1])
                dx = terms[5][z, :, lanes] + jnp.where(at_edge, halo, 0.0)
                dy = terms[6][z, :, lanes]
                accum, transmit = shade(
                    accum, transmit, stack[z + 2] - stack[z],
                    slope_of(dx, dy), norm_of(dx, dy), classify(stack[z + 1], tabs),
                )
            return accum + [transmit]

        own_stack, other_stack = stacks(
            [load(own, z, b, core) for z in range(slices)],
            [load(other, z, b, core) for z in range(slices)],
            load(outer, b, core),
            load(relayed, b),
        )
        both = finish(
            half_slab(own_stack, own_terms, 0), half_slab(other_stack, other_terms, slices)
        )
        for c in range(4):
            at = pl.multiple_of(c * BLOCK + core * HALF, HALF)
            out[b, pl.ds(at, HALF), lanes] = both[c]


def merge_kernel(parts, scales, out, image):
    cols = parts.shape[2]
    colour_scale, opacity_top = scales[0], scales[1]
    for half in range(0, BLOCK, HALF):
        for start in range(0, cols, LANES):
            lanes = slice(start, start + LANES)
            accum, transmit = nothing()
            for s in range(parts.shape[0]):
                part = [
                    parts[s, c * BLOCK + half : c * BLOCK + half + HALF, lanes] for c in range(4)
                ]
                accum = [a + transmit * p for a, p in zip(accum, part[:3])]
                transmit = transmit - transmit * (part[3] * opacity_top)
            whole = [a * colour_scale for a in accum] + [1.0 - transmit]
            for c in range(4):
                at = start // LANES, slice(c * BLOCK + half, c * BLOCK + half + HALF)
                image[at] = whole[c]
    for r in range(BLOCK):
        for start in range(0, cols, LANES):
            out[:, r * cols + start : r * cols + start + LANES] = image[
                start // LANES, pl.ds(r, 4, stride=BLOCK)
            ]


def shards(volume, transfer_table):
    slices, rows, cols = volume.shape
    depth_count = lax.axis_size("depth")
    img_count = lax.axis_size("img")
    chips = depth_count // 2
    depth_total = slices * depth_count
    blocks = rows // (2 * BLOCK)
    core = lax.axis_index("depth") % 2

    half = rows // 2
    split = (slices, blocks, 2, BLOCK, cols)
    core_arg = core.astype(jnp.int32).reshape(1)
    same_core = [[2 * j + c for j in range(chips)] for c in range(2)]
    vmem = pl.BlockSpec(memory_space=pltpu.MemorySpace.VMEM)
    hbm = pl.BlockSpec(memory_space=pltpu.MemorySpace.HBM)
    in_hbm = functools.partial(pltpu.with_memory_space_constraint, memory_space=pltpu.MemorySpace.HBM)
    smem = pl.BlockSpec(memory_space=pltpu.MemorySpace.SMEM)
    params = pltpu.CompilerParams(vmem_limit_bytes=16 << 20)
    quad = jax.ShapeDtypeStruct((4, half, cols), F32)
    two = jax.ShapeDtypeStruct((2, half, cols), F32)
    unit = jax.ShapeDtypeStruct((slices, HALF, cols), F32)
    plane = jax.ShapeDtypeStruct((blocks, BLOCK, cols), BF16)
    edge = jax.ShapeDtypeStruct((2 * slices, HALF, cols), BF16)
    terms = (quad, quad, quad, two, two, unit, unit)

    partner = [(d, d ^ 1) for d in range(depth_count)]
    entries = transfer_table.shape[1]
    outer = pl.pallas_call(
        plane_kernel,
        out_shape=jax.ShapeDtypeStruct((rows, cols), BF16),
        in_specs=[smem, hbm],
        out_specs=vmem,
        scratch_shapes=[pltpu.SemaphoreType.DMA((2 * PARTS,))],
        compiler_params=params,
        name="plane",
    )(core_arg, in_hbm(volume))
    *ops, scales, own = pl.pallas_call(
        functools.partial(
            prepare_kernel, slab_share=2.0 * slices / depth_total, depth_total=depth_total
        ),
        out_shape=(
            jax.ShapeDtypeStruct((half, rows), BF16),
            jax.ShapeDtypeStruct((cols, cols), BF16),
            jax.ShapeDtypeStruct((8, HALF, entries), F32),
            jax.ShapeDtypeStruct((3, HALF, LANES), F32),
            jax.ShapeDtypeStruct(volume.shape, BF16),
        ),
        in_specs=[smem, hbm, hbm, vmem],
        out_specs=(vmem,) * 5,
        scratch_shapes=[
            pltpu.VMEM(transfer_table.shape, BF16), pltpu.SemaphoreType.DMA((slices * PARTS + 1,)),
        ],
        compiler_params=params,
        name="prepare",
    )(
        core_arg, in_hbm(volume), in_hbm(transfer_table), outer
    )
    outer = lax.ppermute(
        outer, "depth",
        [(d, d + 1) for d in range(1, depth_count - 1, 2)]
        + [(d + 1, d) for d in range(1, depth_count - 1, 2)],
    ).reshape(split[1:])
    other = lax.ppermute(volume, "depth", partner).reshape(split)

    def slices_terms(cells, previous, name):
        return pl.pallas_call(
            slices_kernel,
            out_shape=terms,
            in_specs=[smem] + [vmem] * (4 + len(previous)),
            out_specs=(vmem,) * 7,
            scratch_shapes=[pltpu.VMEM((slices - 2, half, cols), F32)] * 2,
            compiler_params=params,
            name=name,
        )(core_arg, cells, *ops, *previous)

    own = own.reshape(split)
    own_terms = slices_terms(own, (), "own")
    outer, _ = lax.optimization_barrier((outer, own_terms[6]))
    relayed, edges = pl.pallas_call(
        relay_kernel,
        out_shape=(plane, edge),
        in_specs=[smem] + [vmem] * 3,
        out_specs=(vmem, vmem),
        compiler_params=params,
        name="relay",
    )(core_arg, own, other, outer)
    other_terms = slices_terms(other, (relayed,), "other")
    relayed = lax.ppermute(relayed, "depth", partner)
    edges = lax.ppermute(
        edges, ("img", "depth"),
        [
            (at * depth_count + d, to * depth_count + d)
            for i in range(img_count - 1)
            for d in range(depth_count)
            for at, to in [((i + 1, i) if d % 2 else (i, i + 1))]
        ],
    )
    partial_image = pl.pallas_call(
        slab_kernel,
        out_shape=jax.ShapeDtypeStruct((blocks, 4 * BLOCK, cols), F32),
        in_specs=[smem] + [vmem] * 21,
        out_specs=vmem,
        compiler_params=params,
        name="slab",
    )(
        core_arg, own, other, outer, relayed, edges, ops[2], scales, *own_terms, *other_terms,
    )
    pieces = lax.all_to_all(
        partial_image.astype(jnp.float16), "depth", split_axis=0, concat_axis=0, tiled=True,
        axis_index_groups=same_core,
    )
    return pl.pallas_call(
        merge_kernel,
        out_shape=jax.ShapeDtypeStruct((4, BLOCK * cols), F32),
        in_specs=[vmem, vmem],
        out_specs=vmem,
        scratch_shapes=[pltpu.VMEM((cols // LANES, 4 * BLOCK, LANES), F32)],
        compiler_params=params,
        name="merge",
    )(pieces.astype(F32), scales)


def solution(mesh):
    placed = (P("depth", "img", None), P())
    return jax.shard_map(
        shards, mesh=mesh, in_specs=placed, out_specs=P(None, ("img", "depth")), check_vma=False
    )
```

```python
import functools

import jax
import jax.numpy as jnp
import numpy as np
from jax import lax
from jax.experimental import pallas as pl
from jax.experimental.pallas import tpu as pltpu
from jax.sharding import PartitionSpec as P

F32 = jnp.float32
BF16 = jnp.bfloat16
BLOCK = 16
HALF = 8
LANES = 128
TINY = 1e-30
SLOPE = 1.4 / 3.0


def row_differences(rows, core):
    shape = (rows // 2, rows)
    local = lax.broadcasted_iota(jnp.int32, shape, 0)
    there = lax.broadcasted_iota(jnp.int32, shape, 1)
    step = there - (local + (local & -BLOCK) + core * BLOCK)
    return jnp.where(step == 1, 1.0, jnp.where(step == -1, -1.0, 0.0)).astype(BF16)


def column_differences(cols):
    step = lax.broadcasted_iota(jnp.int32, (cols, cols), 0) - lax.broadcasted_iota(
        jnp.int32, (cols, cols), 1
    )
    return jnp.where(step == 1, 1.0, jnp.where(step == -1, -1.0, 0.0)).astype(BF16)


def tops(table, slab_share):
    colour = jnp.max(jnp.max(table[0:3], axis=0, keepdims=True), axis=1, keepdims=True)
    extinction = jnp.max(table[3:4], axis=1, keepdims=True)
    return jnp.maximum(colour, TINY), jnp.maximum(extinction * slab_share, TINY)


def plane_kernel(core_ref, volume, outer, sem):
    at = (volume.shape[0] - 1) * core_ref[0]
    copy = pltpu.make_async_copy(volume.at[at], outer, sem.at[0])
    copy.start()
    copy.wait()


def prepare_kernel(
    core_ref, volume, table_hbm, _, rows_op, cols_op, tables, scales, cells, table_ref, sems,
    *, slab_share, depth_total,
):
    slices = volume.shape[0]
    table_copy = pltpu.make_async_copy(table_hbm, table_ref, sems.at[slices])
    copies = [pltpu.make_async_copy(volume.at[z], cells.at[z], sems.at[z]) for z in range(slices)]
    table_copy.start()
    for copy in copies:
        copy.start()
    rows_op[...] = row_differences(rows_op.shape[1], core_ref[0])
    cols_op[...] = column_differences(cols_op.shape[1])
    table_copy.wait()
    table = table_ref[...].astype(F32)
    entries = table.shape[1]
    colour_top, opacity_top = tops(table, slab_share)
    scale = SLOPE / (colour_top * opacity_top)
    last = lax.broadcasted_iota(jnp.int32, (HALF, entries), 1) == entries - 1
    for c in range(4):
        factor = scale if c < 3 else float(-np.log2(np.e) / depth_total)
        lower = jnp.broadcast_to(table[c : c + 1] * factor, (HALF, entries))
        tables[c] = lower
        tables[c + 4] = jnp.where(last, lower, pltpu.roll(lower, entries - 1, 1))
    for at, value in enumerate((colour_top * opacity_top, opacity_top, 1.0 / opacity_top)):
        scales[at] = jnp.broadcast_to(value, (HALF, LANES))
    for copy in copies:
        copy.wait()


def look_up(table, index):
    return jnp.take_along_axis(table, index, axis=1, mode="promise_in_bounds")


def classify(centre, tabs):
    position = centre * float(tabs[0].shape[1] - 1)
    knot = position.astype(jnp.int32)
    part = position - knot.astype(F32)
    upper = part.astype(BF16).astype(F32)
    lower = (1.0 - part).astype(BF16).astype(F32)
    values = [
        lower * look_up(tabs[c], knot) + upper * look_up(tabs[c + 4], knot) for c in range(4)
    ]
    return values[:3] + [jnp.exp2(values[3])]


def shade(accum, transmit, dz, slope_xy, norm_xy, found):
    shading = 0.3 / SLOPE + jnp.abs(dz + slope_xy) * lax.rsqrt(dz * dz + norm_xy)
    left = transmit * found[3]
    gain = (transmit - left) * shading
    return [a + gain * v for a, v in zip(accum, found[:3])], left


def slope_of(dx, dy):
    return 0.5 * dx + dy


def norm_of(dx, dy):
    return dx * dx + dy * dy + 0.04


def over(near, far):
    return [n + near[3] * f for n, f in zip(near[:3], far[:3])] + [near[3] * far[3]]


def nothing():
    return [jnp.zeros((HALF, LANES), F32)] * 3, jnp.ones((HALF, LANES), F32)


def pick(condition, a, b):
    return [jnp.where(condition, x, y) for x, y in zip(a, b)]


def each_block(blocks, unroll, body):
    def step(at, carry):
        for sub in range(unroll):
            body(at * unroll + sub)
        return carry

    lax.fori_loop(0, blocks // unroll, step, 0)


def each_unit(cols):
    for half in range(0, BLOCK, HALF):
        for start in range(0, cols, LANES):
            yield half, slice(half, half + HALF), slice(start, start + LANES)


def keep(ref, centre, tabs, here, lanes):
    for c, value in enumerate(classify(centre, tabs)):
        ref[c, here, lanes] = value


def slices_kernel(
    core_ref, cells, rows_op, cols_op, tables, *refs
):
    first, last, middle, slope, norm, edge_dx, edge_dy, inner_slope, inner_norm = refs[-9:]
    core = core_ref[0]
    slices, blocks, _, _, cols = cells.shape
    rows = blocks * BLOCK
    end = slices - 1
    for z in range(slices):
        dx = jnp.dot(rows_op[...], cells[z].reshape(2 * rows, cols), preferred_element_type=F32)
        dy = jnp.dot(
            cells[z, :, core].reshape(rows, cols), cols_op[...], preferred_element_type=F32
        )
        to_slope, to_norm, at = (
            (slope, norm, z // end) if z in (0, end) else (inner_slope, inner_norm, z - 1)
        )
        to_slope[at] = slope_of(dx, dy)
        to_norm[at] = norm_of(dx, dy)
        edge_dx[z] = jnp.where(core == 0, dx[:HALF], dx[rows - HALF :])
        edge_dy[z] = jnp.where(core == 0, dy[:HALF], dy[rows - HALF :])
    tabs = [tables[c] for c in range(8)]

    def block(b):
        for half, rows, lanes in each_unit(cols):
            here = pl.ds(pl.multiple_of(b * BLOCK + half, HALF), HALF)
            mine = [cells[z, b, core, rows, lanes].astype(F32) for z in range(slices)]
            keep(first, mine[0], tabs, here, lanes)
            accum, transmit = nothing()
            for z in range(1, end):
                accum, transmit = shade(
                    accum, transmit, mine[z + 1] - mine[z - 1],
                    inner_slope[z - 1, here, lanes], inner_norm[z - 1, here, lanes],
                    classify(mine[z], tabs),
                )
            keep(last, mine[end], tabs, here, lanes)
            for c, value in enumerate(accum + [transmit]):
                middle[c, here, lanes] = value

    each_block(blocks, 4, block)


def relay_kernel(core_ref, outer, relayed):
    relayed[...] = outer[:, 1 - core_ref[0]]


def edge_kernel(core_ref, own, other, _, edge):
    slices, blocks, _, _, _ = own.shape
    core = core_ref[0]

    @pl.when(core == 0)
    def _():
        edge[:slices] = own[:, blocks - 1, 1, HALF:, :]
        edge[slices:] = other[:, blocks - 1, 1, HALF:, :]

    @pl.when(core != 0)
    def _():
        edge[:slices] = own[:, 0, 0, :HALF, :]
        edge[slices:] = other[:, 0, 0, :HALF, :]


def slab_kernel(
    core_ref, own, other, outer, relayed, edges, tables, scales, *refs
):
    own_terms, other_terms, out = refs[:7], refs[7:14], refs[14]
    slices, blocks, _, _, cols = own.shape
    core = core_ref[0]
    front = core == 0
    end = slices - 1
    opacity_scale = scales[2]

    def stacks(mine, theirs, end_own, end_other):
        own_stack = (
            [jnp.where(front, end_own, theirs[end])] + mine + [jnp.where(front, theirs[0], end_own)]
        )
        other_stack = (
            [jnp.where(front, mine[end], end_other)]
            + theirs
            + [jnp.where(front, end_other, mine[0])]
        )
        return own_stack, other_stack

    def finish(own_part, other_part):
        both = over(pick(front, own_part, other_part), pick(front, other_part, own_part))
        both[3] = (1.0 - both[3]) * opacity_scale
        return both

    def block(b):
        for half, rows, lanes in each_unit(cols):
            here = pl.ds(pl.multiple_of(b * BLOCK + half, HALF), HALF)

            def half_slab(stack, terms):
                first, last, middle, slope, norm = terms[:5]
                parts = []
                for ref, at, z in ((first, 0, 0), (last, 1, end)):
                    accum, transmit = shade(
                        *nothing(), stack[z + 2] - stack[z],
                        slope[at, here, lanes], norm[at, here, lanes],
                        [ref[c, here, lanes] for c in range(4)],
                    )
                    parts.append(accum + [transmit])
                inner = [middle[c, here, lanes] for c in range(4)]
                return over(parts[0], over(inner, parts[1]))

            own_stack, other_stack = stacks(
                [own[z, b, core, rows, lanes].astype(F32) for z in range(slices)],
                [other[z, b, core, rows, lanes].astype(F32) for z in range(slices)],
                outer[b, core, rows, lanes].astype(F32),
                relayed[b, rows, lanes].astype(F32),
            )
            both = finish(half_slab(own_stack, own_terms), half_slab(other_stack, other_terms))
            for c in range(4):
                at = c * BLOCK + half
                out[b, at : at + HALF, lanes] = both[c]

    each_block(blocks, 2, block)

    tabs = [tables[c] for c in range(8)]
    b = jnp.where(front, 0, blocks - 1)
    row = lax.broadcasted_iota(jnp.int32, (HALF, LANES), 0)
    at_edge = row == jnp.where(front, 0, HALF - 1)
    for start in range(0, cols, LANES):
        lanes = slice(start, start + LANES)

        def load(ref, *index):
            top = ref[(*index, slice(0, HALF), lanes)].astype(F32)
            return jnp.where(front, top, ref[(*index, slice(HALF, BLOCK), lanes)].astype(F32))

        def half_slab(stack, terms, at):
            accum, transmit = nothing()
            for z in range(slices):
                halo = edges[at + z, :, lanes].astype(F32)
                halo = jnp.where(front, -halo[HALF - 1 :], halo[0:1])
                dx = terms[5][z, :, lanes] + jnp.where(at_edge, halo, 0.0)
                dy = terms[6][z, :, lanes]
                accum, transmit = shade(
                    accum, transmit, stack[z + 2] - stack[z],
                    slope_of(dx, dy), norm_of(dx, dy), classify(stack[z + 1], tabs),
                )
            return accum + [transmit]

        own_stack, other_stack = stacks(
            [load(own, z, b, core) for z in range(slices)],
            [load(other, z, b, core) for z in range(slices)],
            load(outer, b, core),
            load(relayed, b),
        )
        both = finish(
            half_slab(own_stack, own_terms, 0), half_slab(other_stack, other_terms, slices)
        )
        for c in range(4):
            at = pl.multiple_of(c * BLOCK + core * HALF, HALF)
            out[b, pl.ds(at, HALF), lanes] = both[c]


def merge_kernel(parts, scales, out, image):
    cols = parts.shape[2]
    colour_scale, opacity_top = scales[0], scales[1]
    for half in range(0, BLOCK, HALF):
        for start in range(0, cols, LANES):
            lanes = slice(start, start + LANES)
            accum, transmit = nothing()
            for s in range(parts.shape[0]):
                part = [
                    parts[s, c * BLOCK + half : c * BLOCK + half + HALF, lanes] for c in range(4)
                ]
                accum = [a + transmit * p for a, p in zip(accum, part[:3])]
                transmit = transmit - transmit * (part[3] * opacity_top)
            whole = [a * colour_scale for a in accum] + [1.0 - transmit]
            for c in range(4):
                at = start // LANES, slice(c * BLOCK + half, c * BLOCK + half + HALF)
                image[at] = whole[c]
    for r in range(BLOCK):
        for start in range(0, cols, LANES):
            out[:, r * cols + start : r * cols + start + LANES] = image[
                start // LANES, pl.ds(r, 4, stride=BLOCK)
            ]


def shards(volume, transfer_table):
    slices, rows, cols = volume.shape
    depth_count = lax.axis_size("depth")
    img_count = lax.axis_size("img")
    chips = depth_count // 2
    depth_total = slices * depth_count
    blocks = rows // (2 * BLOCK)
    core = lax.axis_index("depth") % 2

    half = rows // 2
    split = (slices, blocks, 2, BLOCK, cols)
    core_arg = core.astype(jnp.int32).reshape(1)
    same_core = [[2 * j + c for j in range(chips)] for c in range(2)]
    vmem = pl.BlockSpec(memory_space=pltpu.MemorySpace.VMEM)
    hbm = pl.BlockSpec(memory_space=pltpu.MemorySpace.HBM)
    in_hbm = functools.partial(pltpu.with_memory_space_constraint, memory_space=pltpu.MemorySpace.HBM)
    smem = pl.BlockSpec(memory_space=pltpu.MemorySpace.SMEM)
    params = pltpu.CompilerParams(vmem_limit_bytes=16 << 20)
    quad = jax.ShapeDtypeStruct((4, half, cols), F32)
    two = jax.ShapeDtypeStruct((2, half, cols), F32)
    unit = jax.ShapeDtypeStruct((slices, HALF, cols), F32)
    plane = jax.ShapeDtypeStruct((blocks, BLOCK, cols), BF16)
    edge = jax.ShapeDtypeStruct((2 * slices, HALF, cols), BF16)
    terms = (quad, quad, quad, two, two, unit, unit)

    partner = [(d, d ^ 1) for d in range(depth_count)]
    entries = transfer_table.shape[1]
    outer = pl.pallas_call(
        plane_kernel,
        out_shape=jax.ShapeDtypeStruct((rows, cols), BF16),
        in_specs=[smem, hbm],
        out_specs=vmem,
        scratch_shapes=[pltpu.SemaphoreType.DMA((1,))],
        compiler_params=params,
        name="plane",
    )(core_arg, in_hbm(volume))
    *ops, scales, own = pl.pallas_call(
        functools.partial(
            prepare_kernel, slab_share=2.0 * slices / depth_total, depth_total=depth_total
        ),
        out_shape=(
            jax.ShapeDtypeStruct((half, rows), BF16),
            jax.ShapeDtypeStruct((cols, cols), BF16),
            jax.ShapeDtypeStruct((8, HALF, entries), F32),
            jax.ShapeDtypeStruct((3, HALF, LANES), F32),
            jax.ShapeDtypeStruct(volume.shape, BF16),
        ),
        in_specs=[smem, hbm, hbm, vmem],
        out_specs=(vmem,) * 5,
        scratch_shapes=[
            pltpu.VMEM(transfer_table.shape, BF16), pltpu.SemaphoreType.DMA((slices + 1,)),
        ],
        compiler_params=params,
        name="prepare",
    )(
        core_arg, in_hbm(volume), in_hbm(transfer_table), outer
    )
    outer = lax.ppermute(
        outer, "depth",
        [(d, d + 1) for d in range(1, depth_count - 1, 2)]
        + [(d + 1, d) for d in range(1, depth_count - 1, 2)],
    ).reshape(split[1:])
    other = lax.ppermute(volume, "depth", partner).reshape(split)

    def slices_terms(cells, previous, name):
        return pl.pallas_call(
            slices_kernel,
            out_shape=terms,
            in_specs=[smem] + [vmem] * (4 + len(previous)),
            out_specs=(vmem,) * 7,
            scratch_shapes=[pltpu.VMEM((slices - 2, half, cols), F32)] * 2,
            compiler_params=params,
            name=name,
        )(core_arg, cells, *ops, *previous)

    own = own.reshape(split)
    own_terms = slices_terms(own, (), "own")
    edges = pl.pallas_call(
        edge_kernel,
        out_shape=edge,
        in_specs=[smem] + [vmem] * 3,
        out_specs=vmem,
        compiler_params=params,
        name="edge",
    )(core_arg, own, other, own_terms[6])
    outer, _ = lax.optimization_barrier((outer, edges))
    relayed = pl.pallas_call(
        relay_kernel,
        out_shape=plane,
        in_specs=[smem, vmem],
        out_specs=vmem,
        compiler_params=params,
        name="relay",
    )(core_arg, outer)
    other_terms = slices_terms(other, (relayed,), "other")
    relayed = lax.ppermute(relayed, "depth", partner)
    edges = lax.ppermute(
        edges, ("img", "depth"),
        [
            (at * depth_count + d, to * depth_count + d)
            for i in range(img_count - 1)
            for d in range(depth_count)
            for at, to in [((i + 1, i) if d % 2 else (i, i + 1))]
        ],
    )
    partial_image = pl.pallas_call(
        slab_kernel,
        out_shape=jax.ShapeDtypeStruct((blocks, 4 * BLOCK, cols), F32),
        in_specs=[smem] + [vmem] * 21,
        out_specs=vmem,
        compiler_params=params,
        name="slab",
    )(
        core_arg, own, other, outer, relayed, edges, ops[2], scales, *own_terms, *other_terms,
    )
    pieces = lax.all_to_all(
        partial_image.astype(jnp.float16), "depth", split_axis=0, concat_axis=0, tiled=True,
        axis_index_groups=same_core,
    )
    return pl.pallas_call(
        merge_kernel,
        out_shape=jax.ShapeDtypeStruct((4, BLOCK * cols), F32),
        in_specs=[vmem, vmem],
        out_specs=vmem,
        scratch_shapes=[pltpu.VMEM((cols // LANES, 4 * BLOCK, LANES), F32)],
        compiler_params=params,
        name="merge",
    )(pieces.astype(F32), scales)


def solution(mesh):
    placed = (P("depth", "img", None), P())
    return jax.shard_map(
        shards, mesh=mesh, in_specs=placed, out_specs=P(None, ("img", "depth")), check_vma=False
    )
```

```python
import functools

import jax
import jax.numpy as jnp
import numpy as np
from jax import lax
from jax.experimental import pallas as pl
from jax.experimental.pallas import tpu as pltpu
from jax.sharding import PartitionSpec as P

F32 = jnp.float32
BF16 = jnp.bfloat16
BLOCK = 16
HALF = 8
LANES = 128
TINY = 1e-30
SLOPE = 1.4 / 3.0


def row_differences(rows, core):
    shape = (rows // 2, rows)
    local = lax.broadcasted_iota(jnp.int32, shape, 0)
    there = lax.broadcasted_iota(jnp.int32, shape, 1)
    step = there - (local + (local & -BLOCK) + core * BLOCK)
    return jnp.where(step == 1, 1.0, jnp.where(step == -1, -1.0, 0.0)).astype(BF16)


def column_differences(cols):
    step = lax.broadcasted_iota(jnp.int32, (cols, cols), 0) - lax.broadcasted_iota(
        jnp.int32, (cols, cols), 1
    )
    return jnp.where(step == 1, 1.0, jnp.where(step == -1, -1.0, 0.0)).astype(BF16)


def tops(table, slab_share):
    colour = jnp.max(jnp.max(table[0:3], axis=0, keepdims=True), axis=1, keepdims=True)
    extinction = jnp.max(table[3:4], axis=1, keepdims=True)
    return jnp.maximum(colour, TINY), jnp.maximum(extinction * slab_share, TINY)


def plane_kernel(core_ref, volume, outer, sem):
    at = (volume.shape[0] - 1) * core_ref[0]
    copy = pltpu.make_async_copy(volume.at[at], outer, sem.at[0])
    copy.start()
    copy.wait()


def prepare_kernel(
    core_ref, volume, table_hbm, _, rows_op, cols_op, tables, scales, cells, table_ref, sems,
    *, slab_share, depth_total,
):
    slices = volume.shape[0]
    table_copy = pltpu.make_async_copy(table_hbm, table_ref, sems.at[slices])
    copies = [pltpu.make_async_copy(volume.at[z], cells.at[z], sems.at[z]) for z in range(slices)]
    table_copy.start()
    for copy in copies:
        copy.start()
    rows_op[...] = row_differences(rows_op.shape[1], core_ref[0])
    cols_op[...] = column_differences(cols_op.shape[1])
    table_copy.wait()
    table = table_ref[...].astype(F32)
    entries = table.shape[1]
    colour_top, opacity_top = tops(table, slab_share)
    scale = SLOPE / (colour_top * opacity_top)
    last = lax.broadcasted_iota(jnp.int32, (HALF, entries), 1) == entries - 1
    for c in range(4):
        factor = scale if c < 3 else float(-np.log2(np.e) / depth_total)
        lower = jnp.broadcast_to(table[c : c + 1] * factor, (HALF, entries))
        tables[c] = lower
        tables[c + 4] = jnp.where(last, lower, pltpu.roll(lower, entries - 1, 1))
    for at, value in enumerate((colour_top * opacity_top, opacity_top, 1.0 / opacity_top)):
        scales[at] = jnp.broadcast_to(value, (HALF, LANES))
    for copy in copies:
        copy.wait()


def look_up(table, index):
    return jnp.take_along_axis(table, index, axis=1, mode="promise_in_bounds")


def classify(centre, tabs):
    position = centre * float(tabs[0].shape[1] - 1)
    knot = position.astype(jnp.int32)
    part = position - knot.astype(F32)
    upper = part.astype(BF16).astype(F32)
    lower = (1.0 - part).astype(BF16).astype(F32)
    values = [
        lower * look_up(tabs[c], knot) + upper * look_up(tabs[c + 4], knot) for c in range(4)
    ]
    return values[:3] + [jnp.exp2(values[3])]


def shade(accum, transmit, dz, slope_xy, norm_xy, found):
    shading = 0.3 / SLOPE + jnp.abs(dz + slope_xy) * lax.rsqrt(dz * dz + norm_xy)
    left = transmit * found[3]
    gain = (transmit - left) * shading
    return [a + gain * v for a, v in zip(accum, found[:3])], left


def slope_of(dx, dy):
    return 0.5 * dx + dy


def norm_of(dx, dy):
    return dx * dx + dy * dy + 0.04


def over(near, far):
    return [n + near[3] * f for n, f in zip(near[:3], far[:3])] + [near[3] * far[3]]


def nothing():
    return [jnp.zeros((HALF, LANES), F32)] * 3, jnp.ones((HALF, LANES), F32)


def pick(condition, a, b):
    return [jnp.where(condition, x, y) for x, y in zip(a, b)]


def each_block(blocks, unroll, body):
    def step(at, carry):
        for sub in range(unroll):
            body(at * unroll + sub)
        return carry

    lax.fori_loop(0, blocks // unroll, step, 0)


def each_unit(cols):
    for half in range(0, BLOCK, HALF):
        for start in range(0, cols, LANES):
            yield half, slice(half, half + HALF), slice(start, start + LANES)


def keep(ref, centre, tabs, here, lanes):
    for c, value in enumerate(classify(centre, tabs)):
        ref[c, here, lanes] = value


def slices_kernel(
    core_ref, cells, rows_op, cols_op, tables, *refs
):
    first, last, middle, slope, norm, edge_dx, edge_dy, inner_slope, inner_norm = refs[-9:]
    core = core_ref[0]
    slices, blocks, _, _, cols = cells.shape
    rows = blocks * BLOCK
    end = slices - 1
    for z in range(slices):
        dx = jnp.dot(rows_op[...], cells[z].reshape(2 * rows, cols), preferred_element_type=F32)
        dy = jnp.dot(
            cells[z, :, core].reshape(rows, cols), cols_op[...], preferred_element_type=F32
        )
        to_slope, to_norm, at = (
            (slope, norm, z // end) if z in (0, end) else (inner_slope, inner_norm, z - 1)
        )
        to_slope[at] = slope_of(dx, dy)
        to_norm[at] = norm_of(dx, dy)
        edge_dx[z] = jnp.where(core == 0, dx[:HALF], dx[rows - HALF :])
        edge_dy[z] = jnp.where(core == 0, dy[:HALF], dy[rows - HALF :])
    tabs = [tables[c] for c in range(8)]

    def block(b):
        for half, rows, lanes in each_unit(cols):
            here = pl.ds(pl.multiple_of(b * BLOCK + half, HALF), HALF)
            mine = [cells[z, b, core, rows, lanes].astype(F32) for z in range(slices)]
            keep(first, mine[0], tabs, here, lanes)
            accum, transmit = nothing()
            for z in range(1, end):
                accum, transmit = shade(
                    accum, transmit, mine[z + 1] - mine[z - 1],
                    inner_slope[z - 1, here, lanes], inner_norm[z - 1, here, lanes],
                    classify(mine[z], tabs),
                )
            keep(last, mine[end], tabs, here, lanes)
            for c, value in enumerate(accum + [transmit]):
                middle[c, here, lanes] = value

    each_block(blocks, 8, block)


def relay_kernel(core_ref, own, other, outer, relayed, edge):
    slices, blocks, _, _, _ = own.shape
    core = core_ref[0]
    relayed[...] = outer[:, 1 - core]

    @pl.when(core == 0)
    def _():
        edge[:slices] = own[:, blocks - 1, 1, HALF:, :]
        edge[slices:] = other[:, blocks - 1, 1, HALF:, :]

    @pl.when(core != 0)
    def _():
        edge[:slices] = own[:, 0, 0, :HALF, :]
        edge[slices:] = other[:, 0, 0, :HALF, :]


def slab_kernel(
    core_ref, own, other, outer, relayed, edges, tables, scales, *refs
):
    own_terms, other_terms, out = refs[:7], refs[7:14], refs[14]
    slices, blocks, _, _, cols = own.shape
    core = core_ref[0]
    front = core == 0
    end = slices - 1
    opacity_scale = scales[2]

    def stacks(mine, theirs, end_own, end_other):
        own_stack = (
            [jnp.where(front, end_own, theirs[end])] + mine + [jnp.where(front, theirs[0], end_own)]
        )
        other_stack = (
            [jnp.where(front, mine[end], end_other)]
            + theirs
            + [jnp.where(front, end_other, mine[0])]
        )
        return own_stack, other_stack

    def finish(own_part, other_part):
        both = over(pick(front, own_part, other_part), pick(front, other_part, own_part))
        both[3] = (1.0 - both[3]) * opacity_scale
        return both

    def block(b):
        for half, rows, lanes in each_unit(cols):
            here = pl.ds(pl.multiple_of(b * BLOCK + half, HALF), HALF)

            def half_slab(stack, terms):
                first, last, middle, slope, norm = terms[:5]
                parts = []
                for ref, at, z in ((first, 0, 0), (last, 1, end)):
                    accum, transmit = shade(
                        *nothing(), stack[z + 2] - stack[z],
                        slope[at, here, lanes], norm[at, here, lanes],
                        [ref[c, here, lanes] for c in range(4)],
                    )
                    parts.append(accum + [transmit])
                inner = [middle[c, here, lanes] for c in range(4)]
                return over(parts[0], over(inner, parts[1]))

            own_stack, other_stack = stacks(
                [own[z, b, core, rows, lanes].astype(F32) for z in range(slices)],
                [other[z, b, core, rows, lanes].astype(F32) for z in range(slices)],
                outer[b, core, rows, lanes].astype(F32),
                relayed[b, rows, lanes].astype(F32),
            )
            both = finish(half_slab(own_stack, own_terms), half_slab(other_stack, other_terms))
            for c in range(4):
                at = c * BLOCK + half
                out[b, at : at + HALF, lanes] = both[c]

    each_block(blocks, 2, block)

    tabs = [tables[c] for c in range(8)]
    b = jnp.where(front, 0, blocks - 1)
    row = lax.broadcasted_iota(jnp.int32, (HALF, LANES), 0)
    at_edge = row == jnp.where(front, 0, HALF - 1)
    for start in range(0, cols, LANES):
        lanes = slice(start, start + LANES)

        def load(ref, *index):
            top = ref[(*index, slice(0, HALF), lanes)].astype(F32)
            return jnp.where(front, top, ref[(*index, slice(HALF, BLOCK), lanes)].astype(F32))

        def half_slab(stack, terms, at):
            accum, transmit = nothing()
            for z in range(slices):
                halo = edges[at + z, :, lanes].astype(F32)
                halo = jnp.where(front, -halo[HALF - 1 :], halo[0:1])
                dx = terms[5][z, :, lanes] + jnp.where(at_edge, halo, 0.0)
                dy = terms[6][z, :, lanes]
                accum, transmit = shade(
                    accum, transmit, stack[z + 2] - stack[z],
                    slope_of(dx, dy), norm_of(dx, dy), classify(stack[z + 1], tabs),
                )
            return accum + [transmit]

        own_stack, other_stack = stacks(
            [load(own, z, b, core) for z in range(slices)],
            [load(other, z, b, core) for z in range(slices)],
            load(outer, b, core),
            load(relayed, b),
        )
        both = finish(
            half_slab(own_stack, own_terms, 0), half_slab(other_stack, other_terms, slices)
        )
        for c in range(4):
            at = pl.multiple_of(c * BLOCK + core * HALF, HALF)
            out[b, pl.ds(at, HALF), lanes] = both[c]


def merge_kernel(parts, scales, out, image):
    cols = parts.shape[2]
    colour_scale, opacity_top = scales[0], scales[1]
    for half in range(0, BLOCK, HALF):
        for start in range(0, cols, LANES):
            lanes = slice(start, start + LANES)
            accum, transmit = nothing()
            for s in range(parts.shape[0]):
                part = [
                    parts[s, c * BLOCK + half : c * BLOCK + half + HALF, lanes] for c in range(4)
                ]
                accum = [a + transmit * p for a, p in zip(accum, part[:3])]
                transmit = transmit - transmit * (part[3] * opacity_top)
            whole = [a * colour_scale for a in accum] + [1.0 - transmit]
            for c in range(4):
                at = start // LANES, slice(c * BLOCK + half, c * BLOCK + half + HALF)
                image[at] = whole[c]
    for r in range(BLOCK):
        for start in range(0, cols, LANES):
            out[:, r * cols + start : r * cols + start + LANES] = image[
                start // LANES, pl.ds(r, 4, stride=BLOCK)
            ]


def shards(volume, transfer_table):
    slices, rows, cols = volume.shape
    depth_count = lax.axis_size("depth")
    img_count = lax.axis_size("img")
    chips = depth_count // 2
    depth_total = slices * depth_count
    blocks = rows // (2 * BLOCK)
    core = lax.axis_index("depth") % 2

    half = rows // 2
    split = (slices, blocks, 2, BLOCK, cols)
    core_arg = core.astype(jnp.int32).reshape(1)
    same_core = [[2 * j + c for j in range(chips)] for c in range(2)]
    vmem = pl.BlockSpec(memory_space=pltpu.MemorySpace.VMEM)
    hbm = pl.BlockSpec(memory_space=pltpu.MemorySpace.HBM)
    in_hbm = functools.partial(pltpu.with_memory_space_constraint, memory_space=pltpu.MemorySpace.HBM)
    smem = pl.BlockSpec(memory_space=pltpu.MemorySpace.SMEM)
    params = pltpu.CompilerParams(vmem_limit_bytes=16 << 20)
    quad = jax.ShapeDtypeStruct((4, half, cols), F32)
    two = jax.ShapeDtypeStruct((2, half, cols), F32)
    unit = jax.ShapeDtypeStruct((slices, HALF, cols), F32)
    plane = jax.ShapeDtypeStruct((blocks, BLOCK, cols), BF16)
    edge = jax.ShapeDtypeStruct((2 * slices, HALF, cols), BF16)
    terms = (quad, quad, quad, two, two, unit, unit)

    partner = [(d, d ^ 1) for d in range(depth_count)]
    entries = transfer_table.shape[1]
    outer = pl.pallas_call(
        plane_kernel,
        out_shape=jax.ShapeDtypeStruct((rows, cols), BF16),
        in_specs=[smem, hbm],
        out_specs=vmem,
        scratch_shapes=[pltpu.SemaphoreType.DMA((1,))],
        compiler_params=params,
        name="plane",
    )(core_arg, in_hbm(volume))
    *ops, scales, own = pl.pallas_call(
        functools.partial(
            prepare_kernel, slab_share=2.0 * slices / depth_total, depth_total=depth_total
        ),
        out_shape=(
            jax.ShapeDtypeStruct((half, rows), BF16),
            jax.ShapeDtypeStruct((cols, cols), BF16),
            jax.ShapeDtypeStruct((8, HALF, entries), F32),
            jax.ShapeDtypeStruct((3, HALF, LANES), F32),
            jax.ShapeDtypeStruct(volume.shape, BF16),
        ),
        in_specs=[smem, hbm, hbm, vmem],
        out_specs=(vmem,) * 5,
        scratch_shapes=[
            pltpu.VMEM(transfer_table.shape, BF16), pltpu.SemaphoreType.DMA((slices + 1,)),
        ],
        compiler_params=params,
        name="prepare",
    )(
        core_arg, in_hbm(volume), in_hbm(transfer_table), outer
    )
    outer = lax.ppermute(
        outer, "depth",
        [(d, d + 1) for d in range(1, depth_count - 1, 2)]
        + [(d + 1, d) for d in range(1, depth_count - 1, 2)],
    ).reshape(split[1:])
    other = lax.ppermute(volume, "depth", partner).reshape(split)

    def slices_terms(cells, previous, name):
        return pl.pallas_call(
            slices_kernel,
            out_shape=terms,
            in_specs=[smem] + [vmem] * (4 + len(previous)),
            out_specs=(vmem,) * 7,
            scratch_shapes=[pltpu.VMEM((slices - 2, half, cols), F32)] * 2,
            compiler_params=params,
            name=name,
        )(core_arg, cells, *ops, *previous)

    own = own.reshape(split)
    own_terms = slices_terms(own, (), "own")
    outer, _ = lax.optimization_barrier((outer, own_terms[6]))
    relayed, edges = pl.pallas_call(
        relay_kernel,
        out_shape=(plane, edge),
        in_specs=[smem] + [vmem] * 3,
        out_specs=(vmem, vmem),
        compiler_params=params,
        name="relay",
    )(core_arg, own, other, outer)
    other_terms = slices_terms(other, (relayed,), "other")
    relayed = lax.ppermute(relayed, "depth", partner)
    edges = lax.ppermute(
        edges, ("img", "depth"),
        [
            (at * depth_count + d, to * depth_count + d)
            for i in range(img_count - 1)
            for d in range(depth_count)
            for at, to in [((i + 1, i) if d % 2 else (i, i + 1))]
        ],
    )
    partial_image = pl.pallas_call(
        slab_kernel,
        out_shape=jax.ShapeDtypeStruct((blocks, 4 * BLOCK, cols), F32),
        in_specs=[smem] + [vmem] * 21,
        out_specs=vmem,
        compiler_params=params,
        name="slab",
    )(
        core_arg, own, other, outer, relayed, edges, ops[2], scales, *own_terms, *other_terms,
    )
    pieces = lax.all_to_all(
        partial_image.astype(jnp.float16), "depth", split_axis=0, concat_axis=0, tiled=True,
        axis_index_groups=same_core,
    )
    return pl.pallas_call(
        merge_kernel,
        out_shape=jax.ShapeDtypeStruct((4, BLOCK * cols), F32),
        in_specs=[vmem, vmem],
        out_specs=vmem,
        scratch_shapes=[pltpu.VMEM((cols // LANES, 4 * BLOCK, LANES), F32)],
        compiler_params=params,
        name="merge",
    )(pieces.astype(F32), scales)


def solution(mesh):
    placed = (P("depth", "img", None), P())
    return jax.shard_map(
        shards, mesh=mesh, in_specs=placed, out_specs=P(None, ("img", "depth")), check_vma=False
    )
```
